32 devices in a mesh: head: 4 (over x, core), ctx: 8 (over z, y).
Axes of the slice: x: 2, y: 2, z: 4, core: 2. Of those that a mesh axis runs over, the one named last changes fastest.
Arguments:
- query: bfloat16 [8, 512, 512], P('ctx', 'head'), may hold values from -36 to 36
- key: bfloat16 [8, 512, 512], P('ctx', 'head'), may hold values from -36 to 36
- value: bfloat16 [8, 512, 512], P('ctx', 'head'), may hold values from -6 to 6
- resid_in: bfloat16 [8, 512, 1024], P('ctx', 'head'), may hold values from -6 to 6
- out_grad: bfloat16 [8, 512, 1024], P('ctx', 'head'), may hold values from -6 to 6
- out_weight: bfloat16 [512, 1024], replicated, may hold values from -0.25 to 0.25
- conv_kernel: bfloat16 [31, 1024], replicated, may hold values from -1 to 1
- frame_lengths: int32 [8], replicated, may hold values from 256 to 512, as said below
Outputs:
- d_resid: bfloat16 [8, 512, 1024], P('ctx', None, 'head')
- d_query: bfloat16 [8, 512, 512], P('ctx', None, 'head')
- d_key: bfloat16 [8, 512, 512], P('ctx', None, 'head')
- d_value: bfloat16 [8, 512, 512], P('ctx', None, 'head')
The draws below stay inside these ranges and needn't reach their ends.
Inputs may be any that keep to these rules, and one draw needn't show every extreme that they name: Block b holds audio in its first frame_lengths[b] frames; at least one block is full.
All inputs are finite; a program needn't handle non-finite values.
Results may differ from the reference program's by a relative error of at most 0.0086.
Values may be sent and summed in bfloat16 or wider, within the bound.
No kernel may reach another device: no remote copies, remote signals or barrier semaphores. Data moves between devices by JAX's collectives and lax.ppermute only.
A program may use at most 128 MiB of HBM per device.

```python
import jax
import jax.numpy as jnp
from jax import lax

D = 1024
HEADS = 8
HEAD_DIM = 64
KERNEL = 31
REACH = 2
CTX_ROWS = 512
BLOCKS = 8
FRAMES = 4096
ATT = 512
WINDOW = 1024


def draw_query(key, part):
    noise = jnp.clip(jax.random.normal(jax.random.fold_in(key, 21), (FRAMES, ATT), jnp.float32), -6.0, 6.0)
    return noise.reshape(BLOCKS, CTX_ROWS, ATT).astype(jnp.bfloat16)


def draw_key(key, part):
    noise = 2.0 * jnp.clip(jax.random.normal(jax.random.fold_in(key, 22), (FRAMES, ATT), jnp.float32), -6.0, 6.0)
    return noise.reshape(BLOCKS, CTX_ROWS, ATT).astype(jnp.bfloat16)


def draw_frame_lengths(key, part):
    lengths = jax.random.randint(jax.random.fold_in(key, 31), (BLOCKS,), CTX_ROWS // 2, CTX_ROWS + 1)
    full_block = jax.random.randint(jax.random.fold_in(key, 32), (), 0, BLOCKS)
    return lengths.at[full_block].set(CTX_ROWS).astype(jnp.int32)


def block_levels(key, shape, pieces, low, high):
    def one(axis_at, shards_of):
        heights = jax.random.uniform(jax.random.fold_in(jax.random.fold_in(key, 6), axis_at), (shards_of,), jnp.float32, low / len(pieces), high / len(pieces))
        return jnp.repeat(jnp.exp(heights), shape[axis_at] // shards_of).reshape((-1,) + (1,) * (len(shape) - axis_at - 1))

    gain = one(*pieces[0])
    for cut in pieces[1:]:
        gain = gain * one(*cut)
    return gain


def gaussian(rng, extent, width, bound, shards=(), held_as=jnp.bfloat16):
    drawn = width * jax.random.normal(rng, extent, jnp.float32)
    if shards:
        drawn = drawn * block_levels(rng, extent, shards, -0.22, 0.18)
    return jnp.clip(drawn, -bound, bound).astype(held_as)


def setup_inputs(seed: int = 0) -> dict:
    key_of = jax.random.split(jax.random.key(seed), 9)
    return {
        "query": draw_query(jax.random.fold_in(key_of[8], 71), 0),
        "key": draw_key(jax.random.fold_in(key_of[8], 71), 0),
        "value": gaussian(key_of[2], (BLOCKS, CTX_ROWS, ATT), 1.0, 6.0, ((0, 8), (1, 4))),
        "resid_in": gaussian(key_of[3], (BLOCKS, CTX_ROWS, D), 1.0, 6.0, ((0, 8), (1, 4))),
        "out_grad": gaussian(key_of[4], (BLOCKS, CTX_ROWS, D), 1.0, 6.0, ((0, 8), (1, 4))),
        "out_weight": gaussian(key_of[5], (ATT, D), ATT ** -0.5, 0.25),
        "conv_kernel": gaussian(key_of[6], (KERNEL, D), KERNEL ** -0.5, 1.0),
        "frame_lengths": draw_frame_lengths(jax.random.fold_in(key_of[8], 71), 0),
    }


def swish_slope(before):
    logistic = jax.nn.sigmoid(before)
    return logistic * (1.0 + before * (1.0 - logistic))


def shift_blocks(array, amount):
    if amount == 0:
        return array
    filler = jnp.zeros((abs(amount),) + array.shape[1:], array.dtype)
    if amount > 0:
        return jnp.concatenate([filler, array[:BLOCKS - amount]], axis=0)
    return jnp.concatenate([array[-amount:], filler], axis=0)


def reference(query, key, value, resid_in, out_grad, out_weight, conv_kernel, frame_lengths):
    margin = (KERNEL - 1) // 2
    resid = resid_in.reshape(FRAMES, D).astype(jnp.float32)
    upstream = out_grad.reshape(FRAMES, D).astype(jnp.float32)
    weights_all = conv_kernel.astype(jnp.float32)
    padded = jnp.pad(resid, ((margin, margin), (0, 0)))
    conv_pre = jnp.zeros((FRAMES, D), jnp.float32)
    for offset in range(KERNEL):
        conv_pre = conv_pre + weights_all[offset] * padded[offset:offset + FRAMES]
    conv_grad = upstream * swish_slope(conv_pre)
    grad_pad = jnp.pad(conv_grad, ((margin, margin), (0, 0)))
    total = upstream
    for offset in range(KERNEL):
        start_at = 2 * margin - offset
        total = total + weights_all[offset] * grad_pad[start_at:start_at + FRAMES]
    d_resid = total.astype(jnp.bfloat16)
    head_grad = jnp.dot(d_resid, out_weight.T, preferred_element_type=jnp.float32).astype(jnp.bfloat16)

    scale = HEAD_DIM ** -0.5
    span = 2 * REACH + 1
    edge = REACH * CTX_ROWS

    def split_heads(array):
        return array.reshape(FRAMES, HEADS, HEAD_DIM).transpose(1, 0, 2)

    rows = jnp.arange(CTX_ROWS, dtype=jnp.int32)
    reach_rows = jnp.arange(span * CTX_ROWS, dtype=jnp.int32)

    def one_head(operands):
        query_one, key_one, value_one, grad_one = operands
        key_pad = jnp.pad(key_one, ((edge, edge), (0, 0)))
        value_pad = jnp.pad(value_one, ((edge, edge), (0, 0)))

        def one_block(block):
            first = (block * CTX_ROWS).astype(jnp.int32)
            query_block = lax.dynamic_slice_in_dim(query_one, first, CTX_ROWS, 0)
            grad_block = lax.dynamic_slice_in_dim(grad_one, first, CTX_ROWS, 0)
            key_span = lax.dynamic_slice_in_dim(key_pad, first, span * CTX_ROWS, 0)
            value_span = lax.dynamic_slice_in_dim(value_pad, first, span * CTX_ROWS, 0)
            query_place = first + rows
            key_place = first - edge + reach_rows
            key_block_of = jnp.floor_divide(key_place, CTX_ROWS).astype(jnp.int32)
            inside = (key_place >= 0) & (key_place < FRAMES)
            limit = frame_lengths[jnp.clip(key_block_of, 0, BLOCKS - 1)]
            within = (key_place - key_block_of * CTX_ROWS) < limit
            near = jnp.abs(query_place[:, None] - key_place[None, :]) <= WINDOW
            live = near & (inside & within)[None, :]
            logits = jnp.dot(query_block, key_span.T, preferred_element_type=jnp.float32) * scale
            logits = jnp.where(live, logits, -jnp.inf)
            highest = jnp.max(logits, axis=1, keepdims=True)
            log_total = highest + jnp.log(jnp.sum(jnp.exp(logits - highest), axis=1, keepdims=True))
            probs = jnp.exp(logits - log_total)
            slopes = jnp.dot(grad_block, value_span.T, preferred_element_type=jnp.float32)
            delta = jnp.sum(probs * slopes, axis=1, keepdims=True)
            dlogits = (probs * (slopes - delta)).astype(jnp.bfloat16)
            probs_low = probs.astype(jnp.bfloat16)
            query_part = (jnp.dot(dlogits, key_span, preferred_element_type=jnp.float32) * scale).astype(jnp.bfloat16)
            key_part = (jnp.dot(dlogits.T, query_block, preferred_element_type=jnp.float32) * scale).astype(jnp.bfloat16)
            value_part = jnp.dot(probs_low.T, grad_block, preferred_element_type=jnp.float32).astype(jnp.bfloat16)
            return (query_part, key_part.reshape(span, CTX_ROWS, HEAD_DIM), value_part.reshape(span, CTX_ROWS, HEAD_DIM))

        query_parts, key_parts, value_parts = lax.map(one_block, jnp.arange(BLOCKS, dtype=jnp.int32))
        key_sum = jnp.zeros((BLOCKS, CTX_ROWS, HEAD_DIM), jnp.float32)
        value_sum = jnp.zeros((BLOCKS, CTX_ROWS, HEAD_DIM), jnp.float32)
        for index in range(span):
            key_sum = key_sum + shift_blocks(key_parts[:, index].astype(jnp.float32), index - REACH)
            value_sum = value_sum + shift_blocks(value_parts[:, index].astype(jnp.float32), index - REACH)
        return (query_parts.reshape(FRAMES, HEAD_DIM), key_sum.astype(jnp.bfloat16).reshape(FRAMES, HEAD_DIM), value_sum.astype(jnp.bfloat16).reshape(FRAMES, HEAD_DIM))

    stacked = (split_heads(query), split_heads(key), split_heads(value), split_heads(head_grad))
    query_grad, key_grad, value_grad = lax.map(one_head, stacked)

    def merge_heads(array):
        return array.transpose(1, 0, 2).reshape(BLOCKS, CTX_ROWS, ATT)

    return (d_resid.reshape(BLOCKS, CTX_ROWS, D), merge_heads(query_grad), merge_heads(key_grad), merge_heads(value_grad))
```

```python
import jax
import jax.numpy as jnp
from jax import lax
from jax.experimental import pallas as pl
from jax.experimental.pallas import tpu as pltpu
from jax.sharding import Mesh
from jax.sharding import PartitionSpec as P

HEAD_DIM = 64
KERNEL = 31
REACH = 2
LANES = 128
QT = 256
HALO = 32
HALF = 16
NEG = -1e30
F32 = jnp.float32
BF16 = jnp.bfloat16
NT_DIMS = (((1,), (1,)), ((), ()))
NN_DIMS = (((1,), (0,)), ((), ()))
VMEM_LIMIT = 56 * 1024 * 1024


def dot(a, b, dims):
    return lax.dot_general(a, b, dims, preferred_element_type=F32)


def call(body, outs, n_in, smem=(), scratch=(), name=None):
    vm = pl.BlockSpec(memory_space=pltpu.VMEM)
    sm = pl.BlockSpec(memory_space=pltpu.SMEM)
    return pl.pallas_call(
        body,
        out_shape=outs,
        in_specs=[sm if i in smem else vm for i in range(n_in)],
        out_specs=jax.tree.map(lambda _: vm, outs),
        scratch_shapes=list(scratch),
        compiler_params=pltpu.CompilerParams(vmem_limit_bytes=VMEM_LIMIT),
        name=name,
    )


def arr(shape, dtype=BF16):
    return jax.ShapeDtypeStruct(shape, dtype)


def swap_pairs(count, distance, phase):
    pairs = []
    for i in range(count - distance):
        if (i // distance) % 2 == phase:
            pairs += [(i, i + distance), (i + distance, i)]
    return pairs


def on_device(sizes, query, key, value, resid_in, out_grad, out_weight, conv_kernel, frame_lengths):
    heads_axis, z_count, group = sizes
    ctx_count = z_count * group
    rows = query.shape[1]
    width = query.shape[2]
    channels = resid_in.shape[2]
    block = rows * heads_axis
    supers = group * block
    members = group * heads_axis
    half = rows // 2
    near = -(-REACH // group)
    window = REACH * block
    tiles = 2 * window // QT + 1
    per_block = block // QT
    lead = near * supers - window
    ext = (2 * near + 1) * supers
    out_cols = channels // heads_axis
    scale = HEAD_DIM ** (-0.5)
    chain = heads_axis * ctx_count

    def head_of(member):
        return group * (member % heads_axis) + member // heads_axis

    def cols(head):
        return slice(head * HEAD_DIM, (head + 1) * HEAD_DIM)

    def edge_body(resid_ref, grad_ref, first_ref, second_ref):
        odd = (lax.axis_index("head") % 2) == 1
        bottom = rows - HALO
        for out_ref, low in ((first_ref, odd), (second_ref, jnp.logical_not(odd))):
            out_ref[0:HALO, :] = jnp.where(low, resid_ref[0, 0:HALO, :], resid_ref[0, bottom:rows, :])
            out_ref[HALO : HALO + HALF, :] = jnp.where(
                low, grad_ref[0, 0:HALF, :], grad_ref[0, rows - HALF : rows, :]
            )

    edges = call(edge_body, [arr((HALO + HALF, channels))] * 2, 2, name="edges")(resid_in, out_grad)

    def place(i):
        return (i % heads_axis) * ctx_count + i // heads_axis

    halos = [
        lax.ppermute(
            edges[phase],
            ("head", "z", "y"),
            [(place(a), place(b)) for a, b in swap_pairs(chain, 1, phase)],
        )
        for phase in (0, 1)
    ]

    def pack_body(q_ref, k_ref, v_ref, out_ref):
        for member in range(members):
            c = cols(head_of(member))
            out_ref[member, 0:rows, 0:HEAD_DIM] = k_ref[0, :, c]
            out_ref[member, 0:rows, HEAD_DIM:LANES] = v_ref[0, :, c]
            out_ref[member, rows : rows + half, 0:HEAD_DIM] = q_ref[0, 0:half, c]
            out_ref[member, rows : rows + half, HEAD_DIM:LANES] = q_ref[0, half:rows, c]

    packed = call(pack_body, arr((members, rows + half, LANES)), 3, name="pack")(query, key, value)
    mine = lax.all_to_all(packed, ("y", "head"), 0, 0, tiled=True)

    span = rows + 2 * HALF

    def conv_body(resid_ref, grad_ref, first_ref, second_ref, taps_ref, weight_ref, dres_ref, hg_ref, low_ref):
        odd = (lax.axis_index("head") % 2) == 1

        def taps_sum(x, tap_of, length):
            total = None
            for b in range(8):
                part = None
                for a in range(4):
                    offset = 8 * a + b
                    if offset < 1 or offset > KERNEL:
                        continue
                    term = tap_of(offset - 1) * x[8 * a : 8 * a + length + 8]
                    part = term if part is None else part + term
                if b:
                    part = pltpu.roll(part, length + 8 - b, 0)
                part = part[0:length]
                total = part if total is None else total + part
            return total

        def chunk(c, carry):
            at = pl.multiple_of(c * LANES, LANES)
            lane = pl.ds(at, LANES)
            first = first_ref[:, lane].astype(F32)
            second = second_ref[:, lane].astype(F32)
            before = jnp.where(odd, first, second)
            after = jnp.where(odd, second, first)
            taps = taps_ref[:, lane].astype(F32)
            x = jnp.concatenate([before[0:HALO], resid_ref[0, :, lane].astype(F32), after[0:HALO]], axis=0)
            middle = grad_ref[0, :, lane].astype(F32)
            g = jnp.concatenate([before[HALO:], middle, after[HALO:]], axis=0)
            pre = taps_sum(x, lambda k: taps[k : k + 1], span)
            s = 1.0 / (1.0 + jnp.exp(-pre))
            cg = g * (s * (1.0 + pre * (1.0 - s)))
            out = middle + taps_sum(cg, lambda k: taps[KERNEL - 1 - k : KERNEL - k], rows)
            low_ref[:, lane] = out.astype(BF16)
            return carry

        lax.fori_loop(0, channels // LANES, chunk, 0)
        for h in range(heads_axis):
            dres_ref[h] = low_ref[:, h * out_cols : (h + 1) * out_cols]
        hg = dot(low_ref[...], weight_ref[...], NT_DIMS).astype(BF16)
        for member in range(members):
            c = cols(head_of(member))
            hg_ref[member, :, 0:HEAD_DIM] = hg[0:half, c]
            hg_ref[member, :, HEAD_DIM:LANES] = hg[half:rows, c]

    dres, hg = call(
        conv_body,
        [arr((heads_axis, rows, out_cols)), arr((members, half, LANES))],
        6,
        scratch=[pltpu.VMEM((rows, channels), BF16)],
        name="conv",
    )(resid_in, out_grad, halos[0], halos[1], conv_kernel, out_weight)
    grads = lax.all_to_all(hg, ("y", "head"), 0, 0, tiled=True)

    both = mine[:, 0:rows, :].reshape(supers, LANES)

    def spread(parts):
        return [
            lax.ppermute(parts[2 * d - 2 + phase], "z", swap_pairs(z_count, d, phase))
            for d in range(1, near + 1)
            for phase in (0, 1)
        ]

    around = spread([both] * (2 * near))
    d_resid = lax.all_to_all(dres, "head", 0, 0, tiled=True).reshape(1, block, out_cols)

    def attn_body(*refs):
        len_ref, mine_ref, hg_ref = refs[:3]
        around_refs = refs[3 : 3 + 2 * near]
        dq_ref, own_ref = refs[3 + 2 * near : 5 + 2 * near]
        back_refs = refs[5 + 2 * near : 5 + 4 * near]
        kv, kt, qz, hz, s_sc, d_sc, acc, dq_sc = refs[5 + 4 * near :]
        z = lax.axis_index("z")
        low = lax.broadcasted_iota(jnp.int32, (half, LANES), 1) < HEAD_DIM
        zero = jnp.zeros((half, LANES), BF16)
        for member in range(members):
            at = member * rows
            kv[near * supers + at : near * supers + at + rows, :] = mine_ref[member, 0:rows, :]
            q = mine_ref[member, rows : rows + half, :].astype(F32) * scale
            qz[at : at + half, :] = jnp.where(low, q, 0.0).astype(BF16)
            qz[at + half : at + rows, :] = jnp.where(low, pltpu.roll(q, HEAD_DIM, 1), 0.0).astype(BF16)
            g = hg_ref[member].astype(F32)
            hz[at : at + half, :] = jnp.where(low, 0.0, pltpu.roll(g, HEAD_DIM, 1)).astype(BF16)
            hz[at + half : at + rows, :] = jnp.where(low, 0.0, g).astype(BF16)
        for d in range(1, near + 1):
            left, right = (near - d) * supers, (near + d) * supers
            odd = ((z // d) % 2) == 1

            @pl.when(odd)
            def _():
                kv[left : left + supers, :] = around_refs[2 * d - 2][...]
                kv[right : right + supers, :] = around_refs[2 * d - 1][...]

            @pl.when(jnp.logical_not(odd))
            def _():
                kv[left : left + supers, :] = around_refs[2 * d - 1][...]
                kv[right : right + supers, :] = around_refs[2 * d - 2][...]

        def turn(t, carry):
            at = pl.multiple_of(t * QT, QT)
            kt[t] = jnp.transpose(kv[pl.ds(at, QT), :].astype(F32))[0:HEAD_DIM].astype(BF16)
            return carry

        lax.fori_loop(0, ext // QT, turn, 0)
        acc[...] = jnp.zeros_like(acc)
        key_at = lax.broadcasted_iota(jnp.int32, (QT, QT), 0)
        query_at = lax.broadcasted_iota(jnp.int32, (QT, QT), 1)

        def fold(x, op):
            return op(x.reshape(QT // 8, 8, QT), axis=0)

        def limit(t):
            index = (z - near) * group + t // per_block
            inside = jnp.logical_and(index >= 0, index < ctx_count)
            length = len_ref[jnp.clip(index, 0, ctx_count - 1)]
            return jnp.where(inside, length, 0) - (t % per_block) * QT

        def query_tile(a, carry):
            q_rows = pl.ds(pl.multiple_of(a * QT, QT), QT)
            q = qz[q_rows, :]
            g = hz[q_rows, :]

            def keys(j):
                return pl.ds(pl.multiple_of((a + j) * QT + lead, QT), QT)

            top = jnp.full((8, QT), NEG, F32)
            for j in range(tiles):
                s = dot(kv[keys(j), :], q, NT_DIMS)
                live = key_at < limit(a + j + lead // QT)
                if j == 0:
                    live = jnp.logical_and(live, key_at >= query_at)
                if j == tiles - 1:
                    live = jnp.logical_and(live, key_at <= query_at)
                s = jnp.where(live, s, NEG)
                s_sc[j] = s
                top = jnp.maximum(top, fold(s, jnp.max))
            top = jnp.max(top, axis=0, keepdims=True)
            mass = jnp.zeros((8, QT), F32)
            weighted = jnp.zeros((8, QT), F32)
            for j in range(tiles):
                e = jnp.exp(s_sc[j] - top)
                slopes = dot(kv[keys(j), :], g, NT_DIMS)
                s_sc[j] = e
                d_sc[j] = slopes
                mass = mass + fold(e, jnp.sum)
                weighted = weighted + fold(e * slopes, jnp.sum)
            inverse = 1.0 / jnp.sum(mass, axis=0, keepdims=True)
            delta = jnp.sum(weighted, axis=0, keepdims=True) * inverse
            dq = jnp.zeros((HEAD_DIM, QT), F32)
            for j in range(tiles):
                p = s_sc[j] * inverse
                ds = (p * (d_sc[j] - delta)).astype(BF16)
                acc[keys(j), :] += dot(ds, q, NN_DIMS) + dot(p.astype(BF16), g, NN_DIMS)
                dq = dq + dot(kt[a + j + lead // QT], ds, NN_DIMS)
            dq_sc[q_rows, :] = jnp.transpose(dq * scale).astype(BF16)
            return carry

        lax.fori_loop(0, supers // QT, query_tile, 0)
        own_ref[...] = acc[near * supers : (near + 1) * supers, :]
        for d in range(1, near + 1):
            left, right = (near - d) * supers, (near + d) * supers
            odd = ((z // d) % 2) == 1

            @pl.when(odd)
            def _():
                back_refs[2 * d - 2][...] = acc[left : left + supers, :].astype(BF16)
                back_refs[2 * d - 1][...] = acc[right : right + supers, :].astype(BF16)

            @pl.when(jnp.logical_not(odd))
            def _():
                back_refs[2 * d - 1][...] = acc[left : left + supers, :].astype(BF16)
                back_refs[2 * d - 2][...] = acc[right : right + supers, :].astype(BF16)

        if group == 1:
            dq_ref[0] = dq_sc[...]
        else:
            for b in range(group):
                at = b * block
                mid = at + block // 2
                dq_ref[b, :, 0:HEAD_DIM] = dq_sc[at:mid, :]
                dq_ref[b, :, HEAD_DIM:LANES] = dq_sc[mid : at + block, :]

    dq_shape = (1, supers, HEAD_DIM) if group == 1 else (group, block // 2, LANES)
    outs = call(
        attn_body,
        [arr(dq_shape), arr((supers, LANES), F32)] + [arr((supers, LANES))] * (2 * near),
        3 + 2 * near,
        smem=(0,),
        scratch=[
            pltpu.VMEM((ext, LANES), BF16),
            pltpu.VMEM((ext // QT, HEAD_DIM, QT), BF16),
            pltpu.VMEM((supers, LANES), BF16),
            pltpu.VMEM((supers, LANES), BF16),
            pltpu.VMEM((tiles, QT, QT), F32),
            pltpu.VMEM((tiles, QT, QT), F32),
            pltpu.VMEM((ext, LANES), F32),
            pltpu.VMEM((supers, HEAD_DIM), BF16),
        ],
        name="attn",
    )(frame_lengths, mine, grads, *around)
    dq, own = outs[:2]
    back = spread(outs[2:])

    if group == 1:

        def last_body(*refs):
            total = refs[0][...]
            for ref in refs[1 : 1 + 2 * near]:
                total = total + ref[...].astype(F32)
            total = total.astype(BF16)
            refs[-2][0] = total[:, 0:HEAD_DIM]
            refs[-1][0] = total[:, HEAD_DIM:LANES]

        d_key, d_value = call(last_body, [arr((1, block, HEAD_DIM))] * 2, 1 + 2 * near, name="last")(own, *back)
        return d_resid, dq, d_key, d_value

    hb = block // 2

    def sum_body(*refs):
        dq_ref, own_ref = refs[:2]
        part_refs = refs[2 : 2 + 2 * near]
        keep_ref, send_ref = refs[2 + 2 * near :]
        y = lax.axis_index("y")
        for slot, out_ref in ((y, keep_ref), (1 - y, send_ref)):
            take = pl.ds(pl.multiple_of(slot * block, block), block)
            total = own_ref[take, :]
            for ref in part_refs:
                total = total + ref[take, :].astype(F32)
            out_ref[0:block, :] = total.astype(BF16)
            out_ref[block : block + hb, :] = dq_ref[slot]

    keep, send = call(sum_body, [arr((block + hb, LANES))] * 2, 2 + 2 * near, name="sum")(dq, own, *back)
    other = lax.ppermute(send, "y", [(0, 1), (1, 0)])

    def last_body(keep_ref, other_ref, dq_ref, dk_ref, dv_ref):
        y = lax.axis_index("y")

        def put(lo_ref, up_ref):
            lo, up = lo_ref[0:block, :], up_ref[0:block, :]
            dk_ref[0, :, 0:HEAD_DIM] = lo[:, 0:HEAD_DIM]
            dk_ref[0, :, HEAD_DIM:LANES] = up[:, 0:HEAD_DIM]
            dv_ref[0, :, 0:HEAD_DIM] = lo[:, HEAD_DIM:LANES]
            dv_ref[0, :, HEAD_DIM:LANES] = up[:, HEAD_DIM:LANES]
            for ref, at in ((lo_ref, 0), (up_ref, HEAD_DIM)):
                dq_ref[0, 0:hb, at : at + HEAD_DIM] = ref[block : block + hb, 0:HEAD_DIM]
                dq_ref[0, hb:block, at : at + HEAD_DIM] = ref[block : block + hb, HEAD_DIM:LANES]

        @pl.when(y == 0)
        def _():
            put(keep_ref, other_ref)

        @pl.when(y == 1)
        def _():
            put(other_ref, keep_ref)

    d_query, d_key, d_value = call(last_body, [arr((1, block, LANES))] * 3, 2, name="last")(keep, other)
    return d_resid, d_query, d_key, d_value


def solution(mesh):
    heads_axis = mesh.shape["head"]
    ctx_count = mesh.shape["ctx"]

    def run(query, *rest):
        group = query.shape[2] // HEAD_DIM // heads_axis
        z_count = ctx_count // group
        fine = Mesh(mesh.devices.reshape(heads_axis, z_count, group), ("head", "z", "y"))
        rows_spec = P(("z", "y"), "head", None)
        cols_spec = P(("z", "y"), None, "head")
        sizes = (heads_axis, z_count, group)
        return jax.shard_map(
            lambda *args: on_device(sizes, *args),
            mesh=fine,
            in_specs=(rows_spec,) * 5 + (P(),) * 3,
            out_specs=(cols_spec,) * 4,
            check_vma=False,
        )(query, *rest)

    return run
```

```python
import jax
import jax.numpy as jnp
from jax import lax
from jax.experimental import pallas as pl
from jax.experimental.pallas import tpu as pltpu
from jax.sharding import Mesh
from jax.sharding import PartitionSpec as P

HEAD_DIM = 64
KERNEL = 31
REACH = 2
LANES = 128
QT = 256
HALO = 32
HALF = 16
NEG = -1e30
F32 = jnp.float32
BF16 = jnp.bfloat16
NT_DIMS = (((1,), (1,)), ((), ()))
NN_DIMS = (((1,), (0,)), ((), ()))
VMEM_LIMIT = 12 * 1024 * 1024
CONV_COST = (6_000_000_000, 0, 0)
SCORES_COST = (9_000_000_000, 0, 0)
FAR_COST = (4_000_000_000, 0, 0)
NEAR_COST = (4_000_000_000, 0, 0)


def dot(a, b, dims):
    return lax.dot_general(a, b, dims, preferred_element_type=F32)


def call(body, outs, smem=(), scratch=(), name=None, cost=None):
    on_vmem = pl.BlockSpec(memory_space=pltpu.VMEM)
    on_smem = pl.BlockSpec(memory_space=pltpu.SMEM)

    def run(*args):
        return pl.pallas_call(
            body,
            out_shape=outs,
            in_specs=[on_smem if i in smem else on_vmem for i in range(len(args))],
            out_specs=[on_vmem] * len(outs),
            scratch_shapes=list(scratch),
            compiler_params=pltpu.CompilerParams(vmem_limit_bytes=VMEM_LIMIT),
            cost_estimate=None if cost is None else pl.CostEstimate(*cost),
            name=name,
        )(*args)

    return run


def arr(shape, dtype=BF16):
    return jax.ShapeDtypeStruct(shape, dtype)


def vmem(shape, dtype=BF16):
    return pltpu.VMEM(shape, dtype)


def on_chip(*arrays):
    return [pltpu.with_memory_space_constraint(x, pltpu.VMEM) for x in arrays]


def in_hbm(*arrays):
    return [pltpu.with_memory_space_constraint(x, pltpu.HBM) for x in arrays]


def swap_pairs(count, distance, phase):
    pairs = []
    for i in range(count - distance):
        if (i // distance) % 2 == phase:
            pairs += [(i, i + distance), (i + distance, i)]
    return pairs


def on_device(sizes, query, key, value, resid_in, out_grad, out_weight, conv_kernel, frame_lengths):
    heads_axis, z_count, group = sizes
    ctx_count = z_count * group
    rows = query.shape[1]
    width = query.shape[2]
    channels = resid_in.shape[2]
    block = rows * heads_axis
    supers = group * block
    members = group * heads_axis
    chips = members // 2
    half = rows // 2
    near = -(-REACH // group)
    window = REACH * block
    tiles = 2 * window // QT + 1
    per_block = block // QT
    lead = near * supers - window
    ext = (2 * near + 1) * supers
    out_cols = channels // heads_axis
    scale = HEAD_DIM ** (-0.5)
    chain = heads_axis * ctx_count

    def head_of(member):
        return group * (member % heads_axis) + member // heads_axis

    def cols(head):
        return slice(head * HEAD_DIM, (head + 1) * HEAD_DIM)

    def sides(core, slots):
        first, second = slots
        return jnp.where(core == 0, first, second), jnp.where(core == 0, second, first)

    def member_of(chip, core):
        return chip * 2 + core

    def my_chip():
        return lax.axis_index("y") * (heads_axis // 2) + lax.axis_index("head") // 2

    def my_core():
        return lax.axis_index("head") % 2

    def pack_body(
        q_ref, k_ref, v_ref, resid_ref, grad_ref, taps_ref, weight_ref,
        keep_ref, send_ref, first_ref, second_ref, resid_out, grad_out, taps_out, weight_out, sems,
    ):
        copies = [
            pltpu.make_async_copy(source, target, sems.at[i])
            for i, (source, target) in enumerate(
                ((resid_ref, resid_out), (grad_ref, grad_out), (taps_ref, taps_out), (weight_ref, weight_out))
            )
        ]
        for copy in copies:
            copy.start()
        core = my_core()
        for chip in range(chips):
            heads = [cols(head_of(member_of(chip, c))) for c in (0, 1)]
            for at, width, c_ref, low, high in (
                (0, 0, k_ref, 0, rows),
                (0, HEAD_DIM, v_ref, 0, rows),
                (rows, 0, q_ref, 0, half),
                (rows, HEAD_DIM, q_ref, half, rows),
            ):
                stay, leave = sides(core, [c_ref[0, low:high, c] for c in heads])
                keep_ref[chip, at : at + high - low, width : width + HEAD_DIM] = stay
                send_ref[chip, at : at + high - low, width : width + HEAD_DIM] = leave
        copies[0].wait()
        copies[1].wait()
        odd = core == 1
        for side_ref, low in ((first_ref, odd), (second_ref, jnp.logical_not(odd))):
            side_ref[0:HALO, :] = jnp.where(low, resid_out[0, 0:HALO, :], resid_out[0, rows - HALO : rows, :])
            side_ref[HALO : HALO + HALF, :] = jnp.where(
                low, grad_out[0, 0:HALF, :], grad_out[0, rows - HALF : rows, :]
            )
        copies[2].wait()
        copies[3].wait()

    slot = rows + half
    raw = pl.BlockSpec(memory_space=pltpu.HBM)
    on_vmem = pl.BlockSpec(memory_space=pltpu.VMEM)
    pack_outs = [
        vmem((chips, slot, LANES)), vmem((chips, slot, LANES)),
        vmem((HALO + HALF, channels)), vmem((HALO + HALF, channels)),
        vmem((1, rows, channels)), vmem((1, rows, channels)),
        vmem(conv_kernel.shape), vmem(out_weight.shape),
    ]
    keep, send, first, second, resid, upstream, taps_in, weight_in = pl.pallas_call(
        pack_body,
        out_shape=pack_outs,
        in_specs=[on_vmem] * 3 + [raw] * 4,
        out_specs=[on_vmem] * 8,
        scratch_shapes=[pltpu.SemaphoreType.DMA((4,))],
        compiler_params=pltpu.CompilerParams(vmem_limit_bytes=VMEM_LIMIT),
        name="pack",
    )(*in_hbm(query, key, value, resid_in, out_grad, conv_kernel, out_weight))

    mesh_axes = ("head", "z", "y")

    def place(head, z, y):
        return head * ctx_count + z * group + y

    def everyone(target):
        return [
            (place(h, z, y), place(*target(h, z, y)))
            for h in range(heads_axis)
            for z in range(z_count)
            for y in range(group)
        ]

    def core_swap(x):
        return lax.ppermute(x, mesh_axes, everyone(lambda h, z, y: (h ^ 1, z, y)))

    def exchange(keep, got, count, index, name):
        def body(keep_ref, got_ref, *out_refs):
            me = index()
            for m, out_ref in enumerate(out_refs, 1):
                out_ref[0] = keep_ref[me ^ m]
                out_ref[1] = got_ref[me ^ m]

        per_row = heads_axis // 2

        def target(m):
            def f(h, z, y):
                chip = (y * per_row + h // 2) ^ m
                return (chip % per_row) * 2 + h % 2, z, chip // per_row

            return f

        parts = call(body, [vmem((2,) + keep.shape[1:])] * (count - 1), name=name)(*on_chip(keep, got))
        return [lax.ppermute(part, mesh_axes, everyone(target(m))) for m, part in enumerate(parts, 1)]

    def arrivals(me, core, keep_ref, got_ref, part_refs):
        out = [(member_of(me, core), lambda: keep_ref[me]), (member_of(me, 1 - core), lambda: got_ref[me])]
        for m, ref in enumerate(part_refs, 1):
            out.append((member_of(me ^ m, core), lambda ref=ref: ref[0]))
            out.append((member_of(me ^ m, 1 - core), lambda ref=ref: ref[1]))
        return out

    got = core_swap(send)

    def chain_place(i):
        return place(i % heads_axis, i // heads_axis // group, i // heads_axis % group)

    halos = [
        lax.ppermute(side, mesh_axes, [(chain_place(a), chain_place(b)) for a, b in swap_pairs(chain, 1, phase)])
        for phase, side in enumerate((first, second))
    ]
    mine = [keep, got] + exchange(keep, got, chips, my_chip, "regroup")

    def keys_body(keep_ref, got_ref, *refs):
        out_ref = refs[-1]
        for member, take in arrivals(my_chip(), my_core(), keep_ref, got_ref, refs[:-1]):
            out_ref[pl.ds(pl.multiple_of(member * rows, rows), rows), :] = take()[0:rows]

    (both,) = call(keys_body, [vmem((supers, LANES))], name="keys")(*on_chip(*mine))

    steps = [(d, phase) for d in range(1, near + 1) for phase in (0, 1)]
    around = [lax.ppermute(both, "z", swap_pairs(z_count, d, phase)) for d, phase in steps]

    span = rows + 2 * HALF

    def conv_body(
        resid_ref, grad_ref, first_ref, second_ref, taps_ref, weight_ref,
        hg_keep, hg_send, dres_keep, dres_send, low_ref,
    ):
        odd = (lax.axis_index("head") % 2) == 1

        def taps_sum(x, tap_of, length):
            total = None
            for b in range(8):
                part = None
                for a in range(4):
                    offset = 8 * a + b
                    if offset < 1 or offset > KERNEL:
                        continue
                    term = tap_of(offset - 1) * x[8 * a : 8 * a + length + 8]
                    part = term if part is None else part + term
                if b:
                    part = pltpu.roll(part, length + 8 - b, 0)
                part = part[0:length]
                total = part if total is None else total + part
            return total

        def chunk(c, carry):
            at = pl.multiple_of(c * LANES, LANES)
            lane = pl.ds(at, LANES)
            first = first_ref[:, lane].astype(F32)
            second = second_ref[:, lane].astype(F32)
            before = jnp.where(odd, first, second)
            after = jnp.where(odd, second, first)
            taps = taps_ref[:, lane].astype(F32)
            x = jnp.concatenate([before[0:HALO], resid_ref[0, :, lane].astype(F32), after[0:HALO]], axis=0)
            middle = grad_ref[0, :, lane].astype(F32)
            g = jnp.concatenate([before[HALO:], middle, after[HALO:]], axis=0)
            pre = taps_sum(x, lambda k: taps[k : k + 1], span)
            s = 1.0 / (1.0 + jnp.exp(-pre))
            cg = g * (s * (1.0 + pre * (1.0 - s)))
            out = middle + taps_sum(cg, lambda k: taps[KERNEL - 1 - k : KERNEL - k], rows)
            low_ref[:, lane] = out.astype(BF16)
            return carry

        lax.fori_loop(0, channels // LANES, chunk, 0)
        core = my_core()
        for x in range(heads_axis // 2):
            dres_keep[x], dres_send[x] = sides(
                core, [low_ref[:, h * out_cols : (h + 1) * out_cols] for h in (2 * x, 2 * x + 1)]
            )
        hg = dot(low_ref[...], weight_ref[...], NT_DIMS).astype(BF16)
        for chip in range(chips):
            heads = [cols(head_of(member_of(chip, c))) for c in (0, 1)]
            for at, part in ((0, slice(0, half)), (HEAD_DIM, slice(half, rows))):
                stay, leave = sides(core, [hg[part, c] for c in heads])
                hg_keep[chip, :, at : at + HEAD_DIM] = stay
                hg_send[chip, :, at : at + HEAD_DIM] = leave

    hg_keep, hg_send, dres_keep, dres_send = call(
        conv_body,
        [vmem((chips, half, LANES))] * 2 + [vmem((heads_axis // 2, rows, out_cols))] * 2,
        scratch=[pltpu.VMEM((rows, channels), BF16)],
        name="conv",
        cost=CONV_COST,
    )(*on_chip(resid, upstream, *halos, taps_in, weight_in))
    hg_got = core_swap(hg_send)
    grads = [hg_keep, hg_got] + exchange(hg_keep, hg_got, chips, my_chip, "regroup_grads")
    dres_got = core_swap(dres_send)
    dres = [dres_keep, dres_got] + exchange(
        dres_keep, dres_got, heads_axis // 2, lambda: lax.axis_index("head") // 2, "regroup_resid"
    )
    n_dres = len(dres)
    dres_shape = arr((1, block, out_cols))

    def resid_out(refs, out_ref):
        for member, take in arrivals(lax.axis_index("head") // 2, my_core(), refs[0], refs[1], refs[2:]):
            out_ref[0, pl.ds(pl.multiple_of(member * rows, rows), rows), :] = take()

    q_tiles = supers // QT
    k_tiles = ext // QT
    first_tile = lead // QT
    own_tiles = range(near * q_tiles, (near + 1) * q_tiles)

    def seen(a):
        return range(a + first_tile, a + first_tile + tiles)

    def at_tile(t):
        return slice(t * QT, (t + 1) * QT)

    def score_body(*refs):
        len_ref, both_ref = refs[:2]
        mine_refs = refs[2 : 3 + chips]
        around_refs = refs[3 + chips : 3 + chips + 2 * near]
        e_ref, inv_ref, out_ref, kv, kvt, qz, kb, qs = refs[3 + chips + 2 * near :]
        z = lax.axis_index("z")
        low = lax.broadcasted_iota(jnp.int32, (half, LANES), 1) < HEAD_DIM
        lane = lax.broadcasted_iota(jnp.int32, (half, LANES), 1)
        kv[near * supers : (near + 1) * supers, :] = both_ref[...]
        for member, take in arrivals(my_chip(), my_core(), mine_refs[0], mine_refs[1], mine_refs[2:]):
            q = take()[rows:slot].astype(F32) * scale
            for i, part in enumerate((q, pltpu.roll(q, HEAD_DIM, 1))):
                at = pl.ds(pl.multiple_of(member * rows + i * half, half), half)
                part = jnp.where(low, part, 0.0)
                qz[at, :] = part.astype(BF16)
                qs[at, :] = jnp.where(lane == HEAD_DIM, 1.0, part).astype(BF16)
        for d in range(1, near + 1):
            left, right = (near - d) * supers, (near + d) * supers
            odd = ((z // d) % 2) == 1

            @pl.when(odd)
            def _():
                kv[left : left + supers, :] = around_refs[2 * d - 2][...]
                kv[right : right + supers, :] = around_refs[2 * d - 1][...]

            @pl.when(jnp.logical_not(odd))
            def _():
                kv[left : left + supers, :] = around_refs[2 * d - 1][...]
                kv[right : right + supers, :] = around_refs[2 * d - 2][...]

        def limit(t):
            index = (z - near) * group + t // per_block
            inside = jnp.logical_and(index >= 0, index < ctx_count)
            length = len_ref[jnp.clip(index, 0, ctx_count - 1)]
            return jnp.where(inside, length, 0) - (t % per_block) * QT

        tile_lane = lax.broadcasted_iota(jnp.int32, (QT, LANES), 1)
        tile_row = lax.broadcasted_iota(jnp.int32, (QT, LANES), 0)

        def turn(t, carry):
            at = pl.ds(pl.multiple_of(t * QT, QT), QT)
            tile = kv[at, :].astype(F32)
            kvt[t] = jnp.transpose(tile).astype(BF16)
            dead = jnp.logical_and(tile_lane == HEAD_DIM, tile_row >= limit(t))
            kb[at, :] = jnp.where(tile_lane < HEAD_DIM, tile, jnp.where(dead, NEG, 0.0)).astype(BF16)
            return carry

        lax.fori_loop(0, k_tiles, turn, 0)
        key_at = lax.broadcasted_iota(jnp.int32, (QT, QT), 0)
        query_at = lax.broadcasted_iota(jnp.int32, (QT, QT), 1)

        def fold(x, op):
            return op(x.reshape(QT // 8, 8, QT), axis=0)

        def query_tile(a, carry):
            q = qs[pl.ds(pl.multiple_of(a * QT, QT), QT), :]
            e_at = a * tiles
            top = jnp.full((8, QT), NEG, F32)
            for j in range(tiles):
                t = a + j + first_tile
                s = dot(kb[pl.ds(pl.multiple_of(t * QT, QT), QT), :], q, NT_DIMS)
                if j == 0:
                    s = jnp.where(key_at >= query_at, s, NEG)
                if j == tiles - 1:
                    s = jnp.where(key_at <= query_at, s, NEG)
                e_ref[e_at + j] = s
                top = jnp.maximum(top, fold(s, jnp.max))
            top = jnp.max(top, axis=0, keepdims=True)
            mass = jnp.zeros((8, QT), F32)
            out = jnp.zeros((HEAD_DIM, QT), F32)
            for j in range(tiles):
                e = jnp.exp(e_ref[e_at + j] - top)
                e_ref[e_at + j] = e
                mass = mass + fold(e, jnp.sum)
                out = out + dot(kvt[a + j + first_tile, HEAD_DIM:LANES, :], e.astype(BF16), NN_DIMS)
            inverse = 1.0 / jnp.sum(mass, axis=0, keepdims=True)
            inv_ref[a] = inverse
            out_ref[a] = out * inverse
            return carry

        lax.fori_loop(0, q_tiles, query_tile, 0)

    exps, inverse, outs, kv, kvt, qz = call(
        score_body,
        [
            vmem((q_tiles * tiles, QT, QT), F32),
            vmem((q_tiles, 1, QT), F32),
            vmem((q_tiles, HEAD_DIM, QT), F32),
            vmem((ext, LANES)),
            vmem((k_tiles, LANES, QT)),
            vmem((supers, LANES)),
        ],
        smem=(0,),
        scratch=[pltpu.VMEM((ext, LANES), BF16), pltpu.VMEM((supers, LANES), BF16)],
        name="scores",
        cost=SCORES_COST,
    )(frame_lengths, *on_chip(both, *mine, *around))

    def key_tile(t, e_ref, inv_ref, delta_ref, kv, kvt, qz, hz, dq):
        total = None
        for a in range(q_tiles):
            if t not in seen(a):
                continue
            q = qz[at_tile(a), :]
            g = hz[at_tile(a), :]
            p = e_ref[a * tiles + t - a - first_tile] * inv_ref[a]
            slopes = dot(kv[at_tile(t), :], g, NT_DIMS)
            ds = (p * (slopes - delta_ref[a])).astype(BF16)
            part = dot(ds, q, NN_DIMS) + dot(p.astype(BF16), g, NN_DIMS)
            total = part if total is None else total + part
            dq[a] += dot(kvt[t, 0:HEAD_DIM, :], ds, NN_DIMS)
        return jnp.zeros((QT, LANES), F32) if total is None else total

    n_back = 2 * near * group

    def far_body(*refs):
        grad_refs = refs[: 1 + chips]
        e_ref, inv_ref, out_ref, kv, kvt, qz, hz, delta_ref, dq = refs[1 + chips : 10 + chips]
        back_refs = refs[10 + chips : -1]
        acc = refs[-1]
        z, y = lax.axis_index("z"), lax.axis_index("y")
        low = lax.broadcasted_iota(jnp.int32, (half, LANES), 1) < HEAD_DIM
        for member, take in arrivals(my_chip(), my_core(), grad_refs[0], grad_refs[1], grad_refs[2:]):
            g = take().astype(F32)
            for i, part in enumerate((pltpu.roll(g, HEAD_DIM, 1), g)):
                at = pl.ds(pl.multiple_of(member * rows + i * half, half), half)
                hz[at, :] = jnp.where(low, 0.0, part).astype(BF16)
        for a in range(q_tiles):
            g = jnp.transpose(hz[at_tile(a), :].astype(F32))[HEAD_DIM:LANES]
            delta_ref[a] = jnp.sum(g * out_ref[a], axis=0, keepdims=True)
        dq[...] = jnp.zeros_like(dq)
        for t in range(k_tiles):
            if t not in own_tiles:
                acc[at_tile(t), :] = key_tile(t, e_ref, inv_ref, delta_ref, kv, kvt, qz, hz, dq)
        for i, (d, phase) in enumerate(steps):
            odd = ((z // d) % 2) == 1
            right = odd if phase else jnp.logical_not(odd)
            side = jnp.where(right, near + d, near - d) * supers
            for cross in range(group):
                slot = jnp.where(cross == 1, 1 - y, y)
                take = pl.ds(pl.multiple_of(side + slot * block, block), block)
                back_refs[i * group + cross][...] = acc[take, :].astype(BF16)

    far = call(
        far_body,
        [vmem((supers, LANES)), vmem((q_tiles, 1, QT), F32), vmem((q_tiles, HEAD_DIM, QT), F32)]
        + [vmem((block, LANES))] * n_back,
        scratch=[pltpu.VMEM((ext, LANES), F32)],
        name="far",
        cost=FAR_COST,
    )(*on_chip(*grads, exps, inverse, outs, kv, kvt, qz))
    hz, delta, dq_far = far[:3]

    def across(d, phase, cross):
        return [
            (a * group + i, b * group + (i ^ cross))
            for a, b in swap_pairs(z_count, d, phase)
            for i in range(group)
        ]

    back = [
        lax.ppermute(far[3 + i * group + cross], ("z", "y"), across(d, phase, cross))
        for i, (d, phase) in enumerate(steps)
        for cross in range(group)
    ]

    hb = block // 2
    sent = (group - 1) * (block + hb)

    def near_body(*refs):
        e_ref, inv_ref, delta_ref, kv, kvt, qz, hz, far_ref = refs[:8]
        keep_ref, dq_ref = refs[8:10]
        acc, dq, dq_sc = refs[-3:]
        y = lax.axis_index("y")
        dq[...] = far_ref[...]
        for t in own_tiles:
            acc[at_tile(t - near * q_tiles), :] = key_tile(t, e_ref, inv_ref, delta_ref, kv, kvt, qz, hz, dq)
        for a in range(q_tiles):
            dq_sc[at_tile(a), 0:HEAD_DIM] = jnp.transpose(dq[a] * scale)
        if group == 1:
            keep_ref[...] = acc[...]
            dq_ref[0] = dq_sc[:, 0:HEAD_DIM].astype(BF16)
            return
        send_ref = refs[10]
        keep_at = pl.multiple_of(y * block, block)
        send_at = pl.multiple_of((1 - y) * block, block)
        keep_ref[...] = acc[pl.ds(keep_at, block), :]
        send_ref[0:block, :] = acc[pl.ds(send_at, block), :].astype(BF16)
        for ref, at, base in ((dq_ref, keep_at, 0), (send_ref, send_at, block)):
            upper = dq_sc[pl.ds(at, hb), 0:HEAD_DIM]
            lower = dq_sc[pl.ds(pl.multiple_of(at + hb, hb), hb), 0:HEAD_DIM]
            ref[base : base + hb, :] = jnp.concatenate([upper, lower], axis=1).astype(BF16)

    results = call(
        near_body,
        [vmem((block, LANES), F32)]
        + ([arr((1, block, HEAD_DIM))] if group == 1 else [vmem((hb, LANES)), vmem((sent, LANES))]),
        scratch=[
            pltpu.VMEM((supers, LANES), F32),
            pltpu.VMEM((q_tiles, HEAD_DIM, QT), F32),
            pltpu.VMEM((supers, LANES), F32),
        ],
        name="near",
        cost=NEAR_COST,
    )(*on_chip(exps, inverse, delta, kv, kvt, qz, hz, dq_far))
    keep, dq = results[:2]

    if group == 1:

        def last_body(*refs):
            total = refs[0][...]
            for ref in refs[1 : 1 + n_back]:
                total = total + ref[...].astype(F32)
            total = total.astype(BF16)
            refs[-2][0] = total[:, 0:HEAD_DIM]
            refs[-1][0] = total[:, HEAD_DIM:LANES]
            resid_out(refs[1 + n_back : 1 + n_back + n_dres], refs[-3])

        d_resid, d_key, d_value = call(last_body, [dres_shape] + [arr((1, block, HEAD_DIM))] * 2, name="last")(
            *on_chip(keep, *back, *dres)
        )
        return d_resid, dq, d_key, d_value

    other = lax.ppermute(results[2], "y", [(0, 1), (1, 0)])

    def last_body(*refs):
        keep_ref, dq_keep_ref, other_ref = refs[:3]
        back_refs = refs[3 : 3 + n_back]
        dres_refs = refs[3 + n_back : 3 + n_back + n_dres]
        dres_ref, dq_ref, dk_ref, dv_ref = refs[3 + n_back + n_dres :]
        resid_out(dres_refs, dres_ref)
        y = lax.axis_index("y")
        own = keep_ref[...]
        peer = other_ref[0:block, :].astype(F32)
        for i in range(2 * near):
            own = own + back_refs[2 * i][...].astype(F32)
            peer = peer + back_refs[2 * i + 1][...].astype(F32)
        first = y == 0
        lo = jnp.where(first, own, peer)
        up = jnp.where(first, peer, own)
        low = lax.broadcasted_iota(jnp.int32, (block, LANES), 1) < HEAD_DIM
        dk_ref[0] = jnp.where(low, lo, pltpu.roll(up, HEAD_DIM, 1)).astype(BF16)
        dv_ref[0] = jnp.where(low, pltpu.roll(lo, HEAD_DIM, 1), up).astype(BF16)
        own = dq_keep_ref[...].astype(F32)
        peer = other_ref[block : block + hb, :].astype(F32)
        lo = jnp.where(first, own, peer)
        up = jnp.where(first, peer, own)
        low = low[0:hb]
        dq_ref[0, 0:hb, :] = jnp.where(low, lo, pltpu.roll(up, HEAD_DIM, 1)).astype(BF16)
        dq_ref[0, hb:block, :] = jnp.where(low, pltpu.roll(lo, HEAD_DIM, 1), up).astype(BF16)

    d_resid, d_query, d_key, d_value = call(
        last_body, [dres_shape] + [arr((1, block, LANES))] * 3, name="last"
    )(*on_chip(keep, dq, other, *back, *dres))
    return d_resid, d_query, d_key, d_value


def solution(mesh):
    heads_axis = mesh.shape["head"]
    ctx_count = mesh.shape["ctx"]

    def run(query, *rest):
        group = query.shape[2] // HEAD_DIM // heads_axis
        z_count = ctx_count // group
        fine = Mesh(mesh.devices.reshape(heads_axis, z_count, group), ("head", "z", "y"))
        rows_spec = P(("z", "y"), "head", None)
        cols_spec = P(("z", "y"), None, "head")
        sizes = (heads_axis, z_count, group)
        return jax.shard_map(
            lambda *args: on_device(sizes, *args),
            mesh=fine,
            in_specs=(rows_spec,) * 5 + (P(),) * 3,
            out_specs=(cols_spec,) * 4,
            check_vma=False,
        )(query, *rest)

    return run
```

```python
import jax
import jax.numpy as jnp
from jax import lax
from jax.experimental import pallas as pl
from jax.experimental.pallas import tpu as pltpu
from jax.sharding import Mesh
from jax.sharding import PartitionSpec as P

HEAD_DIM = 64
KERNEL = 31
REACH = 2
LANES = 128
QT = 256
HALO = 32
HALF = 16
NEG = -1e30
ONES = 16
F32 = jnp.float32
BF16 = jnp.bfloat16
NT_DIMS = (((1,), (1,)), ((), ()))
NN_DIMS = (((1,), (0,)), ((), ()))
VMEM_LIMIT = 12 * 1024 * 1024
CONV_COST = (6_000_000_000, 0, 0)
SCORES_COST = (9_000_000_000, 0, 0)
FAR_COST = (4_000_000_000, 0, 0)
NEAR_COST = (4_000_000_000, 0, 0)


def dot(a, b, dims):
    return lax.dot_general(a, b, dims, preferred_element_type=F32)


def call(body, outs, smem=(), raw=(), scratch=(), name=None, cost=None):
    on_vmem = pl.BlockSpec(memory_space=pltpu.VMEM)
    spaces = {i: pltpu.SMEM for i in smem} | {i: pltpu.HBM for i in raw}

    def run(*args):
        return pl.pallas_call(
            body,
            out_shape=outs,
            in_specs=[pl.BlockSpec(memory_space=spaces.get(i, pltpu.VMEM)) for i in range(len(args))],
            out_specs=[on_vmem] * len(outs),
            scratch_shapes=list(scratch),
            compiler_params=pltpu.CompilerParams(vmem_limit_bytes=VMEM_LIMIT),
            cost_estimate=None if cost is None else pl.CostEstimate(*cost),
            name=name,
        )(*args)

    return run


def arr(shape, dtype=BF16):
    return jax.ShapeDtypeStruct(shape, dtype)


def vmem(shape, dtype=BF16):
    return pltpu.VMEM(shape, dtype)


def on_chip(*arrays):
    return [pltpu.with_memory_space_constraint(x, pltpu.VMEM) for x in arrays]


def in_hbm(*arrays):
    return [pltpu.with_memory_space_constraint(x, pltpu.HBM) for x in arrays]


def on_device(sizes, query, key, value, resid_in, out_grad, out_weight, conv_kernel, frame_lengths):
    heads_axis, z_count, group = sizes
    ctx_count = z_count * group
    rows = query.shape[1]
    width = query.shape[2]
    channels = resid_in.shape[2]
    block = rows * heads_axis
    supers = group * block
    members = group * heads_axis
    chips = members // 2
    half = rows // 2
    near = -(-REACH // group)
    window = REACH * block
    tiles = 2 * window // QT + 1
    per_block = block // QT
    lead = near * supers - window
    ext = (2 * near + 1) * supers
    out_cols = channels // heads_axis
    scale = HEAD_DIM ** (-0.5)

    def head_of(member):
        return group * (member % heads_axis) + member // heads_axis

    def cols(head):
        return slice(head * HEAD_DIM, (head + 1) * HEAD_DIM)

    def sides(core, slots):
        first, second = slots
        return jnp.where(core == 0, first, second), jnp.where(core == 0, second, first)

    def member_of(chip, core):
        return chip * 2 + core

    def my_chip():
        return lax.axis_index("y") * (heads_axis // 2) + lax.axis_index("head") // 2

    def my_core():
        return lax.axis_index("head") % 2

    def pack_body(q_hbm, k_hbm, v_hbm, resid_ref, grad_ref, taps_ref, *refs):
        keep_ref, send_ref, first_ref, second_ref, resid_out, grad_out, taps_out, q_ref, k_ref, v_ref, sems = refs
        copies = [
            pltpu.make_async_copy(source, target, sems.at[i])
            for i, (source, target) in enumerate(
                (
                    (resid_ref, resid_out), (grad_ref, grad_out), (k_hbm, k_ref), (v_hbm, v_ref),
                    (q_hbm, q_ref), (taps_ref, taps_out),
                )
            )
        ]
        for copy in copies:
            copy.start()
        core = my_core()
        copies[0].wait()
        copies[1].wait()
        odd = core == 1
        for side_ref, low in ((first_ref, odd), (second_ref, jnp.logical_not(odd))):
            side_ref[0:HALO, :] = jnp.where(low, resid_out[0, 0:HALO, :], resid_out[0, rows - HALO : rows, :])
            side_ref[HALO : HALO + HALF, :] = jnp.where(
                low, grad_out[0, 0:HALF, :], grad_out[0, rows - HALF : rows, :]
            )
        for copy in copies[2:]:
            copy.wait()
        for chip in range(chips):
            heads = [cols(head_of(member_of(chip, c))) for c in (0, 1)]
            for at, width, c_ref, low, high in (
                (0, 0, k_ref, 0, rows),
                (0, HEAD_DIM, v_ref, 0, rows),
                (rows, 0, q_ref, 0, half),
                (rows, HEAD_DIM, q_ref, half, rows),
            ):
                stay, leave = sides(core, [c_ref[0, low:high, c] for c in heads])
                keep_ref[chip, at : at + high - low, width : width + HEAD_DIM] = stay
                send_ref[chip, at : at + high - low, width : width + HEAD_DIM] = leave

    slot = rows + half
    raw = pl.BlockSpec(memory_space=pltpu.HBM)
    on_vmem = pl.BlockSpec(memory_space=pltpu.VMEM)
    pack_outs = [
        vmem((chips, slot, LANES)), vmem((chips, slot, LANES)),
        vmem((HALO + HALF, channels)), vmem((HALO + HALF, channels)),
        vmem((1, rows, channels)), vmem((1, rows, channels)), vmem(conv_kernel.shape),
    ]
    keep, send, first, second, resid, upstream, taps_in = pl.pallas_call(
        pack_body,
        out_shape=pack_outs,
        in_specs=[raw] * 6,
        out_specs=[on_vmem] * 7,
        scratch_shapes=[pltpu.VMEM((1, rows, width), BF16)] * 3 + [pltpu.SemaphoreType.DMA((6,))],
        compiler_params=pltpu.CompilerParams(vmem_limit_bytes=VMEM_LIMIT),
        name="pack",
    )(*in_hbm(query, key, value, resid_in, out_grad, conv_kernel))

    mesh_axes = ("head", "z", "y")

    def place(head, z, y):
        return head * ctx_count + z * group + y

    def everyone(target):
        return [
            (place(h, z, y), place(*target(h, z, y)))
            for h in range(heads_axis)
            for z in range(z_count)
            for y in range(group)
        ]

    def core_swap(x):
        return lax.ppermute(x, mesh_axes, everyone(lambda h, z, y: (h ^ 1, z, y)))

    def step(x, d, phase):
        def target(h, z, y):
            partner = z + d if (z // d) % 2 == phase else z - d
            return (h, partner, y) if 0 <= partner < z_count else (h ^ 1, z, y)

        return lax.ppermute(x, mesh_axes, everyone(target))

    def exchange(keep, got, count, index, name):
        def body(keep_ref, got_ref, *out_refs):
            me = index()
            for m, out_ref in enumerate(out_refs, 1):
                out_ref[0] = keep_ref[me ^ m]
                out_ref[1] = got_ref[me ^ m]

        per_row = heads_axis // 2

        def target(m):
            def f(h, z, y):
                chip = (y * per_row + h // 2) ^ m
                return (chip % per_row) * 2 + h % 2, z, chip // per_row

            return f

        parts = call(body, [vmem((2,) + keep.shape[1:])] * (count - 1), name=name)(*on_chip(keep, got))
        return [lax.ppermute(part, mesh_axes, everyone(target(m))) for m, part in enumerate(parts, 1)]

    def arrivals(me, core, keep_ref, got_ref, part_refs):
        out = [(member_of(me, core), lambda: keep_ref[me]), (member_of(me, 1 - core), lambda: got_ref[me])]
        for m, ref in enumerate(part_refs, 1):
            out.append((member_of(me ^ m, core), lambda ref=ref: ref[0]))
            out.append((member_of(me ^ m, 1 - core), lambda ref=ref: ref[1]))
        return out

    got = core_swap(send)

    last_head = heads_axis - 1

    def inside(h, z, y):
        return (h + 1 if h % 2 else h - 1) if 0 < h < last_head else last_head - h, z, y

    outer = {}
    idle = []
    for ctx in range(ctx_count):
        for h in range(heads_axis):
            if h == last_head and ctx < ctx_count - 1:
                outer[h, ctx] = (0, ctx + 1)
                outer[0, ctx + 1] = (h, ctx)
            elif 0 < h < last_head or (h, ctx) in ((0, 0), (last_head, ctx_count - 1)):
                idle.append((h, ctx))
    for one, two in zip(idle[::2], idle[1::2]):
        outer[one], outer[two] = two, one

    def outside(h, z, y):
        head, ctx = outer[h, z * group + y]
        return head, ctx // group, ctx % group

    halos = [
        core_swap(first),
        lax.ppermute(second, mesh_axes, everyone(inside)),
        lax.ppermute(second, mesh_axes, everyone(outside)),
    ]
    mine = [keep, got] + exchange(keep, got, chips, my_chip, "regroup")

    def keys_body(keep_ref, got_ref, *refs):
        out_ref = refs[-1]
        for member, take in arrivals(my_chip(), my_core(), keep_ref, got_ref, refs[:-1]):
            out_ref[pl.ds(pl.multiple_of(member * rows, rows), rows), :] = take()[0:rows]

    (both,) = call(keys_body, [vmem((supers, LANES))], name="keys")(*on_chip(*mine))

    steps = [(d, phase) for d in range(1, near + 1) for phase in (0, 1)]
    around = [step(both, d, phase) for d, phase in steps]

    span = rows + 2 * HALF

    def conv_body(
        resid_ref, grad_ref, core_ref, inside_ref, outside_ref, taps_ref, weight_hbm,
        hg_keep, hg_send, dres_keep, dres_send, low_ref, weight_ref, sem,
    ):
        fetch = pltpu.make_async_copy(weight_hbm, weight_ref, sem)
        fetch.start()
        head, ctx = lax.axis_index("head"), lax.axis_index("z") * group + lax.axis_index("y")
        odd = (head % 2) == 1
        edge = jnp.logical_or(head == 0, head == heads_axis - 1)
        starts = jnp.logical_and(head == 0, ctx == 0)
        ends = jnp.logical_and(head == heads_axis - 1, ctx == ctx_count - 1)

        def taps_sum(x, tap_of, length):
            total = None
            for b in range(8):
                part = None
                for a in range(4):
                    offset = 8 * a + b
                    if offset < 1 or offset > KERNEL:
                        continue
                    term = tap_of(offset - 1) * x[8 * a : 8 * a + length + 8]
                    part = term if part is None else part + term
                if b:
                    part = pltpu.roll(part, length + 8 - b, 0)
                part = part[0:length]
                total = part if total is None else total + part
            return total

        def chunk(c, carry):
            at = pl.multiple_of(c * LANES, LANES)
            lane = pl.ds(at, LANES)
            first = core_ref[:, lane].astype(F32)
            second = jnp.where(edge, outside_ref[:, lane].astype(F32), inside_ref[:, lane].astype(F32))
            before = jnp.where(starts, 0.0, jnp.where(odd, first, second))
            after = jnp.where(ends, 0.0, jnp.where(odd, second, first))
            taps = taps_ref[:, lane].astype(F32)
            x = jnp.concatenate([before[0:HALO], resid_ref[0, :, lane].astype(F32), after[0:HALO]], axis=0)
            middle = grad_ref[0, :, lane].astype(F32)
            g = jnp.concatenate([before[HALO:], middle, after[HALO:]], axis=0)
            pre = taps_sum(x, lambda k: taps[k : k + 1], span)
            s = 1.0 / (1.0 + jnp.exp(-pre))
            cg = g * (s * (1.0 + pre * (1.0 - s)))
            out = middle + taps_sum(cg, lambda k: taps[KERNEL - 1 - k : KERNEL - k], rows)
            low_ref[:, lane] = out.astype(BF16)
            return carry

        lax.fori_loop(0, channels // LANES, chunk, 0)
        core = my_core()
        for x in range(heads_axis // 2):
            dres_keep[x], dres_send[x] = sides(
                core, [low_ref[:, h * out_cols : (h + 1) * out_cols] for h in (2 * x, 2 * x + 1)]
            )
        fetch.wait()
        hg = dot(low_ref[...], weight_ref[...], NT_DIMS).astype(BF16)
        for chip in range(chips):
            heads = [cols(head_of(member_of(chip, c))) for c in (0, 1)]
            for at, part in ((0, slice(0, half)), (HEAD_DIM, slice(half, rows))):
                stay, leave = sides(core, [hg[part, c] for c in heads])
                hg_keep[chip, :, at : at + HEAD_DIM] = stay
                hg_send[chip, :, at : at + HEAD_DIM] = leave

    hg_keep, hg_send, dres_keep, dres_send = call(
        conv_body,
        [vmem((chips, half, LANES))] * 2 + [vmem((heads_axis // 2, rows, out_cols))] * 2,
        raw=(6,),
        scratch=[
            pltpu.VMEM((rows, channels), BF16),
            pltpu.VMEM(out_weight.shape, BF16),
            pltpu.SemaphoreType.DMA,
        ],
        name="conv",
        cost=CONV_COST,
    )(*on_chip(resid, upstream, *halos, taps_in), *in_hbm(out_weight))
    hg_got = core_swap(hg_send)
    grads = [hg_keep, hg_got] + exchange(hg_keep, hg_got, chips, my_chip, "regroup_grads")
    n_dres = 2 + heads_axis // 2 - 1
    dres_shape = arr((1, block, out_cols))

    def resid_out(refs, out_ref):
        for member, take in arrivals(lax.axis_index("head") // 2, my_core(), refs[0], refs[1], refs[2:]):
            out_ref[0, pl.ds(pl.multiple_of(member * rows, rows), rows), :] = take()

    q_tiles = supers // QT
    k_tiles = ext // QT
    first_tile = lead // QT
    own_tiles = range(near * q_tiles, (near + 1) * q_tiles)

    def seen(a):
        return range(a + first_tile, a + first_tile + tiles)

    def at_tile(t):
        return slice(t * QT, (t + 1) * QT)

    def score_body(*refs):
        len_ref, both_ref = refs[:2]
        mine_refs = refs[2 : 3 + chips]
        around_refs = refs[3 + chips : 3 + chips + 2 * near]
        e_ref, inv_ref, out_ref, kv, kt, qz, kb, qs, vt, s_sc = refs[3 + chips + 2 * near :]
        z = lax.axis_index("z")
        low = lax.broadcasted_iota(jnp.int32, (half, LANES), 1) < HEAD_DIM
        lane = lax.broadcasted_iota(jnp.int32, (half, LANES), 1)
        kv[near * supers : (near + 1) * supers, :] = both_ref[...]
        for member, take in arrivals(my_chip(), my_core(), mine_refs[0], mine_refs[1], mine_refs[2:]):
            q = take()[rows:slot].astype(F32) * scale
            for i, part in enumerate((q, pltpu.roll(q, HEAD_DIM, 1))):
                at = pl.ds(pl.multiple_of(member * rows + i * half, half), half)
                part = jnp.where(low, part, 0.0)
                qz[at, :] = part.astype(BF16)
                qs[at, :] = jnp.where(lane == HEAD_DIM, 1.0, part).astype(BF16)
        for d in range(1, near + 1):
            left, right = (near - d) * supers, (near + d) * supers
            odd = ((z // d) % 2) == 1

            @pl.when(odd)
            def _():
                kv[left : left + supers, :] = around_refs[2 * d - 2][...]
                kv[right : right + supers, :] = around_refs[2 * d - 1][...]

            @pl.when(jnp.logical_not(odd))
            def _():
                kv[left : left + supers, :] = around_refs[2 * d - 1][...]
                kv[right : right + supers, :] = around_refs[2 * d - 2][...]

        def limit(t):
            index = (z - near) * group + t // per_block
            inside = jnp.logical_and(index >= 0, index < ctx_count)
            length = len_ref[jnp.clip(index, 0, ctx_count - 1)]
            return jnp.where(inside, length, 0) - (t % per_block) * QT

        tile_lane = lax.broadcasted_iota(jnp.int32, (QT, LANES), 1)
        tile_row = lax.broadcasted_iota(jnp.int32, (QT, LANES), 0)

        for t in range(k_tiles):
            tile = kv[at_tile(t), :].astype(F32)
            turned = jnp.transpose(tile).astype(BF16)
            kt[:, at_tile(t)] = turned[0:HEAD_DIM]
            vt[0:HEAD_DIM, at_tile(t)] = turned[HEAD_DIM:LANES]
            dead = jnp.logical_and(tile_lane == HEAD_DIM, tile_row >= limit(t))
            kb[at_tile(t), :] = jnp.where(tile_lane < HEAD_DIM, tile, jnp.where(dead, NEG, 0.0)).astype(BF16)
        vt[HEAD_DIM:, :] = jnp.ones((ONES, ext), BF16)
        key_at = lax.broadcasted_iota(jnp.int32, (QT, QT), 0)
        query_at = lax.broadcasted_iota(jnp.int32, (QT, QT), 1)

        def scores(a, j, top):
            s = dot(kb[at_tile(a + j + first_tile), :], qs[at_tile(a), :], NT_DIMS)
            if j == 0:
                s = jnp.where(key_at >= query_at, s, NEG)
            if j == tiles - 1:
                s = jnp.where(key_at <= query_at, s, NEG)
            s_sc[a % 2, j] = s
            return jnp.maximum(top, jnp.max(s.reshape(QT // 8, 8, QT), axis=0))

        tops = [jnp.full((8, QT), NEG, F32) for _ in range(q_tiles)]
        for j in range(tiles):
            tops[0] = scores(0, j, tops[0])
        for a in range(q_tiles):
            top = jnp.max(tops[a], axis=0, keepdims=True)
            for j in range(tiles):
                if a + 1 < q_tiles:
                    tops[a + 1] = scores(a + 1, j, tops[a + 1])
                e = jnp.exp(s_sc[a % 2, j] - top)
                e_ref[a, at_tile(j), :] = e.astype(BF16)
            keys = slice((a + first_tile) * QT, (a + first_tile + tiles) * QT)
            out = dot(vt[:, keys], e_ref[a], NN_DIMS)
            inverse = 1.0 / out[HEAD_DIM : HEAD_DIM + 1]
            inv_ref[a] = inverse
            out_ref[a] = out[0:HEAD_DIM] * inverse

    exps, inverse, outs, kv, kt, qz = call(
        score_body,
        [
            vmem((q_tiles, tiles * QT, QT)),
            vmem((q_tiles, 1, QT), F32),
            vmem((q_tiles, HEAD_DIM, QT), F32),
            vmem((ext, LANES)),
            vmem((HEAD_DIM, ext)),
            vmem((supers, LANES)),
        ],
        smem=(0,),
        scratch=[
            pltpu.VMEM((ext, LANES), BF16),
            pltpu.VMEM((supers, LANES), BF16),
            pltpu.VMEM((HEAD_DIM + ONES, ext), BF16),
            pltpu.VMEM((2, tiles, QT, QT), F32),
        ],
        name="scores",
        cost=SCORES_COST,
    )(frame_lengths, *on_chip(both, *mine, *around))

    def key_tiles(a, ts, e_ref, inv_ref, delta_ref, kv, kt, qz, hz, acc, ds_sc, base):
        q, g = qz[at_tile(a), :], hz[at_tile(a), :]
        for i, t in enumerate(ts):
            p = e_ref[a, at_tile(t - a - first_tile), :].astype(F32) * inv_ref[a]
            slopes = dot(kv[at_tile(t), :], g, NT_DIMS)
            ds = (p * (slopes - delta_ref[a])).astype(BF16)
            ds_sc[at_tile(i), :] = ds
            part = dot(ds, q, NN_DIMS) + dot(p.astype(BF16), g, NN_DIMS)
            fresh = not any(t in seen(b) for b in range(a))
            acc[at_tile(t - base), :] = part if fresh else acc[at_tile(t - base), :] + part
        keys = slice(ts[0] * QT, (ts[-1] + 1) * QT)
        return dot(kt[:, keys], ds_sc[0 : len(ts) * QT, :], NN_DIMS)

    n_back = 2 * near

    def arrived(i, ref):
        d, phase = steps[i]
        z = lax.axis_index("z")
        partner = jnp.where((z // d) % 2 == phase, z + d, z - d)
        real = jnp.logical_and(partner >= 0, partner < z_count)
        return jnp.where(real, ref[...].astype(F32), 0.0)

    def far_body(*refs):
        grad_refs = refs[: 1 + chips]
        e_ref, inv_ref, out_ref, kv, kt, qz, hz, delta_ref, dq = refs[1 + chips : 10 + chips]
        back_refs = refs[10 + chips : -2]
        acc, ds_sc = refs[-2:]
        z = lax.axis_index("z")
        low = lax.broadcasted_iota(jnp.int32, (half, LANES), 1) < HEAD_DIM
        for member, take in arrivals(my_chip(), my_core(), grad_refs[0], grad_refs[1], grad_refs[2:]):
            g = take().astype(F32)
            for i, part in enumerate((pltpu.roll(g, HEAD_DIM, 1), g)):
                at = pl.ds(pl.multiple_of(member * rows + i * half, half), half)
                hz[at, :] = jnp.where(low, 0.0, part).astype(BF16)
        for a in range(q_tiles):
            g = jnp.transpose(hz[at_tile(a), :].astype(F32))[HEAD_DIM:LANES]
            delta_ref[a] = jnp.sum(g * out_ref[a], axis=0, keepdims=True)
        for t in range(k_tiles):
            if not any(t in seen(a) for a in range(q_tiles)):
                acc[at_tile(t), :] = jnp.zeros((QT, LANES), F32)
        for a in range(q_tiles):
            left = [t for t in seen(a) if t < own_tiles[0]]
            right = [t for t in seen(a) if t > own_tiles[-1]]
            dq[a] = sum(
                key_tiles(a, ts, e_ref, inv_ref, delta_ref, kv, kt, qz, hz, acc, ds_sc.at[side], 0)
                for side, ts in enumerate((left, right))
            )
        for i, (d, phase) in enumerate(steps):
            odd = ((z // d) % 2) == 1
            right = odd if phase else jnp.logical_not(odd)
            side = jnp.where(right, near + d, near - d) * supers
            back_refs[i][...] = acc[pl.ds(pl.multiple_of(side, supers), supers), :].astype(BF16)

    far = call(
        far_body,
        [vmem((supers, LANES)), vmem((q_tiles, 1, QT), F32), vmem((q_tiles, HEAD_DIM, QT), F32)]
        + [vmem((supers, LANES))] * n_back,
        scratch=[pltpu.VMEM((ext, LANES), F32), pltpu.VMEM((2, tiles * QT, QT), BF16)],
        name="far",
        cost=FAR_COST,
    )(*on_chip(*grads, exps, inverse, outs, kv, kt, qz))
    hz, delta, dq_far = far[:3]
    back = [step(far[3 + i], d, phase) for i, (d, phase) in enumerate(steps)]

    hb = block // 2

    def near_body(*refs):
        e_ref, inv_ref, delta_ref, kv, kt, qz, hz, far_ref = refs[:8]
        acc, dq_ref = refs[8:10]
        dq_sc, ds_sc = refs[-2:]
        for a in range(q_tiles):
            dq = far_ref[a] + key_tiles(
                a, own_tiles, e_ref, inv_ref, delta_ref, kv, kt, qz, hz, acc, ds_sc.at[a % 2], own_tiles[0]
            )
            dq_sc[at_tile(a), 0:HEAD_DIM] = jnp.transpose(dq * scale)
        if group == 1:
            dq_ref[0] = dq_sc[:, 0:HEAD_DIM].astype(BF16)
            return
        y = lax.axis_index("y")
        for ref, slot in ((dq_ref, y), (refs[10], 1 - y)):
            at = pl.multiple_of(slot * block, block)
            upper = dq_sc[pl.ds(at, hb), 0:HEAD_DIM]
            lower = dq_sc[pl.ds(pl.multiple_of(at + hb, hb), hb), 0:HEAD_DIM]
            ref[...] = jnp.concatenate([upper, lower], axis=1).astype(BF16)

    results = call(
        near_body,
        [vmem((supers, LANES), F32)]
        + ([arr((1, block, HEAD_DIM))] if group == 1 else [vmem((hb, LANES))] * 2),
        scratch=[
            pltpu.VMEM((supers, LANES), F32),
            pltpu.VMEM((2, supers, QT), BF16),
        ],
        name="near",
        cost=NEAR_COST,
    )(*on_chip(exps, inverse, delta, kv, kt, qz, hz, dq_far))
    own, dq = results[:2]
    dres_keep, dres_send, _ = lax.optimization_barrier((dres_keep, dres_send, results[0]))
    dres_got = core_swap(dres_send)
    dres = [dres_keep, dres_got] + exchange(
        dres_keep, dres_got, heads_axis // 2, lambda: lax.axis_index("head") // 2, "regroup_resid"
    )


    if group == 1:

        def last_body(*refs):
            total = refs[0][...]
            for i in range(n_back):
                total = total + arrived(i, refs[1 + i])
            total = total.astype(BF16)
            refs[-2][0] = total[:, 0:HEAD_DIM]
            refs[-1][0] = total[:, HEAD_DIM:LANES]
            resid_out(refs[1 + n_back : 1 + n_back + n_dres], refs[-3])

        d_resid, d_key, d_value = call(last_body, [dres_shape] + [arr((1, block, HEAD_DIM))] * 2, name="last")(
            *on_chip(own, *back, *dres)
        )
        return d_resid, dq, d_key, d_value

    def y_swap(x):
        return lax.ppermute(x, mesh_axes, everyone(lambda h, z, y: (h, z, 1 - y)))

    dq_other = y_swap(results[2])

    def sum_body(own_ref, *refs):
        keep_ref, send_ref = refs[-2:]
        total = own_ref[...]
        for i in range(n_back):
            total = total + arrived(i, refs[i])
        total = total.astype(BF16)
        first = lax.axis_index("y") == 0
        keep_ref[...] = jnp.where(first, total[0:block], total[block:supers])
        send_ref[...] = jnp.where(first, total[block:supers], total[0:block])

    keep, send = call(sum_body, [vmem((block, LANES))] * 2, name="sum")(*on_chip(own, *back))
    other = y_swap(send)

    def last_body(*refs):
        keep_ref, other_ref, dq_keep_ref, dq_other_ref = refs[:4]
        dq_ref, dk_ref, dv_ref = refs[-3:]
        resid_out(refs[4 : 4 + n_dres], refs[-4])
        first = lax.axis_index("y") == 0
        low = lax.broadcasted_iota(jnp.int32, (block, LANES), 1) < HEAD_DIM

        def ordered(mine_ref, peer_ref):
            mine, peer = mine_ref[...].astype(F32), peer_ref[...].astype(F32)
            return jnp.where(first, mine, peer), jnp.where(first, peer, mine)

        lo, up = ordered(keep_ref, other_ref)
        dk_ref[0] = jnp.where(low, lo, pltpu.roll(up, HEAD_DIM, 1)).astype(BF16)
        dv_ref[0] = jnp.where(low, pltpu.roll(lo, HEAD_DIM, 1), up).astype(BF16)
        lo, up = ordered(dq_keep_ref, dq_other_ref)
        low = low[0:hb]
        dq_ref[0, 0:hb, :] = jnp.where(low, lo, pltpu.roll(up, HEAD_DIM, 1)).astype(BF16)
        dq_ref[0, hb:block, :] = jnp.where(low, pltpu.roll(lo, HEAD_DIM, 1), up).astype(BF16)

    d_resid, d_query, d_key, d_value = call(
        last_body, [dres_shape] + [arr((1, block, LANES))] * 3, name="last"
    )(*on_chip(keep, other, dq, dq_other, *dres))
    return d_resid, d_query, d_key, d_value


def solution(mesh):
    heads_axis = mesh.shape["head"]
    ctx_count = mesh.shape["ctx"]

    def run(query, *rest):
        group = query.shape[2] // HEAD_DIM // heads_axis
        z_count = ctx_count // group
        fine = Mesh(mesh.devices.reshape(heads_axis, z_count, group), ("head", "z", "y"))
        rows_spec = P(("z", "y"), "head", None)
        cols_spec = P(("z", "y"), None, "head")
        sizes = (heads_axis, z_count, group)
        return jax.shard_map(
            lambda *args: on_device(sizes, *args),
            mesh=fine,
            in_specs=(rows_spec,) * 5 + (P(),) * 3,
            out_specs=(cols_spec,) * 4,
            check_vma=False,
        )(query, *rest)

    return run
```

```python
import jax
import jax.numpy as jnp
from jax import lax
from jax.experimental import pallas as pl
from jax.experimental.pallas import tpu as pltpu
from jax.sharding import Mesh
from jax.sharding import PartitionSpec as P

HEAD_DIM = 64
KERNEL = 31
REACH = 2
LANES = 128
QT = 256
HALO = 32
HALF = 16
NEG = -1e30
ONES = 16
F32 = jnp.float32
BF16 = jnp.bfloat16
NT_DIMS = (((1,), (1,)), ((), ()))
NN_DIMS = (((1,), (0,)), ((), ()))
VMEM_LIMIT = 12 * 1024 * 1024
CONV_COST = (3_000_000_000, 0, 0)
SCORES_COST = (9_000_000_000, 0, 0)
FAR_COST = (4_000_000_000, 0, 0)
NEAR_COST = (4_000_000_000, 0, 0)
RESID_COST = (1_000_000_000, 0, 0)


def dot(a, b, dims):
    return lax.dot_general(a, b, dims, preferred_element_type=F32)


def call(body, outs, smem=(), raw=(), scratch=(), name=None, cost=None):
    on_vmem = pl.BlockSpec(memory_space=pltpu.VMEM)
    spaces = {i: pltpu.SMEM for i in smem} | {i: pltpu.HBM for i in raw}

    def run(*args):
        return pl.pallas_call(
            body,
            out_shape=outs,
            in_specs=[pl.BlockSpec(memory_space=spaces.get(i, pltpu.VMEM)) for i in range(len(args))],
            out_specs=[on_vmem] * len(outs),
            scratch_shapes=list(scratch),
            compiler_params=pltpu.CompilerParams(vmem_limit_bytes=VMEM_LIMIT),
            cost_estimate=None if cost is None else pl.CostEstimate(*cost),
            name=name,
        )(*args)

    return run


def arr(shape, dtype=BF16):
    return jax.ShapeDtypeStruct(shape, dtype)


def vmem(shape, dtype=BF16):
    return pltpu.VMEM(shape, dtype)


def on_chip(*arrays):
    return [pltpu.with_memory_space_constraint(x, pltpu.VMEM) for x in arrays]


def in_hbm(*arrays):
    return [pltpu.with_memory_space_constraint(x, pltpu.HBM) for x in arrays]


def on_device(sizes, query, key, value, resid_in, out_grad, out_weight, conv_kernel, frame_lengths):
    heads_axis, z_count, group = sizes
    ctx_count = z_count * group
    rows = query.shape[1]
    width = query.shape[2]
    channels = resid_in.shape[2]
    block = rows * heads_axis
    supers = group * block
    members = group * heads_axis
    chips = members // 2
    half = rows // 2
    near = -(-REACH // group)
    window = REACH * block
    tiles = 2 * window // QT + 1
    per_block = block // QT
    lead = near * supers - window
    ext = (2 * near + 1) * supers
    out_cols = channels // heads_axis
    scale = HEAD_DIM ** (-0.5)

    def head_of(member):
        return group * (member % heads_axis) + member // heads_axis

    def cols(head):
        return slice(head * HEAD_DIM, (head + 1) * HEAD_DIM)

    def sides(core, slots):
        first, second = slots
        return jnp.where(core == 0, first, second), jnp.where(core == 0, second, first)

    def member_of(chip, core):
        return chip * 2 + core

    def my_chip():
        return lax.axis_index("y") * (heads_axis // 2) + lax.axis_index("head") // 2

    def my_core():
        return lax.axis_index("head") % 2

    slot = rows + half
    edge_rows = HALO + HALF

    def pack_body(q_hbm, k_hbm, v_hbm, resid_ref, grad_ref, taps_ref, *refs):
        keep_ref, send_ref, second_ref, resid_out, grad_out, taps_out, q_ref, k_ref, v_ref, sems = refs
        copies = [
            pltpu.make_async_copy(source, target, sems.at[i])
            for i, (source, target) in enumerate(
                (
                    (resid_ref, resid_out), (grad_ref, grad_out), (k_hbm, k_ref), (v_hbm, v_ref),
                    (q_hbm, q_ref), (taps_ref, taps_out),
                )
            )
        ]
        for copy in copies:
            copy.start()
        core = my_core()
        copies[0].wait()
        copies[1].wait()
        odd = core == 1
        resid_top, resid_low = resid_out[0, 0:HALO, :], resid_out[0, rows - HALO : rows, :]
        grad_top, grad_low = grad_out[0, 0:HALF, :], grad_out[0, rows - HALF : rows, :]
        second_ref[0:HALO, :] = jnp.where(odd, resid_low, resid_top)
        second_ref[HALO:edge_rows, :] = jnp.where(odd, grad_low, grad_top)
        resid_first = jnp.where(odd, resid_top, resid_low)
        grad_first = jnp.where(odd, grad_top, grad_low)
        for c in range(channels // LANES):
            at = chips * slot + c * edge_rows
            lane = slice(c * LANES, (c + 1) * LANES)
            send_ref[at : at + HALO, :] = resid_first[:, lane]
            send_ref[at + HALO : at + edge_rows, :] = grad_first[:, lane]
        for copy in copies[2:]:
            copy.wait()
        for chip in range(chips):
            heads = [cols(head_of(member_of(chip, c))) for c in (0, 1)]
            for at, width, c_ref, low, high in (
                (0, 0, k_ref, 0, rows),
                (0, HEAD_DIM, v_ref, 0, rows),
                (rows, 0, q_ref, 0, half),
                (rows, HEAD_DIM, q_ref, half, rows),
            ):
                stay, leave = sides(core, [c_ref[0, low:high, c] for c in heads])
                keep_ref[chip, at : at + high - low, width : width + HEAD_DIM] = stay
                at = at + chip * slot
                send_ref[at : at + high - low, width : width + HEAD_DIM] = leave

    raw = pl.BlockSpec(memory_space=pltpu.HBM)
    on_vmem = pl.BlockSpec(memory_space=pltpu.VMEM)
    pack_outs = [
        vmem((chips, slot, LANES)), vmem((chips * slot + edge_rows * channels // LANES, LANES)),
        vmem((edge_rows, channels)),
        vmem((1, rows, channels)), vmem((1, rows, channels)), vmem(conv_kernel.shape),
    ]
    keep, send, second, resid, upstream, taps_in = pl.pallas_call(
        pack_body,
        out_shape=pack_outs,
        in_specs=[raw] * 6,
        out_specs=[on_vmem] * 6,
        scratch_shapes=[pltpu.VMEM((1, rows, width), BF16)] * 3 + [pltpu.SemaphoreType.DMA((6,))],
        compiler_params=pltpu.CompilerParams(vmem_limit_bytes=VMEM_LIMIT),
        name="pack",
    )(*in_hbm(query, key, value, resid_in, out_grad, conv_kernel))

    mesh_axes = ("head", "z", "y")

    def place(head, z, y):
        return head * ctx_count + z * group + y

    def everyone(target):
        return [
            (place(h, z, y), place(*target(h, z, y)))
            for h in range(heads_axis)
            for z in range(z_count)
            for y in range(group)
        ]

    def core_swap(x):
        return lax.ppermute(x, mesh_axes, everyone(lambda h, z, y: (h ^ 1, z, y)))

    def step(x, d, phase):
        def target(h, z, y):
            partner = z + d if (z // d) % 2 == phase else z - d
            return (h, partner, y) if 0 <= partner < z_count else (h ^ 1, z, y)

        return lax.ppermute(x, mesh_axes, everyone(target))

    def slot_of(ref, i, like):
        size = like.shape[1]
        return ref[i] if len(ref.shape) == 3 else ref[pl.ds(pl.multiple_of(i * size, size), size), :]

    def exchange(keep, got, count, index, name):
        def body(keep_ref, got_ref, *out_refs):
            me = index()
            for m, out_ref in enumerate(out_refs, 1):
                out_ref[0] = keep_ref[me ^ m]
                out_ref[1] = slot_of(got_ref, me ^ m, keep_ref)

        per_row = heads_axis // 2

        def target(m):
            def f(h, z, y):
                chip = (y * per_row + h // 2) ^ m
                return (chip % per_row) * 2 + h % 2, z, chip // per_row

            return f

        parts = call(body, [vmem((2,) + keep.shape[1:])] * (count - 1), name=name)(*on_chip(keep, got))
        return [lax.ppermute(part, mesh_axes, everyone(target(m))) for m, part in enumerate(parts, 1)]

    def arrivals(me, core, keep_ref, got_ref, part_refs):
        out = [(member_of(me, core), lambda: keep_ref[me]), (member_of(me, 1 - core), lambda: slot_of(got_ref, me, keep_ref))]
        for m, ref in enumerate(part_refs, 1):
            out.append((member_of(me ^ m, core), lambda ref=ref: ref[0]))
            out.append((member_of(me ^ m, 1 - core), lambda ref=ref: ref[1]))
        return out

    got = core_swap(send)

    last_head = heads_axis - 1

    def inside(h, z, y):
        if 0 < h < last_head:
            return (h + 1 if h % 2 else h - 1), z, y
        return (h, z, 1 - y) if group == 2 else (last_head - h, z, y)

    outer = {}
    idle = []
    for ctx in range(ctx_count):
        for h in range(heads_axis):
            if h == last_head and ctx < ctx_count - 1:
                outer[h, ctx] = (0, ctx + 1)
                outer[0, ctx + 1] = (h, ctx)
            elif 0 < h < last_head or (h, ctx) in ((0, 0), (last_head, ctx_count - 1)):
                idle.append((h, ctx))
    for one, two in zip(idle[::2], idle[1::2]):
        outer[one], outer[two] = two, one

    def outside(h, z, y):
        head, ctx = outer[h, z * group + y]
        return head, ctx // group, ctx % group

    halos = [
        lax.ppermute(second, mesh_axes, everyone(inside)),
        lax.ppermute(second, mesh_axes, everyone(outside)),
    ]
    span = rows + 2 * HALF

    part_chunks = channels // LANES // 2
    part_cols = part_chunks * LANES

    def conv_chunks(start, resid_ref, grad_ref, core_ref, inside_ref, outside_ref, taps_ref, low_ref):
        head, ctx = lax.axis_index("head"), lax.axis_index("z") * group + lax.axis_index("y")
        odd = (head % 2) == 1
        edge = jnp.logical_or(head == 0, head == heads_axis - 1)
        starts = jnp.logical_and(head == 0, ctx == 0)
        ends = jnp.logical_and(head == heads_axis - 1, ctx == ctx_count - 1)

        def taps_sum(x, tap_of, length):
            total = None
            for b in range(8):
                part = None
                for a in range(4):
                    offset = 8 * a + b
                    if offset < 1 or offset > KERNEL:
                        continue
                    term = tap_of(offset - 1) * x[8 * a : 8 * a + length + 8]
                    part = term if part is None else part + term
                if b:
                    part = pltpu.roll(part, length + 8 - b, 0)
                part = part[0:length]
                total = part if total is None else total + part
            return total

        def chunk(c, carry):
            at = pl.multiple_of(c * LANES, LANES)
            lane = pl.ds(at, LANES)
            at = pl.multiple_of(chips * slot + c * edge_rows, HALF)
            first = core_ref[pl.ds(at, edge_rows), :].astype(F32)
            second = jnp.where(edge, outside_ref[:, lane].astype(F32), inside_ref[:, lane].astype(F32))
            before = jnp.where(starts, 0.0, jnp.where(odd, first, second))
            after = jnp.where(ends, 0.0, jnp.where(odd, second, first))
            taps = taps_ref[:, lane].astype(F32)
            x = jnp.concatenate([before[0:HALO], resid_ref[0, :, lane].astype(F32), after[0:HALO]], axis=0)
            middle = grad_ref[0, :, lane].astype(F32)
            g = jnp.concatenate([before[HALO:], middle, after[HALO:]], axis=0)
            pre = taps_sum(x, lambda k: taps[k : k + 1], span)
            s = 1.0 / (1.0 + jnp.exp(-pre))
            cg = g * (s * (1.0 + pre * (1.0 - s)))
            out = middle + taps_sum(cg, lambda k: taps[KERNEL - 1 - k : KERNEL - k], rows)
            low_ref[:, lane] = out.astype(BF16)
            return carry

        lax.fori_loop(start, start + part_chunks, chunk, 0)

    def conv_first(*refs):
        conv_chunks(0, *refs)

    def conv_second(*refs):
        first_ref, weight_hbm, hg_keep, hg_send, dres_keep, dres_send, low_ref, weight_ref, sem = refs[6:]
        fetch = pltpu.make_async_copy(weight_hbm, weight_ref, sem)
        fetch.start()
        low_ref[:, 0:part_cols] = first_ref[...]
        conv_chunks(part_chunks, *refs[:6], low_ref)
        core = my_core()
        for x in range(heads_axis // 2):
            dres_keep[x], dres_send[x] = sides(
                core, [low_ref[:, h * out_cols : (h + 1) * out_cols] for h in (2 * x, 2 * x + 1)]
            )
        fetch.wait()
        hg = dot(low_ref[...], weight_ref[...], NT_DIMS).astype(BF16)
        for chip in range(chips):
            heads = [cols(head_of(member_of(chip, c))) for c in (0, 1)]
            for at, part in ((0, slice(0, half)), (HEAD_DIM, slice(half, rows))):
                stay, leave = sides(core, [hg[part, c] for c in heads])
                hg_keep[chip, :, at : at + HEAD_DIM] = stay
                hg_send[chip, :, at : at + HEAD_DIM] = leave

    conv_in = (resid, upstream, got, *halos, taps_in)
    (conv_low,) = call(conv_first, [vmem((rows, part_cols))], name="conv", cost=CONV_COST)(*on_chip(*conv_in))
    mine = [keep, got] + exchange(keep, got, chips, my_chip, "regroup")

    def keys_body(keep_ref, got_ref, *refs):
        out_ref = refs[-1]
        for member, take in arrivals(my_chip(), my_core(), keep_ref, got_ref, refs[:-1]):
            out_ref[pl.ds(pl.multiple_of(member * rows, rows), rows), :] = take()[0:rows]

    *mine_here, _ = lax.optimization_barrier((*mine, conv_low))
    (both,) = call(keys_body, [vmem((supers, LANES))], name="keys")(*on_chip(*mine_here))

    steps = [(d, phase) for d in range(1, near + 1) for phase in (0, 1)]
    around = [step(both, d, phase) for d, phase in steps]

    conv_low, both_here = lax.optimization_barrier((conv_low, both))
    hg_keep, hg_send, dres_keep, dres_send = call(
        conv_second,
        [vmem((chips, half, LANES))] * 2 + [vmem((heads_axis // 2, rows, out_cols))] * 2,
        raw=(7,),
        scratch=[
            pltpu.VMEM((rows, channels), BF16),
            pltpu.VMEM(out_weight.shape, BF16),
            pltpu.SemaphoreType.DMA,
        ],
        name="conv_last",
        cost=CONV_COST,
    )(*on_chip(*conv_in, conv_low), *in_hbm(out_weight))
    hg_got = core_swap(hg_send)
    grads = [hg_keep, hg_got] + exchange(hg_keep, hg_got, chips, my_chip, "regroup_grads")
    q_tiles = supers // QT
    k_tiles = ext // QT
    first_tile = lead // QT
    own_tiles = range(near * q_tiles, (near + 1) * q_tiles)

    def seen(a):
        return range(a + first_tile, a + first_tile + tiles)

    def at_tile(t):
        return slice(t * QT, (t + 1) * QT)

    def score_body(*refs):
        len_ref, both_ref = refs[:2]
        mine_refs = refs[2 : 3 + chips]
        around_refs = refs[3 + chips : 3 + chips + 2 * near]
        e_ref, inv_ref, out_ref, kv, kt, qz, kb, qs, vt, s_sc = refs[3 + chips + 2 * near :]
        z = lax.axis_index("z")
        low = lax.broadcasted_iota(jnp.int32, (half, LANES), 1) < HEAD_DIM
        lane = lax.broadcasted_iota(jnp.int32, (half, LANES), 1)
        kv[near * supers : (near + 1) * supers, :] = both_ref[...]
        for member, take in arrivals(my_chip(), my_core(), mine_refs[0], mine_refs[1], mine_refs[2:]):
            q = take()[rows:slot].astype(F32) * scale
            for i, part in enumerate((q, pltpu.roll(q, HEAD_DIM, 1))):
                at = pl.ds(pl.multiple_of(member * rows + i * half, half), half)
                part = jnp.where(low, part, 0.0)
                qz[at, :] = part.astype(BF16)
                qs[at, :] = jnp.where(lane == HEAD_DIM, 1.0, part).astype(BF16)
        for d in range(1, near + 1):
            left, right = (near - d) * supers, (near + d) * supers
            odd = ((z // d) % 2) == 1

            @pl.when(odd)
            def _():
                kv[left : left + supers, :] = around_refs[2 * d - 2][...]
                kv[right : right + supers, :] = around_refs[2 * d - 1][...]

            @pl.when(jnp.logical_not(odd))
            def _():
                kv[left : left + supers, :] = around_refs[2 * d - 1][...]
                kv[right : right + supers, :] = around_refs[2 * d - 2][...]

        def limit(t):
            index = (z - near) * group + t // per_block
            inside = jnp.logical_and(index >= 0, index < ctx_count)
            length = len_ref[jnp.clip(index, 0, ctx_count - 1)]
            return jnp.where(inside, length, 0) - (t % per_block) * QT

        tile_lane = lax.broadcasted_iota(jnp.int32, (QT, LANES), 1)
        tile_row = lax.broadcasted_iota(jnp.int32, (QT, LANES), 0)

        for t in range(k_tiles):
            tile = kv[at_tile(t), :].astype(F32)
            turned = jnp.transpose(tile).astype(BF16)
            kt[:, at_tile(t)] = turned[0:HEAD_DIM]
            vt[0:HEAD_DIM, at_tile(t)] = turned[HEAD_DIM:LANES]
            dead = jnp.logical_and(tile_lane == HEAD_DIM, tile_row >= limit(t))
            kb[at_tile(t), :] = jnp.where(tile_lane < HEAD_DIM, tile, jnp.where(dead, NEG, 0.0)).astype(BF16)
        vt[HEAD_DIM:, :] = jnp.ones((ONES, ext), BF16)
        key_at = lax.broadcasted_iota(jnp.int32, (QT, QT), 0)
        query_at = lax.broadcasted_iota(jnp.int32, (QT, QT), 1)

        def scores(a, j, top):
            s = dot(kb[at_tile(a + j + first_tile), :], qs[at_tile(a), :], NT_DIMS)
            if j == 0:
                s = jnp.where(key_at >= query_at, s, NEG)
            if j == tiles - 1:
                s = jnp.where(key_at <= query_at, s, NEG)
            s_sc[a % 2, j] = s
            return jnp.maximum(top, jnp.max(s.reshape(QT // 8, 8, QT), axis=0))

        tops = [jnp.full((8, QT), NEG, F32) for _ in range(q_tiles)]
        for j in range(tiles):
            tops[0] = scores(0, j, tops[0])
        for a in range(q_tiles):
            top = jnp.max(tops[a], axis=0, keepdims=True)
            for j in range(tiles):
                if a + 1 < q_tiles:
                    tops[a + 1] = scores(a + 1, j, tops[a + 1])
                e = jnp.exp(s_sc[a % 2, j] - top)
                e_ref[a, at_tile(j), :] = e.astype(BF16)
            keys = slice((a + first_tile) * QT, (a + first_tile + tiles) * QT)
            out = dot(vt[:, keys], e_ref[a], NN_DIMS)
            inverse = 1.0 / out[HEAD_DIM : HEAD_DIM + 1]
            inv_ref[a] = inverse
            out_ref[a] = out[0:HEAD_DIM] * inverse

    exps, inverse, outs, kv, kt, qz = call(
        score_body,
        [
            vmem((q_tiles, tiles * QT, QT)),
            vmem((q_tiles, 1, QT), F32),
            vmem((q_tiles, HEAD_DIM, QT), F32),
            vmem((ext, LANES)),
            vmem((HEAD_DIM, ext)),
            vmem((supers, LANES)),
        ],
        smem=(0,),
        scratch=[
            pltpu.VMEM((ext, LANES), BF16),
            pltpu.VMEM((supers, LANES), BF16),
            pltpu.VMEM((HEAD_DIM + ONES, ext), BF16),
            pltpu.VMEM((2, tiles, QT, QT), F32),
        ],
        name="scores",
        cost=SCORES_COST,
    )(frame_lengths, *on_chip(both, *mine, *around))

    def key_tiles(a, ts, e_ref, inv_ref, delta_ref, kv, kt, qz, hz, acc, ds_sc, base):
        q, g = qz[at_tile(a), :], hz[at_tile(a), :]
        for i, t in enumerate(ts):
            p = e_ref[a, at_tile(t - a - first_tile), :].astype(F32) * inv_ref[a]
            slopes = dot(kv[at_tile(t), :], g, NT_DIMS)
            ds = (p * (slopes - delta_ref[a])).astype(BF16)
            ds_sc[at_tile(i), :] = ds
            part = dot(ds, q, NN_DIMS) + dot(p.astype(BF16), g, NN_DIMS)
            fresh = not any(t in seen(b) for b in range(a))
            acc[at_tile(t - base), :] = part if fresh else acc[at_tile(t - base), :] + part
        keys = slice(ts[0] * QT, (ts[-1] + 1) * QT)
        return dot(kt[:, keys], ds_sc[0 : len(ts) * QT, :], NN_DIMS)

    n_back = 2 * near

    def arrived(i, ref):
        d, phase = steps[i]
        z = lax.axis_index("z")
        partner = jnp.where((z // d) % 2 == phase, z + d, z - d)
        real = jnp.logical_and(partner >= 0, partner < z_count)
        return jnp.where(real, ref[...].astype(F32), 0.0)

    def far_body(*refs):
        grad_refs = refs[: 1 + chips]
        e_ref, inv_ref, out_ref, kv, kt, qz, hz, delta_ref, dq = refs[1 + chips : 10 + chips]
        back_refs = refs[10 + chips : -2]
        acc, ds_sc = refs[-2:]
        z = lax.axis_index("z")
        low = lax.broadcasted_iota(jnp.int32, (half, LANES), 1) < HEAD_DIM
        for member, take in arrivals(my_chip(), my_core(), grad_refs[0], grad_refs[1], grad_refs[2:]):
            g = take().astype(F32)
            for i, part in enumerate((pltpu.roll(g, HEAD_DIM, 1), g)):
                at = pl.ds(pl.multiple_of(member * rows + i * half, half), half)
                hz[at, :] = jnp.where(low, 0.0, part).astype(BF16)
        for a in range(q_tiles):
            g = jnp.transpose(hz[at_tile(a), :].astype(F32))[HEAD_DIM:LANES]
            delta_ref[a] = jnp.sum(g * out_ref[a], axis=0, keepdims=True)
        for t in range(k_tiles):
            if not any(t in seen(a) for a in range(q_tiles)):
                acc[at_tile(t), :] = jnp.zeros((QT, LANES), F32)
        for a in range(q_tiles):
            left = [t for t in seen(a) if t < own_tiles[0]]
            right = [t for t in seen(a) if t > own_tiles[-1]]
            dq[a] = sum(
                key_tiles(a, ts, e_ref, inv_ref, delta_ref, kv, kt, qz, hz, acc, ds_sc.at[side], 0)
                for side, ts in enumerate((left, right))
            )
        for i, (d, phase) in enumerate(steps):
            odd = ((z // d) % 2) == 1
            right = odd if phase else jnp.logical_not(odd)
            side = jnp.where(right, near + d, near - d) * supers
            back_refs[i][...] = acc[pl.ds(pl.multiple_of(side, supers), supers), :].astype(BF16)

    far = call(
        far_body,
        [vmem((supers, LANES)), vmem((q_tiles, 1, QT), F32), vmem((q_tiles, HEAD_DIM, QT), F32)]
        + [vmem((supers, LANES))] * n_back,
        scratch=[pltpu.VMEM((ext, LANES), F32), pltpu.VMEM((2, tiles * QT, QT), BF16)],
        name="far",
        cost=FAR_COST,
    )(*on_chip(*grads, exps, inverse, outs, kv, kt, qz))
    hz, delta, dq_far = far[:3]
    back = [step(far[3 + i], d, phase) for i, (d, phase) in enumerate(steps)]

    hb = block // 2

    def near_body(*refs):
        e_ref, inv_ref, delta_ref, kv, kt, qz, hz, far_ref = refs[:8]
        acc, dq_ref = refs[8:10]
        dq_sc, ds_sc = refs[-2:]
        for a in range(q_tiles):
            dq = far_ref[a] + key_tiles(
                a, own_tiles, e_ref, inv_ref, delta_ref, kv, kt, qz, hz, acc, ds_sc.at[a % 2], own_tiles[0]
            )
            dq_sc[at_tile(a), 0:HEAD_DIM] = jnp.transpose(dq * scale)
        if group == 1:
            dq_ref[0] = dq_sc[:, 0:HEAD_DIM].astype(BF16)
            return
        y = lax.axis_index("y")
        for ref, slot in ((dq_ref, y), (refs[10], 1 - y)):
            at = pl.multiple_of(slot * block, block)
            upper = dq_sc[pl.ds(at, hb), 0:HEAD_DIM]
            lower = dq_sc[pl.ds(pl.multiple_of(at + hb, hb), hb), 0:HEAD_DIM]
            ref[...] = jnp.concatenate([upper, lower], axis=1).astype(BF16)

    results = call(
        near_body,
        [vmem((supers, LANES), F32)]
        + ([arr((1, block, HEAD_DIM))] if group == 1 else [vmem((hb, LANES))] * 2),
        scratch=[
            pltpu.VMEM((supers, LANES), F32),
            pltpu.VMEM((2, supers, QT), BF16),
        ],
        name="near",
        cost=NEAR_COST,
    )(*on_chip(exps, inverse, delta, kv, kt, qz, hz, dq_far))
    own, dq = results[:2]
    dres_keep, dres_send, _ = lax.optimization_barrier((dres_keep, dres_send, results[0]))
    dres_got = core_swap(dres_send)
    dres = [dres_keep, dres_got] + exchange(
        dres_keep, dres_got, heads_axis // 2, lambda: lax.axis_index("head") // 2, "regroup_resid"
    )

    def resid_body(*refs):
        for member, take in arrivals(lax.axis_index("head") // 2, my_core(), refs[0], refs[1], refs[2:-1]):
            refs[-1][0, pl.ds(pl.multiple_of(member * rows, rows), rows), :] = take()

    (d_resid,) = call(resid_body, [arr((1, block, out_cols))], name="resid", cost=RESID_COST)(*on_chip(*dres))

    if group == 1:

        def last_body(*refs):
            total = refs[0][...]
            for i in range(n_back):
                total = total + arrived(i, refs[1 + i])
            total = total.astype(BF16)
            refs[-2][0] = total[:, 0:HEAD_DIM]
            refs[-1][0] = total[:, HEAD_DIM:LANES]

        d_key, d_value = call(last_body, [arr((1, block, HEAD_DIM))] * 2, name="last")(*on_chip(own, *back))
        return d_resid, dq, d_key, d_value

    def y_swap(x):
        return lax.ppermute(x, mesh_axes, everyone(lambda h, z, y: (h, z, 1 - y)))

    def sum_body(own_ref, dq_send_ref, *refs):
        keep_ref, send_ref = refs[-2:]
        total = own_ref[...]
        for i in range(n_back):
            total = total + arrived(i, refs[i])
        total = total.astype(BF16)
        first = lax.axis_index("y") == 0
        keep_ref[...] = jnp.where(first, total[0:block], total[block:supers])
        send_ref[0:block, :] = jnp.where(first, total[block:supers], total[0:block])
        send_ref[block:, :] = dq_send_ref[...]

    keep, send = call(sum_body, [vmem((block, LANES)), vmem((block + hb, LANES))], name="sum")(
        *on_chip(own, results[2], *back)
    )
    other = y_swap(send)

    def last_body(*refs):
        keep_ref, other_ref, dq_keep_ref = refs[:3]
        dq_ref, dk_ref, dv_ref = refs[-3:]
        first = lax.axis_index("y") == 0
        low = lax.broadcasted_iota(jnp.int32, (block, LANES), 1) < HEAD_DIM

        def ordered(mine, peer):
            mine, peer = mine.astype(F32), peer.astype(F32)
            return jnp.where(first, mine, peer), jnp.where(first, peer, mine)

        lo, up = ordered(keep_ref[...], other_ref[0:block, :])
        dk_ref[0] = jnp.where(low, lo, pltpu.roll(up, HEAD_DIM, 1)).astype(BF16)
        dv_ref[0] = jnp.where(low, pltpu.roll(lo, HEAD_DIM, 1), up).astype(BF16)
        lo, up = ordered(dq_keep_ref[...], other_ref[block:, :])
        low = low[0:hb]
        dq_ref[0, 0:hb, :] = jnp.where(low, lo, pltpu.roll(up, HEAD_DIM, 1)).astype(BF16)
        dq_ref[0, hb:block, :] = jnp.where(low, pltpu.roll(lo, HEAD_DIM, 1), up).astype(BF16)

    d_query, d_key, d_value = call(last_body, [arr((1, block, LANES))] * 3, name="last")(
        *on_chip(keep, other, dq)
    )
    return d_resid, d_query, d_key, d_value


def solution(mesh):
    heads_axis = mesh.shape["head"]
    ctx_count = mesh.shape["ctx"]

    def run(query, *rest):
        group = query.shape[2] // HEAD_DIM // heads_axis
        z_count = ctx_count // group
        fine = Mesh(mesh.devices.reshape(heads_axis, z_count, group), ("head", "z", "y"))
        rows_spec = P(("z", "y"), "head", None)
        cols_spec = P(("z", "y"), None, "head")
        sizes = (heads_axis, z_count, group)
        return jax.shard_map(
            lambda *args: on_device(sizes, *args),
            mesh=fine,
            in_specs=(rows_spec,) * 5 + (P(),) * 3,
            out_specs=(cols_spec,) * 4,
            check_vma=False,
        )(query, *rest)

    return run
```

```python
import jax
import jax.numpy as jnp
from jax import lax
from jax.experimental import pallas as pl
from jax.experimental.pallas import tpu as pltpu
from jax.sharding import Mesh
from jax.sharding import PartitionSpec as P

HEAD_DIM = 64
KERNEL = 31
REACH = 2
LANES = 128
QT = 256
HALO = 32
HALF = 16
NEG = -1e30
ONES = 16
F32 = jnp.float32
BF16 = jnp.bfloat16
NT_DIMS = (((1,), (1,)), ((), ()))
NN_DIMS = (((1,), (0,)), ((), ()))
VMEM_LIMIT = 12 * 1024 * 1024
CONV_COST = (3_000_000_000, 0, 0)
SCORES_COST = (9_000_000_000, 0, 0)
FAR_COST = (4_000_000_000, 0, 0)
NEAR_COST = (4_000_000_000, 0, 0)
RESID_COST = (1_000_000_000, 0, 0)


def dot(a, b, dims):
    return lax.dot_general(a, b, dims, preferred_element_type=F32)


def call(body, outs, smem=(), raw=(), scratch=(), name=None, cost=None):
    on_vmem = pl.BlockSpec(memory_space=pltpu.VMEM)
    spaces = {i: pltpu.SMEM for i in smem} | {i: pltpu.HBM for i in raw}

    def run(*args):
        return pl.pallas_call(
            body,
            out_shape=outs,
            in_specs=[pl.BlockSpec(memory_space=spaces.get(i, pltpu.VMEM)) for i in range(len(args))],
            out_specs=[on_vmem] * len(outs),
            scratch_shapes=list(scratch),
            compiler_params=pltpu.CompilerParams(vmem_limit_bytes=VMEM_LIMIT),
            cost_estimate=None if cost is None else pl.CostEstimate(*cost),
            name=name,
        )(*args)

    return run


def arr(shape, dtype=BF16):
    return jax.ShapeDtypeStruct(shape, dtype)


def vmem(shape, dtype=BF16):
    return pltpu.VMEM(shape, dtype)


def on_chip(*arrays):
    return [pltpu.with_memory_space_constraint(x, pltpu.VMEM) for x in arrays]


def in_hbm(*arrays):
    return [pltpu.with_memory_space_constraint(x, pltpu.HBM) for x in arrays]


def on_device(sizes, query, key, value, resid_in, out_grad, out_weight, conv_kernel, frame_lengths):
    heads_axis, z_count, group = sizes
    ctx_count = z_count * group
    rows = query.shape[1]
    width = query.shape[2]
    channels = resid_in.shape[2]
    block = rows * heads_axis
    supers = group * block
    members = group * heads_axis
    chips = members // 2
    half = rows // 2
    near = -(-REACH // group)
    window = REACH * block
    tiles = 2 * window // QT + 1
    per_block = block // QT
    lead = near * supers - window
    ext = (2 * near + 1) * supers
    out_cols = channels // heads_axis
    scale = HEAD_DIM ** (-0.5)

    def head_of(member):
        return group * (member % heads_axis) + member // heads_axis

    def cols(head):
        return slice(head * HEAD_DIM, (head + 1) * HEAD_DIM)

    def sides(core, slots):
        first, second = slots
        return jnp.where(core == 0, first, second), jnp.where(core == 0, second, first)

    def member_of(chip, core):
        return chip * 2 + core

    def my_chip():
        return lax.axis_index("y") * (heads_axis // 2) + lax.axis_index("head") // 2

    def my_core():
        return lax.axis_index("head") % 2

    slot = rows + half
    edge_rows = HALO + HALF

    def pack_body(q_hbm, k_hbm, v_hbm, resid_ref, grad_ref, taps_ref, *refs):
        keep_ref, send_ref, second_ref, resid_out, grad_out, taps_out, q_ref, k_ref, v_ref, sems = refs
        copies = [
            pltpu.make_async_copy(source, target, sems.at[i])
            for i, (source, target) in enumerate(
                (
                    (resid_ref, resid_out), (grad_ref, grad_out), (k_hbm, k_ref), (v_hbm, v_ref),
                    (q_hbm, q_ref), (taps_ref, taps_out),
                )
            )
        ]
        for copy in copies:
            copy.start()
        core = my_core()
        copies[0].wait()
        copies[1].wait()
        odd = core == 1
        resid_top, resid_low = resid_out[0, 0:HALO, :], resid_out[0, rows - HALO : rows, :]
        grad_top, grad_low = grad_out[0, 0:HALF, :], grad_out[0, rows - HALF : rows, :]
        second_ref[0:HALO, :] = jnp.where(odd, resid_low, resid_top)
        second_ref[HALO:edge_rows, :] = jnp.where(odd, grad_low, grad_top)
        resid_first = jnp.where(odd, resid_top, resid_low)
        grad_first = jnp.where(odd, grad_top, grad_low)
        for c in range(channels // LANES):
            at = chips * slot + c * edge_rows
            lane = slice(c * LANES, (c + 1) * LANES)
            send_ref[at : at + HALO, :] = resid_first[:, lane]
            send_ref[at + HALO : at + edge_rows, :] = grad_first[:, lane]
        for copy in copies[2:]:
            copy.wait()
        for chip in range(chips):
            heads = [cols(head_of(member_of(chip, c))) for c in (0, 1)]
            for at, width, c_ref, low, high in (
                (0, 0, k_ref, 0, rows),
                (0, HEAD_DIM, v_ref, 0, rows),
                (rows, 0, q_ref, 0, half),
                (rows, HEAD_DIM, q_ref, half, rows),
            ):
                stay, leave = sides(core, [c_ref[0, low:high, c] for c in heads])
                keep_ref[chip, at : at + high - low, width : width + HEAD_DIM] = stay
                at = at + chip * slot
                send_ref[at : at + high - low, width : width + HEAD_DIM] = leave

    raw = pl.BlockSpec(memory_space=pltpu.HBM)
    on_vmem = pl.BlockSpec(memory_space=pltpu.VMEM)
    pack_outs = [
        vmem((chips, slot, LANES)), vmem((chips * slot + edge_rows * channels // LANES, LANES)),
        vmem((edge_rows, channels)),
        vmem((1, rows, channels)), vmem((1, rows, channels)), vmem(conv_kernel.shape),
    ]
    keep, send, second, resid, upstream, taps_in = pl.pallas_call(
        pack_body,
        out_shape=pack_outs,
        in_specs=[raw] * 6,
        out_specs=[on_vmem] * 6,
        scratch_shapes=[pltpu.VMEM((1, rows, width), BF16)] * 3 + [pltpu.SemaphoreType.DMA((6,))],
        compiler_params=pltpu.CompilerParams(vmem_limit_bytes=VMEM_LIMIT),
        name="pack",
    )(*in_hbm(query, key, value, resid_in, out_grad, conv_kernel))

    mesh_axes = ("head", "z", "y")

    def place(head, z, y):
        return head * ctx_count + z * group + y

    def everyone(target):
        return [
            (place(h, z, y), place(*target(h, z, y)))
            for h in range(heads_axis)
            for z in range(z_count)
            for y in range(group)
        ]

    def core_swap(x):
        return lax.ppermute(x, mesh_axes, everyone(lambda h, z, y: (h ^ 1, z, y)))

    def step(x, d, phase):
        def target(h, z, y):
            partner = z + d if (z // d) % 2 == phase else z - d
            return (h, partner, y) if 0 <= partner < z_count else (h ^ 1, z, y)

        return lax.ppermute(x, mesh_axes, everyone(target))

    def slot_of(ref, i, like):
        size = like.shape[1]
        return ref[i] if len(ref.shape) == 3 else ref[pl.ds(pl.multiple_of(i * size, size), size), :]

    def exchange(keep, got, count, index, name):
        def body(keep_ref, got_ref, *out_refs):
            me = index()
            for m, out_ref in enumerate(out_refs, 1):
                out_ref[0] = keep_ref[me ^ m]
                out_ref[1] = slot_of(got_ref, me ^ m, keep_ref)

        per_row = heads_axis // 2

        def target(m):
            def f(h, z, y):
                chip = (y * per_row + h // 2) ^ m
                return (chip % per_row) * 2 + h % 2, z, chip // per_row

            return f

        parts = call(body, [vmem((2,) + keep.shape[1:])] * (count - 1), name=name)(*on_chip(keep, got))
        return [lax.ppermute(part, mesh_axes, everyone(target(m))) for m, part in enumerate(parts, 1)]

    def arrivals(me, core, keep_ref, got_ref, part_refs):
        out = [(member_of(me, core), lambda: keep_ref[me]), (member_of(me, 1 - core), lambda: slot_of(got_ref, me, keep_ref))]
        for m, ref in enumerate(part_refs, 1):
            out.append((member_of(me ^ m, core), lambda ref=ref: ref[0]))
            out.append((member_of(me ^ m, 1 - core), lambda ref=ref: ref[1]))
        return out

    got = core_swap(send)

    last_head = heads_axis - 1

    def inside(h, z, y):
        if 0 < h < last_head:
            return (h + 1 if h % 2 else h - 1), z, y
        return (h, z, 1 - y) if group == 2 else (last_head - h, z, y)

    outer = {}
    idle = []
    for ctx in range(ctx_count):
        for h in range(heads_axis):
            if h == last_head and ctx < ctx_count - 1:
                outer[h, ctx] = (0, ctx + 1)
                outer[0, ctx + 1] = (h, ctx)
            elif 0 < h < last_head or (h, ctx) in ((0, 0), (last_head, ctx_count - 1)):
                idle.append((h, ctx))
    for one, two in zip(idle[::2], idle[1::2]):
        outer[one], outer[two] = two, one

    def outside(h, z, y):
        head, ctx = outer[h, z * group + y]
        return head, ctx // group, ctx % group

    halos = [
        lax.ppermute(second, mesh_axes, everyone(inside)),
        lax.ppermute(second, mesh_axes, everyone(outside)),
    ]
    span = rows + 2 * HALF

    part_chunks = channels // LANES * 6 // 8
    part_cols = part_chunks * LANES

    def conv_chunks(start, stop, resid_ref, grad_ref, core_ref, inside_ref, outside_ref, taps_ref, low_ref):
        head, ctx = lax.axis_index("head"), lax.axis_index("z") * group + lax.axis_index("y")
        odd = (head % 2) == 1
        edge = jnp.logical_or(head == 0, head == heads_axis - 1)
        starts = jnp.logical_and(head == 0, ctx == 0)
        ends = jnp.logical_and(head == heads_axis - 1, ctx == ctx_count - 1)

        def taps_sum(x, tap_of, length):
            total = None
            for b in range(8):
                part = None
                for a in range(4):
                    offset = 8 * a + b
                    if offset < 1 or offset > KERNEL:
                        continue
                    term = tap_of(offset - 1) * x[8 * a : 8 * a + length + 8]
                    part = term if part is None else part + term
                if b:
                    part = pltpu.roll(part, length + 8 - b, 0)
                part = part[0:length]
                total = part if total is None else total + part
            return total

        def chunk(c, carry):
            at = pl.multiple_of(c * LANES, LANES)
            lane = pl.ds(at, LANES)
            at = pl.multiple_of(chips * slot + c * edge_rows, HALF)
            first = core_ref[pl.ds(at, edge_rows), :].astype(F32)
            second = jnp.where(edge, outside_ref[:, lane].astype(F32), inside_ref[:, lane].astype(F32))
            before = jnp.where(starts, 0.0, jnp.where(odd, first, second))
            after = jnp.where(ends, 0.0, jnp.where(odd, second, first))
            taps = taps_ref[:, lane].astype(F32)
            x = jnp.concatenate([before[0:HALO], resid_ref[0, :, lane].astype(F32), after[0:HALO]], axis=0)
            middle = grad_ref[0, :, lane].astype(F32)
            g = jnp.concatenate([before[HALO:], middle, after[HALO:]], axis=0)
            pre = taps_sum(x, lambda k: taps[k : k + 1], span)
            s = 1.0 / (1.0 + jnp.exp(-pre))
            cg = g * (s * (1.0 + pre * (1.0 - s)))
            out = middle + taps_sum(cg, lambda k: taps[KERNEL - 1 - k : KERNEL - k], rows)
            low_ref[:, lane] = out.astype(BF16)
            return carry

        lax.fori_loop(start, stop, chunk, 0)

    def conv_first(*refs):
        conv_chunks(0, part_chunks, *refs)

    def conv_second(*refs):
        first_ref, weight_hbm, hg_keep, hg_send, dres_keep, dres_send, low_ref, weight_ref, sem = refs[6:]
        fetch = pltpu.make_async_copy(weight_hbm, weight_ref, sem)
        fetch.start()
        low_ref[:, 0:part_cols] = first_ref[...]
        conv_chunks(part_chunks, channels // LANES, *refs[:6], low_ref)
        core = my_core()
        for x in range(heads_axis // 2):
            dres_keep[x], dres_send[x] = sides(
                core, [low_ref[:, h * out_cols : (h + 1) * out_cols] for h in (2 * x, 2 * x + 1)]
            )
        fetch.wait()
        hg = dot(low_ref[...], weight_ref[...], NT_DIMS).astype(BF16)
        for chip in range(chips):
            heads = [cols(head_of(member_of(chip, c))) for c in (0, 1)]
            for at, part in ((0, slice(0, half)), (HEAD_DIM, slice(half, rows))):
                stay, leave = sides(core, [hg[part, c] for c in heads])
                hg_keep[chip, :, at : at + HEAD_DIM] = stay
                hg_send[chip, :, at : at + HEAD_DIM] = leave

    conv_in = (resid, upstream, got, *halos, taps_in)
    (conv_low,) = call(conv_first, [vmem((rows, part_cols))], name="conv", cost=CONV_COST)(*on_chip(*conv_in))
    mine = [keep, got] + exchange(keep, got, chips, my_chip, "regroup")

    def keys_body(keep_ref, got_ref, *refs):
        out_ref = refs[-1]
        for member, take in arrivals(my_chip(), my_core(), keep_ref, got_ref, refs[:-1]):
            out_ref[pl.ds(pl.multiple_of(member * rows, rows), rows), :] = take()[0:rows]

    *mine_here, _ = lax.optimization_barrier((*mine, conv_low))
    (both,) = call(keys_body, [vmem((supers, LANES))], name="keys")(*on_chip(*mine_here))

    steps = [(d, phase) for d in range(1, near + 1) for phase in (0, 1)]
    around = [step(both, d, phase) for d, phase in steps]

    conv_low, both_here = lax.optimization_barrier((conv_low, both))
    hg_keep, hg_send, dres_keep, dres_send = call(
        conv_second,
        [vmem((chips, half, LANES))] * 2 + [vmem((heads_axis // 2, rows, out_cols))] * 2,
        raw=(7,),
        scratch=[
            pltpu.VMEM((rows, channels), BF16),
            pltpu.VMEM(out_weight.shape, BF16),
            pltpu.SemaphoreType.DMA,
        ],
        name="conv_last",
        cost=CONV_COST,
    )(*on_chip(*conv_in, conv_low), *in_hbm(out_weight))
    hg_got = core_swap(hg_send)
    grads = [hg_keep, hg_got] + exchange(hg_keep, hg_got, chips, my_chip, "regroup_grads")
    q_tiles = supers // QT
    k_tiles = ext // QT
    first_tile = lead // QT
    own_tiles = range(near * q_tiles, (near + 1) * q_tiles)

    def seen(a):
        return range(a + first_tile, a + first_tile + tiles)

    def at_tile(t):
        return slice(t * QT, (t + 1) * QT)

    def score_body(*refs):
        len_ref, both_ref = refs[:2]
        mine_refs = refs[2 : 3 + chips]
        around_refs = refs[3 + chips : 3 + chips + 2 * near]
        e_ref, inv_ref, out_ref, kv, kt, qz, kb, qs, vt, s_sc = refs[3 + chips + 2 * near :]
        z = lax.axis_index("z")
        low = lax.broadcasted_iota(jnp.int32, (half, LANES), 1) < HEAD_DIM
        lane = lax.broadcasted_iota(jnp.int32, (half, LANES), 1)
        kv[near * supers : (near + 1) * supers, :] = both_ref[...]
        for member, take in arrivals(my_chip(), my_core(), mine_refs[0], mine_refs[1], mine_refs[2:]):
            q = take()[rows:slot].astype(F32) * scale
            for i, part in enumerate((q, pltpu.roll(q, HEAD_DIM, 1))):
                at = pl.ds(pl.multiple_of(member * rows + i * half, half), half)
                part = jnp.where(low, part, 0.0)
                qz[at, :] = part.astype(BF16)
                qs[at, :] = jnp.where(lane == HEAD_DIM, 1.0, part).astype(BF16)
        for d in range(1, near + 1):
            left, right = (near - d) * supers, (near + d) * supers
            odd = ((z // d) % 2) == 1

            @pl.when(odd)
            def _():
                kv[left : left + supers, :] = around_refs[2 * d - 2][...]
                kv[right : right + supers, :] = around_refs[2 * d - 1][...]

            @pl.when(jnp.logical_not(odd))
            def _():
                kv[left : left + supers, :] = around_refs[2 * d - 1][...]
                kv[right : right + supers, :] = around_refs[2 * d - 2][...]

        def limit(t):
            index = (z - near) * group + t // per_block
            inside = jnp.logical_and(index >= 0, index < ctx_count)
            length = len_ref[jnp.clip(index, 0, ctx_count - 1)]
            return jnp.where(inside, length, 0) - (t % per_block) * QT

        tile_lane = lax.broadcasted_iota(jnp.int32, (QT, LANES), 1)
        tile_row = lax.broadcasted_iota(jnp.int32, (QT, LANES), 0)

        for t in range(k_tiles):
            tile = kv[at_tile(t), :].astype(F32)
            turned = jnp.transpose(tile).astype(BF16)
            kt[:, at_tile(t)] = turned[0:HEAD_DIM]
            vt[0:HEAD_DIM, at_tile(t)] = turned[HEAD_DIM:LANES]
            dead = jnp.logical_and(tile_lane == HEAD_DIM, tile_row >= limit(t))
            kb[at_tile(t), :] = jnp.where(tile_lane < HEAD_DIM, tile, jnp.where(dead, NEG, 0.0)).astype(BF16)
        vt[HEAD_DIM:, :] = jnp.ones((ONES, ext), BF16)
        key_at = lax.broadcasted_iota(jnp.int32, (QT, QT), 0)
        query_at = lax.broadcasted_iota(jnp.int32, (QT, QT), 1)

        def scores(a, j, top):
            s = dot(kb[at_tile(a + j + first_tile), :], qs[at_tile(a), :], NT_DIMS)
            if j == 0:
                s = jnp.where(key_at >= query_at, s, NEG)
            if j == tiles - 1:
                s = jnp.where(key_at <= query_at, s, NEG)
            s_sc[a % 2, j] = s
            return jnp.maximum(top, jnp.max(s.reshape(QT // 8, 8, QT), axis=0))

        tops = [jnp.full((8, QT), NEG, F32) for _ in range(q_tiles)]
        for j in range(tiles):
            tops[0] = scores(0, j, tops[0])
        for a in range(q_tiles):
            top = jnp.max(tops[a], axis=0, keepdims=True)
            for j in range(tiles):
                if a + 1 < q_tiles:
                    tops[a + 1] = scores(a + 1, j, tops[a + 1])
                e = jnp.exp(s_sc[a % 2, j] - top)
                e_ref[a, at_tile(j), :] = e.astype(BF16)
            keys = slice((a + first_tile) * QT, (a + first_tile + tiles) * QT)
            out = dot(vt[:, keys], e_ref[a], NN_DIMS)
            inverse = 1.0 / out[HEAD_DIM : HEAD_DIM + 1]
            inv_ref[a] = inverse
            out_ref[a] = out[0:HEAD_DIM] * inverse

    exps, inverse, outs, kv, kt, qz = call(
        score_body,
        [
            vmem((q_tiles, tiles * QT, QT)),
            vmem((q_tiles, 1, QT), F32),
            vmem((q_tiles, HEAD_DIM, QT), F32),
            vmem((ext, LANES)),
            vmem((HEAD_DIM, ext)),
            vmem((supers, LANES)),
        ],
        smem=(0,),
        scratch=[
            pltpu.VMEM((ext, LANES), BF16),
            pltpu.VMEM((supers, LANES), BF16),
            pltpu.VMEM((HEAD_DIM + ONES, ext), BF16),
            pltpu.VMEM((2, tiles, QT, QT), F32),
        ],
        name="scores",
        cost=SCORES_COST,
    )(frame_lengths, *on_chip(both, *mine, *around))

    def key_tiles(a, ts, e_ref, inv_ref, delta_ref, kv, kt, qz, hz, acc, ds_sc, slopes_sc, base):
        q, g = qz[at_tile(a), :], hz[at_tile(a), :]
        keys = slice(ts[0] * QT, (ts[-1] + 1) * QT)
        slopes_sc[0 : len(ts) * QT, :] = dot(kv[keys, :], g, NT_DIMS)
        for i, t in enumerate(ts):
            p = e_ref[a, at_tile(t - a - first_tile), :].astype(F32) * inv_ref[a]
            ds = (p * (slopes_sc[at_tile(i), :] - delta_ref[a])).astype(BF16)
            ds_sc[at_tile(i), :] = ds
            part = dot(ds, q, NN_DIMS) + dot(p.astype(BF16), g, NN_DIMS)
            fresh = not any(t in seen(b) for b in range(a))
            acc[at_tile(t - base), :] = part if fresh else acc[at_tile(t - base), :] + part
        return dot(kt[:, keys], ds_sc[0 : len(ts) * QT, :], NN_DIMS)

    n_back = 2 * near

    def arrived(i, ref):
        d, phase = steps[i]
        z = lax.axis_index("z")
        partner = jnp.where((z // d) % 2 == phase, z + d, z - d)
        real = jnp.logical_and(partner >= 0, partner < z_count)
        return jnp.where(real, ref[...].astype(F32), 0.0)

    def far_body(*refs):
        grad_refs = refs[: 1 + chips]
        e_ref, inv_ref, out_ref, kv, kt, qz, hz, delta_ref, dq = refs[1 + chips : 10 + chips]
        back_refs = refs[10 + chips : -3]
        acc, ds_sc, slopes_sc = refs[-3:]
        z = lax.axis_index("z")
        low = lax.broadcasted_iota(jnp.int32, (half, LANES), 1) < HEAD_DIM
        for member, take in arrivals(my_chip(), my_core(), grad_refs[0], grad_refs[1], grad_refs[2:]):
            g = take().astype(F32)
            for i, part in enumerate((pltpu.roll(g, HEAD_DIM, 1), g)):
                at = pl.ds(pl.multiple_of(member * rows + i * half, half), half)
                hz[at, :] = jnp.where(low, 0.0, part).astype(BF16)
        for a in range(q_tiles):
            g = jnp.transpose(hz[at_tile(a), :].astype(F32))[HEAD_DIM:LANES]
            delta_ref[a] = jnp.sum(g * out_ref[a], axis=0, keepdims=True)
        for t in range(k_tiles):
            if not any(t in seen(a) for a in range(q_tiles)):
                acc[at_tile(t), :] = jnp.zeros((QT, LANES), F32)
        for a in range(q_tiles):
            left = [t for t in seen(a) if t < own_tiles[0]]
            right = [t for t in seen(a) if t > own_tiles[-1]]
            dq[a] = sum(
                key_tiles(a, ts, e_ref, inv_ref, delta_ref, kv, kt, qz, hz, acc, ds_sc.at[side], slopes_sc.at[side], 0)
                for side, ts in enumerate((left, right))
            )
        for i, (d, phase) in enumerate(steps):
            odd = ((z // d) % 2) == 1
            right = odd if phase else jnp.logical_not(odd)
            side = jnp.where(right, near + d, near - d) * supers
            back_refs[i][...] = acc[pl.ds(pl.multiple_of(side, supers), supers), :].astype(BF16)

    far = call(
        far_body,
        [vmem((supers, LANES)), vmem((q_tiles, 1, QT), F32), vmem((q_tiles, HEAD_DIM, QT), F32)]
        + [vmem((supers, LANES))] * n_back,
        scratch=[
            pltpu.VMEM((ext, LANES), F32),
            pltpu.VMEM((2, near * supers, QT), BF16),
            pltpu.VMEM((2, near * supers, QT), F32),
        ],
        name="far",
        cost=FAR_COST,
    )(*on_chip(*grads, exps, inverse, outs, kv, kt, qz))
    hz, delta, dq_far = far[:3]
    back = [step(far[3 + i], d, phase) for i, (d, phase) in enumerate(steps)]

    hb = block // 2

    def near_body(*refs):
        e_ref, inv_ref, delta_ref, kv, kt, qz, hz, far_ref = refs[:8]
        acc, dq_ref = refs[8:10]
        dq_sc, ds_sc, slopes_sc = refs[-3:]
        for a in range(q_tiles):
            dq = far_ref[a] + key_tiles(
                a, own_tiles, e_ref, inv_ref, delta_ref, kv, kt, qz, hz, acc, ds_sc.at[a % 2], slopes_sc.at[a % 2],
                own_tiles[0],
            )
            dq_sc[at_tile(a), 0:HEAD_DIM] = jnp.transpose(dq * scale)
        if group == 1:
            dq_ref[0] = dq_sc[:, 0:HEAD_DIM].astype(BF16)
            return
        y = lax.axis_index("y")
        for ref, slot in ((dq_ref, y), (refs[10], 1 - y)):
            at = pl.multiple_of(slot * block, block)
            upper = dq_sc[pl.ds(at, hb), 0:HEAD_DIM]
            lower = dq_sc[pl.ds(pl.multiple_of(at + hb, hb), hb), 0:HEAD_DIM]
            ref[...] = jnp.concatenate([upper, lower], axis=1).astype(BF16)

    results = call(
        near_body,
        [vmem((supers, LANES), F32)]
        + ([arr((1, block, HEAD_DIM))] if group == 1 else [vmem((hb, LANES))] * 2),
        scratch=[
            pltpu.VMEM((supers, LANES), F32),
            pltpu.VMEM((2, supers, QT), BF16),
            pltpu.VMEM((2, supers, QT), F32),
        ],
        name="near",
        cost=NEAR_COST,
    )(*on_chip(exps, inverse, delta, kv, kt, qz, hz, dq_far))
    own, dq = results[:2]
    dres_got = core_swap(dres_send)
    dres_keep, dres_got, _ = lax.optimization_barrier((dres_keep, dres_got, results[0]))
    dres = [dres_keep, dres_got] + exchange(
        dres_keep, dres_got, heads_axis // 2, lambda: lax.axis_index("head") // 2, "regroup_resid"
    )

    def resid_body(*refs):
        for member, take in arrivals(lax.axis_index("head") // 2, my_core(), refs[0], refs[1], refs[2:-1]):
            refs[-1][0, pl.ds(pl.multiple_of(member * rows, rows), rows), :] = take()

    (d_resid,) = call(resid_body, [arr((1, block, out_cols))], name="resid", cost=RESID_COST)(*on_chip(*dres))

    if group == 1:

        def last_body(*refs):
            total = refs[0][...]
            for i in range(n_back):
                total = total + arrived(i, refs[1 + i])
            total = total.astype(BF16)
            refs[-2][0] = total[:, 0:HEAD_DIM]
            refs[-1][0] = total[:, HEAD_DIM:LANES]

        d_key, d_value = call(last_body, [arr((1, block, HEAD_DIM))] * 2, name="last")(*on_chip(own, *back))
        return d_resid, dq, d_key, d_value

    def y_swap(x):
        return lax.ppermute(x, mesh_axes, everyone(lambda h, z, y: (h, z, 1 - y)))

    def sum_body(own_ref, dq_send_ref, *refs):
        keep_ref, send_ref = refs[-2:]
        total = own_ref[...]
        for i in range(n_back):
            total = total + arrived(i, refs[i])
        total = total.astype(BF16)
        first = lax.axis_index("y") == 0
        keep_ref[...] = jnp.where(first, total[0:block], total[block:supers])
        send_ref[0:block, :] = jnp.where(first, total[block:supers], total[0:block])
        send_ref[block:, :] = dq_send_ref[...]

    keep, send = call(sum_body, [vmem((block, LANES)), vmem((block + hb, LANES))], name="sum")(
        *on_chip(own, results[2], *back)
    )
    other = y_swap(send)

    def last_body(*refs):
        keep_ref, other_ref, dq_keep_ref = refs[:3]
        dq_ref, dk_ref, dv_ref = refs[-3:]
        first = lax.axis_index("y") == 0
        low = lax.broadcasted_iota(jnp.int32, (block, LANES), 1) < HEAD_DIM

        def ordered(mine, peer):
            mine, peer = mine.astype(F32), peer.astype(F32)
            return jnp.where(first, mine, peer), jnp.where(first, peer, mine)

        lo, up = ordered(keep_ref[...], other_ref[0:block, :])
        dk_ref[0] = jnp.where(low, lo, pltpu.roll(up, HEAD_DIM, 1)).astype(BF16)
        dv_ref[0] = jnp.where(low, pltpu.roll(lo, HEAD_DIM, 1), up).astype(BF16)
        lo, up = ordered(dq_keep_ref[...], other_ref[block:, :])
        low = low[0:hb]
        dq_ref[0, 0:hb, :] = jnp.where(low, lo, pltpu.roll(up, HEAD_DIM, 1)).astype(BF16)
        dq_ref[0, hb:block, :] = jnp.where(low, pltpu.roll(lo, HEAD_DIM, 1), up).astype(BF16)

    d_query, d_key, d_value = call(last_body, [arr((1, block, LANES))] * 3, name="last")(
        *on_chip(keep, other, dq)
    )
    return d_resid, d_query, d_key, d_value


def solution(mesh):
    heads_axis = mesh.shape["head"]
    ctx_count = mesh.shape["ctx"]

    def run(query, *rest):
        group = query.shape[2] // HEAD_DIM // heads_axis
        z_count = ctx_count // group
        fine = Mesh(mesh.devices.reshape(heads_axis, z_count, group), ("head", "z", "y"))
        rows_spec = P(("z", "y"), "head", None)
        cols_spec = P(("z", "y"), None, "head")
        sizes = (heads_axis, z_count, group)
        return jax.shard_map(
            lambda *args: on_device(sizes, *args),
            mesh=fine,
            in_specs=(rows_spec,) * 5 + (P(),) * 3,
            out_specs=(cols_spec,) * 4,
            check_vma=False,
        )(query, *rest)

    return run
```

```python
import jax
import jax.numpy as jnp
from jax import lax
from jax.experimental import pallas as pl
from jax.experimental.pallas import tpu as pltpu
from jax.sharding import Mesh
from jax.sharding import PartitionSpec as P

HEAD_DIM = 64
KERNEL = 31
REACH = 2
LANES = 128
QT = 256
HALO = 32
HALF = 16
NEG = -1e30
ONES = 16
F32 = jnp.float32
BF16 = jnp.bfloat16
NT_DIMS = (((1,), (1,)), ((), ()))
NN_DIMS = (((1,), (0,)), ((), ()))
VMEM_LIMIT = 12 * 1024 * 1024
CONV_COST = (3_000_000_000, 0, 0)
SCORES_COST = (9_000_000_000, 0, 0)
FAR_COST = (2_000_000_000, 0, 0)
NEAR_COST = (4_000_000_000, 0, 0)
RESID_COST = (1_000_000_000, 0, 0)


def dot(a, b, dims):
    return lax.dot_general(a, b, dims, preferred_element_type=F32)


def call(body, outs, smem=(), raw=(), scratch=(), name=None, cost=None):
    on_vmem = pl.BlockSpec(memory_space=pltpu.VMEM)
    spaces = {i: pltpu.SMEM for i in smem} | {i: pltpu.HBM for i in raw}

    def run(*args):
        return pl.pallas_call(
            body,
            out_shape=outs,
            in_specs=[pl.BlockSpec(memory_space=spaces.get(i, pltpu.VMEM)) for i in range(len(args))],
            out_specs=[on_vmem] * len(outs),
            scratch_shapes=list(scratch),
            compiler_params=pltpu.CompilerParams(vmem_limit_bytes=VMEM_LIMIT),
            cost_estimate=None if cost is None else pl.CostEstimate(*cost),
            name=name,
        )(*args)

    return run


def arr(shape, dtype=BF16):
    return jax.ShapeDtypeStruct(shape, dtype)


def vmem(shape, dtype=BF16):
    return pltpu.VMEM(shape, dtype)


def on_chip(*arrays):
    return [pltpu.with_memory_space_constraint(x, pltpu.VMEM) for x in arrays]


def in_hbm(*arrays):
    return [pltpu.with_memory_space_constraint(x, pltpu.HBM) for x in arrays]


def on_device(sizes, query, key, value, resid_in, out_grad, out_weight, conv_kernel, frame_lengths):
    heads_axis, z_count, group = sizes
    ctx_count = z_count * group
    rows = query.shape[1]
    width = query.shape[2]
    channels = resid_in.shape[2]
    block = rows * heads_axis
    supers = group * block
    members = group * heads_axis
    chips = members // 2
    half = rows // 2
    near = -(-REACH // group)
    window = REACH * block
    tiles = 2 * window // QT + 1
    per_block = block // QT
    lead = near * supers - window
    ext = (2 * near + 1) * supers
    out_cols = channels // heads_axis
    scale = HEAD_DIM ** (-0.5)

    def head_of(member):
        return group * (member % heads_axis) + member // heads_axis

    def cols(head):
        return slice(head * HEAD_DIM, (head + 1) * HEAD_DIM)

    def sides(core, slots):
        first, second = slots
        return jnp.where(core == 0, first, second), jnp.where(core == 0, second, first)

    def member_of(chip, core):
        return chip * 2 + core

    def my_chip():
        return lax.axis_index("y") * (heads_axis // 2) + lax.axis_index("head") // 2

    def my_core():
        return lax.axis_index("head") % 2

    slot = rows + half
    edge_rows = HALO + HALF

    def pack_body(q_hbm, k_hbm, v_hbm, resid_ref, grad_ref, taps_ref, *refs):
        keep_ref, send_ref, second_ref, resid_out, grad_out, taps_out, q_ref, k_ref, v_ref, sems = refs
        copies = [
            pltpu.make_async_copy(source, target, sems.at[i])
            for i, (source, target) in enumerate(
                (
                    (resid_ref, resid_out), (grad_ref, grad_out), (k_hbm, k_ref), (v_hbm, v_ref),
                    (q_hbm, q_ref), (taps_ref, taps_out),
                )
            )
        ]
        for copy in copies:
            copy.start()
        core = my_core()
        copies[0].wait()
        copies[1].wait()
        odd = core == 1
        resid_top, resid_low = resid_out[0, 0:HALO, :], resid_out[0, rows - HALO : rows, :]
        grad_top, grad_low = grad_out[0, 0:HALF, :], grad_out[0, rows - HALF : rows, :]
        second_ref[0:HALO, :] = jnp.where(odd, resid_low, resid_top)
        second_ref[HALO:edge_rows, :] = jnp.where(odd, grad_low, grad_top)
        resid_first = jnp.where(odd, resid_top, resid_low)
        grad_first = jnp.where(odd, grad_top, grad_low)
        for c in range(channels // LANES):
            at = chips * slot + c * edge_rows
            lane = slice(c * LANES, (c + 1) * LANES)
            send_ref[at : at + HALO, :] = resid_first[:, lane]
            send_ref[at + HALO : at + edge_rows, :] = grad_first[:, lane]
        for copy in copies[2:]:
            copy.wait()
        for chip in range(chips):
            heads = [cols(head_of(member_of(chip, c))) for c in (0, 1)]
            for at, width, c_ref, low, high in (
                (0, 0, k_ref, 0, rows),
                (0, HEAD_DIM, v_ref, 0, rows),
                (rows, 0, q_ref, 0, half),
                (rows, HEAD_DIM, q_ref, half, rows),
            ):
                stay, leave = sides(core, [c_ref[0, low:high, c] for c in heads])
                keep_ref[chip, at : at + high - low, width : width + HEAD_DIM] = stay
                at = at + chip * slot
                send_ref[at : at + high - low, width : width + HEAD_DIM] = leave

    raw = pl.BlockSpec(memory_space=pltpu.HBM)
    on_vmem = pl.BlockSpec(memory_space=pltpu.VMEM)
    pack_outs = [
        vmem((chips, slot, LANES)), vmem((chips * slot + edge_rows * channels // LANES, LANES)),
        vmem((edge_rows, channels)),
        vmem((1, rows, channels)), vmem((1, rows, channels)), vmem(conv_kernel.shape),
    ]
    keep, send, second, resid, upstream, taps_in = pl.pallas_call(
        pack_body,
        out_shape=pack_outs,
        in_specs=[raw] * 6,
        out_specs=[on_vmem] * 6,
        scratch_shapes=[pltpu.VMEM((1, rows, width), BF16)] * 3 + [pltpu.SemaphoreType.DMA((6,))],
        compiler_params=pltpu.CompilerParams(vmem_limit_bytes=VMEM_LIMIT),
        name="pack",
    )(*in_hbm(query, key, value, resid_in, out_grad, conv_kernel))

    mesh_axes = ("head", "z", "y")

    def place(head, z, y):
        return head * ctx_count + z * group + y

    def everyone(target):
        return [
            (place(h, z, y), place(*target(h, z, y)))
            for h in range(heads_axis)
            for z in range(z_count)
            for y in range(group)
        ]

    def core_swap(x):
        return lax.ppermute(x, mesh_axes, everyone(lambda h, z, y: (h ^ 1, z, y)))

    def step(x, d, phase):
        def target(h, z, y):
            partner = z + d if (z // d) % 2 == phase else z - d
            return (h, partner, y) if 0 <= partner < z_count else (h ^ 1, z, y)

        return lax.ppermute(x, mesh_axes, everyone(target))

    def slot_of(ref, i, like):
        size = like.shape[1]
        return ref[i] if len(ref.shape) == 3 else ref[pl.ds(pl.multiple_of(i * size, size), size), :]

    def exchange(keep, got, count, index, name):
        def body(keep_ref, got_ref, *out_refs):
            me = index()
            for m, out_ref in enumerate(out_refs, 1):
                out_ref[0] = keep_ref[me ^ m]
                out_ref[1] = slot_of(got_ref, me ^ m, keep_ref)

        per_row = heads_axis // 2

        def target(m):
            def f(h, z, y):
                chip = (y * per_row + h // 2) ^ m
                return (chip % per_row) * 2 + h % 2, z, chip // per_row

            return f

        parts = call(body, [vmem((2,) + keep.shape[1:])] * (count - 1), name=name)(*on_chip(keep, got))
        return [lax.ppermute(part, mesh_axes, everyone(target(m))) for m, part in enumerate(parts, 1)]

    def arrivals(me, core, keep_ref, got_ref, part_refs):
        out = [(member_of(me, core), lambda: keep_ref[me]), (member_of(me, 1 - core), lambda: slot_of(got_ref, me, keep_ref))]
        for m, ref in enumerate(part_refs, 1):
            out.append((member_of(me ^ m, core), lambda ref=ref: ref[0]))
            out.append((member_of(me ^ m, 1 - core), lambda ref=ref: ref[1]))
        return out

    got = core_swap(send)

    last_head = heads_axis - 1

    def inside(h, z, y):
        if 0 < h < last_head:
            return (h + 1 if h % 2 else h - 1), z, y
        return (h, z, 1 - y) if group == 2 else (last_head - h, z, y)

    outer = {}
    idle = []
    for ctx in range(ctx_count):
        for h in range(heads_axis):
            if h == last_head and ctx < ctx_count - 1:
                outer[h, ctx] = (0, ctx + 1)
                outer[0, ctx + 1] = (h, ctx)
            elif 0 < h < last_head or (h, ctx) in ((0, 0), (last_head, ctx_count - 1)):
                idle.append((h, ctx))
    for one, two in zip(idle[::2], idle[1::2]):
        outer[one], outer[two] = two, one

    def outside(h, z, y):
        head, ctx = outer[h, z * group + y]
        return head, ctx // group, ctx % group

    halos = [
        lax.ppermute(second, mesh_axes, everyone(inside)),
        lax.ppermute(second, mesh_axes, everyone(outside)),
    ]
    span = rows + 2 * HALF

    part_chunks = channels // LANES * 6 // 8
    part_cols = part_chunks * LANES

    def conv_chunks(start, stop, resid_ref, grad_ref, core_ref, inside_ref, outside_ref, taps_ref, low_ref):
        head, ctx = lax.axis_index("head"), lax.axis_index("z") * group + lax.axis_index("y")
        odd = (head % 2) == 1
        edge = jnp.logical_or(head == 0, head == heads_axis - 1)
        starts = jnp.logical_and(head == 0, ctx == 0)
        ends = jnp.logical_and(head == heads_axis - 1, ctx == ctx_count - 1)

        def taps_sum(x, tap_of, length):
            total = None
            for b in range(8):
                part = None
                for a in range(4):
                    offset = 8 * a + b
                    if offset < 1 or offset > KERNEL:
                        continue
                    term = tap_of(offset - 1) * x[8 * a : 8 * a + length + 8]
                    part = term if part is None else part + term
                if b:
                    part = pltpu.roll(part, length + 8 - b, 0)
                part = part[0:length]
                total = part if total is None else total + part
            return total

        def chunk(c, carry):
            at = pl.multiple_of(c * LANES, LANES)
            lane = pl.ds(at, LANES)
            at = pl.multiple_of(chips * slot + c * edge_rows, HALF)
            first = core_ref[pl.ds(at, edge_rows), :].astype(F32)
            second = jnp.where(edge, outside_ref[:, lane].astype(F32), inside_ref[:, lane].astype(F32))
            before = jnp.where(starts, 0.0, jnp.where(odd, first, second))
            after = jnp.where(ends, 0.0, jnp.where(odd, second, first))
            taps = taps_ref[:, lane].astype(F32)
            x = jnp.concatenate([before[0:HALO], resid_ref[0, :, lane].astype(F32), after[0:HALO]], axis=0)
            middle = grad_ref[0, :, lane].astype(F32)
            g = jnp.concatenate([before[HALO:], middle, after[HALO:]], axis=0)
            pre = taps_sum(x, lambda k: taps[k : k + 1], span)
            s = 1.0 / (1.0 + jnp.exp(-pre))
            cg = g * (s * (1.0 + pre * (1.0 - s)))
            out = middle + taps_sum(cg, lambda k: taps[KERNEL - 1 - k : KERNEL - k], rows)
            low_ref[:, lane] = out.astype(BF16)
            return carry

        lax.fori_loop(start, stop, chunk, 0)

    def conv_first(*refs):
        conv_chunks(0, part_chunks, *refs)

    def conv_second(*refs):
        first_ref, weight_hbm, hg_keep, hg_send, dres_keep, dres_send, low_ref, weight_ref, sem = refs[6:]
        fetch = pltpu.make_async_copy(weight_hbm, weight_ref, sem)
        fetch.start()
        low_ref[:, 0:part_cols] = first_ref[...]
        conv_chunks(part_chunks, channels // LANES, *refs[:6], low_ref)
        core = my_core()
        for x in range(heads_axis // 2):
            dres_keep[x], dres_send[x] = sides(
                core, [low_ref[:, h * out_cols : (h + 1) * out_cols] for h in (2 * x, 2 * x + 1)]
            )
        fetch.wait()
        hg = dot(low_ref[...], weight_ref[...], NT_DIMS).astype(BF16)
        for chip in range(chips):
            heads = [cols(head_of(member_of(chip, c))) for c in (0, 1)]
            for at, part in ((0, slice(0, half)), (HEAD_DIM, slice(half, rows))):
                stay, leave = sides(core, [hg[part, c] for c in heads])
                hg_keep[chip, :, at : at + HEAD_DIM] = stay
                hg_send[chip, :, at : at + HEAD_DIM] = leave

    conv_in = (resid, upstream, got, *halos, taps_in)
    (conv_low,) = call(conv_first, [vmem((rows, part_cols))], name="conv", cost=CONV_COST)(*on_chip(*conv_in))
    mine = [keep, got] + exchange(keep, got, chips, my_chip, "regroup")

    def keys_body(keep_ref, got_ref, *refs):
        out_ref = refs[-1]
        for member, take in arrivals(my_chip(), my_core(), keep_ref, got_ref, refs[:-1]):
            out_ref[pl.ds(pl.multiple_of(member * rows, rows), rows), :] = take()[0:rows]

    *mine_here, _ = lax.optimization_barrier((*mine, conv_low))
    (both,) = call(keys_body, [vmem((supers, LANES))], name="keys")(*on_chip(*mine_here))

    steps = [(d, phase) for d in range(1, near + 1) for phase in (0, 1)]
    around = [step(both, d, phase) for d, phase in steps]

    conv_low, both_here = lax.optimization_barrier((conv_low, both))
    hg_keep, hg_send, dres_keep, dres_send = call(
        conv_second,
        [vmem((chips, half, LANES))] * 2 + [vmem((heads_axis // 2, rows, out_cols))] * 2,
        raw=(7,),
        scratch=[
            pltpu.VMEM((rows, channels), BF16),
            pltpu.VMEM(out_weight.shape, BF16),
            pltpu.SemaphoreType.DMA,
        ],
        name="conv_last",
        cost=CONV_COST,
    )(*on_chip(*conv_in, conv_low), *in_hbm(out_weight))
    hg_got = core_swap(hg_send)
    grads = [hg_keep, hg_got] + exchange(hg_keep, hg_got, chips, my_chip, "regroup_grads")
    q_tiles = supers // QT
    k_tiles = ext // QT
    first_tile = lead // QT
    own_tiles = range(near * q_tiles, (near + 1) * q_tiles)

    def seen(a):
        return range(a + first_tile, a + first_tile + tiles)

    def at_tile(t):
        return slice(t * QT, (t + 1) * QT)

    def score_body(*refs):
        len_ref, both_ref = refs[:2]
        mine_refs = refs[2 : 3 + chips]
        around_refs = refs[3 + chips : 3 + chips + 2 * near]
        e_ref, inv_ref, out_ref, kv, kt, qz, kb, qs, vt, s_sc = refs[3 + chips + 2 * near :]
        z = lax.axis_index("z")
        low = lax.broadcasted_iota(jnp.int32, (half, LANES), 1) < HEAD_DIM
        lane = lax.broadcasted_iota(jnp.int32, (half, LANES), 1)
        kv[near * supers : (near + 1) * supers, :] = both_ref[...]
        for member, take in arrivals(my_chip(), my_core(), mine_refs[0], mine_refs[1], mine_refs[2:]):
            q = take()[rows:slot].astype(F32) * scale
            for i, part in enumerate((q, pltpu.roll(q, HEAD_DIM, 1))):
                at = pl.ds(pl.multiple_of(member * rows + i * half, half), half)
                part = jnp.where(low, part, 0.0)
                qz[at, :] = part.astype(BF16)
                qs[at, :] = jnp.where(lane == HEAD_DIM, 1.0, part).astype(BF16)
        for d in range(1, near + 1):
            left, right = (near - d) * supers, (near + d) * supers
            odd = ((z // d) % 2) == 1

            @pl.when(odd)
            def _():
                kv[left : left + supers, :] = around_refs[2 * d - 2][...]
                kv[right : right + supers, :] = around_refs[2 * d - 1][...]

            @pl.when(jnp.logical_not(odd))
            def _():
                kv[left : left + supers, :] = around_refs[2 * d - 1][...]
                kv[right : right + supers, :] = around_refs[2 * d - 2][...]

        def limit(t):
            index = (z - near) * group + t // per_block
            inside = jnp.logical_and(index >= 0, index < ctx_count)
            length = len_ref[jnp.clip(index, 0, ctx_count - 1)]
            return jnp.where(inside, length, 0) - (t % per_block) * QT

        tile_lane = lax.broadcasted_iota(jnp.int32, (QT, LANES), 1)
        tile_row = lax.broadcasted_iota(jnp.int32, (QT, LANES), 0)

        for t in range(k_tiles):
            tile = kv[at_tile(t), :].astype(F32)
            turned = jnp.transpose(tile).astype(BF16)
            kt[:, at_tile(t)] = turned[0:HEAD_DIM]
            vt[0:HEAD_DIM, at_tile(t)] = turned[HEAD_DIM:LANES]
            dead = jnp.logical_and(tile_lane == HEAD_DIM, tile_row >= limit(t))
            kb[at_tile(t), :] = jnp.where(tile_lane < HEAD_DIM, tile, jnp.where(dead, NEG, 0.0)).astype(BF16)
        vt[HEAD_DIM:, :] = jnp.ones((ONES, ext), BF16)
        key_at = lax.broadcasted_iota(jnp.int32, (QT, QT), 0)
        query_at = lax.broadcasted_iota(jnp.int32, (QT, QT), 1)

        def scores(a, j, top):
            s = dot(kb[at_tile(a + j + first_tile), :], qs[at_tile(a), :], NT_DIMS)
            if j == 0:
                s = jnp.where(key_at >= query_at, s, NEG)
            if j == tiles - 1:
                s = jnp.where(key_at <= query_at, s, NEG)
            s_sc[a % 2, j] = s
            return jnp.maximum(top, jnp.max(s.reshape(QT // 8, 8, QT), axis=0))

        tops = [jnp.full((8, QT), NEG, F32) for _ in range(q_tiles)]
        for j in range(tiles):
            tops[0] = scores(0, j, tops[0])
        for a in range(q_tiles):
            top = jnp.max(tops[a], axis=0, keepdims=True)
            for j in range(tiles):
                if a + 1 < q_tiles:
                    tops[a + 1] = scores(a + 1, j, tops[a + 1])
                e = jnp.exp(s_sc[a % 2, j] - top)
                e_ref[a, at_tile(j), :] = e.astype(BF16)
            keys = slice((a + first_tile) * QT, (a + first_tile + tiles) * QT)
            out = dot(vt[:, keys], e_ref[a], NN_DIMS)
            inverse = 1.0 / out[HEAD_DIM : HEAD_DIM + 1]
            inv_ref[a] = inverse
            out_ref[a] = out[0:HEAD_DIM] * inverse

    exps, inverse, outs, kv, kt, qz = call(
        score_body,
        [
            vmem((q_tiles, tiles * QT, QT)),
            vmem((q_tiles, 1, QT), F32),
            vmem((q_tiles, HEAD_DIM, QT), F32),
            vmem((ext, LANES)),
            vmem((HEAD_DIM, ext)),
            vmem((supers, LANES)),
        ],
        smem=(0,),
        scratch=[
            pltpu.VMEM((ext, LANES), BF16),
            pltpu.VMEM((supers, LANES), BF16),
            pltpu.VMEM((HEAD_DIM + ONES, ext), BF16),
            pltpu.VMEM((2, tiles, QT, QT), F32),
        ],
        name="scores",
        cost=SCORES_COST,
    )(frame_lengths, *on_chip(both, *mine, *around))

    def key_tiles(a, ts, e_ref, inv_ref, delta_ref, kv, kt, qz, hz, acc, ds_sc, slopes_sc, base):
        q, g = qz[at_tile(a), :], hz[at_tile(a), :]
        keys = slice(ts[0] * QT, (ts[-1] + 1) * QT)
        slopes_sc[0 : len(ts) * QT, :] = dot(kv[keys, :], g, NT_DIMS)
        for i, t in enumerate(ts):
            p = e_ref[a, at_tile(t - a - first_tile), :].astype(F32) * inv_ref[a]
            ds = (p * (slopes_sc[at_tile(i), :] - delta_ref[a])).astype(BF16)
            ds_sc[at_tile(i), :] = ds
            part = dot(ds, q, NN_DIMS) + dot(p.astype(BF16), g, NN_DIMS)
            fresh = not any(t in seen(b) for b in range(a))
            acc[at_tile(t - base), :] = part if fresh else acc[at_tile(t - base), :] + part
        return dot(kt[:, keys], ds_sc[0 : len(ts) * QT, :], NN_DIMS)

    n_back = 2 * near

    def arrived(i, ref):
        d, phase = steps[i]
        z = lax.axis_index("z")
        partner = jnp.where((z // d) % 2 == phase, z + d, z - d)
        real = jnp.logical_and(partner >= 0, partner < z_count)
        return jnp.where(real, ref[...].astype(F32), 0.0)

    def far_call(i, first, ins):
        d, phase = steps[i]

        def body(*refs):
            if first:
                grad_refs = refs[: 1 + chips]
                e_ref, inv_ref, out_ref, kv, kt, qz, hz, delta_ref, dq, back_ref = refs[1 + chips : 11 + chips]
                low = lax.broadcasted_iota(jnp.int32, (half, LANES), 1) < HEAD_DIM
                for member, take in arrivals(my_chip(), my_core(), grad_refs[0], grad_refs[1], grad_refs[2:]):
                    g = take().astype(F32)
                    for k, piece in enumerate((pltpu.roll(g, HEAD_DIM, 1), g)):
                        at = pl.ds(pl.multiple_of(member * rows + k * half, half), half)
                        hz[at, :] = jnp.where(low, 0.0, piece).astype(BF16)
                for a in range(q_tiles):
                    g = jnp.transpose(hz[at_tile(a), :].astype(F32))[HEAD_DIM:LANES]
                    delta_ref[a] = jnp.sum(g * out_ref[a], axis=0, keepdims=True)
            else:
                e_ref, inv_ref, kv, kt, qz, hz, delta_ref, dq_in, dq, back_ref = refs[:10]
            acc, ds_sc, slopes_sc = refs[-3:]
            odd = ((lax.axis_index("z") // d) % 2) == 1
            right = odd if phase else jnp.logical_not(odd)

            def side(tiles_here):
                for t in tiles_here:
                    if not any(t in seen(a) for a in range(q_tiles)):
                        acc[at_tile(t - tiles_here[0]), :] = jnp.zeros((QT, LANES), F32)
                for a in range(q_tiles):
                    ts = [t for t in tiles_here if t in seen(a)]
                    total = jnp.zeros((HEAD_DIM, QT), F32) if first else dq_in[a]
                    if ts:
                        total = total + key_tiles(
                            a, ts, e_ref, inv_ref, delta_ref, kv, kt, qz, hz, acc,
                            ds_sc.at[a % 2], slopes_sc.at[a % 2], tiles_here[0],
                        )
                    dq[a] = total

            def tiles_at(distance):
                return range((near + distance) * q_tiles, (near + distance + 1) * q_tiles)

            @pl.when(right)
            def _():
                side(tiles_at(d))

            @pl.when(jnp.logical_not(right))
            def _():
                side(tiles_at(-d))

            back_ref[...] = acc[...].astype(BF16)

        ready = [vmem((supers, LANES)), vmem((q_tiles, 1, QT), F32)] if first else []
        return call(
            body,
            ready + [vmem((q_tiles, HEAD_DIM, QT), F32), vmem((supers, LANES))],
            scratch=[
                pltpu.VMEM((supers, LANES), F32),
                pltpu.VMEM((2, supers, QT), BF16),
                pltpu.VMEM((2, supers, QT), F32),
            ],
            name="far" if first else "far_next",
            cost=FAR_COST,
        )(*on_chip(*ins))

    hz, delta, dq_far, part_here = far_call(0, True, (*grads, exps, inverse, outs, kv, kt, qz))
    back = [step(part_here, *steps[0])]
    for i in range(1, n_back):
        dq_far, part_here = far_call(i, False, (exps, inverse, kv, kt, qz, hz, delta, dq_far))
        back.append(step(part_here, *steps[i]))

    hb = block // 2

    def near_body(*refs):
        e_ref, inv_ref, delta_ref, kv, kt, qz, hz, far_ref = refs[:8]
        acc, dq_ref = refs[8:10]
        dq_sc, ds_sc, slopes_sc = refs[-3:]
        for a in range(q_tiles):
            dq = far_ref[a] + key_tiles(
                a, own_tiles, e_ref, inv_ref, delta_ref, kv, kt, qz, hz, acc, ds_sc.at[a % 2], slopes_sc.at[a % 2],
                own_tiles[0],
            )
            dq_sc[at_tile(a), 0:HEAD_DIM] = jnp.transpose(dq * scale)
        if group == 1:
            dq_ref[0] = dq_sc[:, 0:HEAD_DIM].astype(BF16)
            return
        y = lax.axis_index("y")
        for ref, slot in ((dq_ref, y), (refs[10], 1 - y)):
            at = pl.multiple_of(slot * block, block)
            upper = dq_sc[pl.ds(at, hb), 0:HEAD_DIM]
            lower = dq_sc[pl.ds(pl.multiple_of(at + hb, hb), hb), 0:HEAD_DIM]
            ref[...] = jnp.concatenate([upper, lower], axis=1).astype(BF16)

    results = call(
        near_body,
        [vmem((supers, LANES), F32)]
        + ([arr((1, block, HEAD_DIM))] if group == 1 else [vmem((hb, LANES))] * 2),
        scratch=[
            pltpu.VMEM((supers, LANES), F32),
            pltpu.VMEM((2, supers, QT), BF16),
            pltpu.VMEM((2, supers, QT), F32),
        ],
        name="near",
        cost=NEAR_COST,
    )(*on_chip(exps, inverse, delta, kv, kt, qz, hz, dq_far))
    own, dq = results[:2]
    dres_got = core_swap(dres_send)
    dres_keep, dres_got, _ = lax.optimization_barrier((dres_keep, dres_got, results[0]))
    dres = [dres_keep, dres_got] + exchange(
        dres_keep, dres_got, heads_axis // 2, lambda: lax.axis_index("head") // 2, "regroup_resid"
    )

    def resid_body(*refs):
        for member, take in arrivals(lax.axis_index("head") // 2, my_core(), refs[0], refs[1], refs[2:-1]):
            refs[-1][0, pl.ds(pl.multiple_of(member * rows, rows), rows), :] = take()

    (d_resid,) = call(resid_body, [arr((1, block, out_cols))], name="resid", cost=RESID_COST)(*on_chip(*dres))

    if group == 1:

        def last_body(*refs):
            total = refs[0][...]
            for i in range(n_back):
                total = total + arrived(i, refs[1 + i])
            total = total.astype(BF16)
            refs[-2][0] = total[:, 0:HEAD_DIM]
            refs[-1][0] = total[:, HEAD_DIM:LANES]

        d_key, d_value = call(last_body, [arr((1, block, HEAD_DIM))] * 2, name="last")(*on_chip(own, *back))
        return d_resid, dq, d_key, d_value

    def y_swap(x):
        return lax.ppermute(x, mesh_axes, everyone(lambda h, z, y: (h, z, 1 - y)))

    def sum_body(own_ref, dq_send_ref, *refs):
        keep_ref, send_ref = refs[-2:]
        total = own_ref[...]
        for i in range(n_back):
            total = total + arrived(i, refs[i])
        total = total.astype(BF16)
        first = lax.axis_index("y") == 0
        keep_ref[...] = jnp.where(first, total[0:block], total[block:supers])
        send_ref[0:block, :] = jnp.where(first, total[block:supers], total[0:block])
        send_ref[block:, :] = dq_send_ref[...]

    keep, send = call(sum_body, [vmem((block, LANES)), vmem((block + hb, LANES))], name="sum")(
        *on_chip(own, results[2], *back)
    )
    other = y_swap(send)

    def last_body(*refs):
        keep_ref, other_ref, dq_keep_ref = refs[:3]
        dq_ref, dk_ref, dv_ref = refs[-3:]
        first = lax.axis_index("y") == 0
        low = lax.broadcasted_iota(jnp.int32, (block, LANES), 1) < HEAD_DIM

        def ordered(mine, peer):
            mine, peer = mine.astype(F32), peer.astype(F32)
            return jnp.where(first, mine, peer), jnp.where(first, peer, mine)

        lo, up = ordered(keep_ref[...], other_ref[0:block, :])
        dk_ref[0] = jnp.where(low, lo, pltpu.roll(up, HEAD_DIM, 1)).astype(BF16)
        dv_ref[0] = jnp.where(low, pltpu.roll(lo, HEAD_DIM, 1), up).astype(BF16)
        lo, up = ordered(dq_keep_ref[...], other_ref[block:, :])
        low = low[0:hb]
        dq_ref[0, 0:hb, :] = jnp.where(low, lo, pltpu.roll(up, HEAD_DIM, 1)).astype(BF16)
        dq_ref[0, hb:block, :] = jnp.where(low, pltpu.roll(lo, HEAD_DIM, 1), up).astype(BF16)

    d_query, d_key, d_value = call(last_body, [arr((1, block, LANES))] * 3, name="last")(
        *on_chip(keep, other, dq)
    )
    return d_resid, d_query, d_key, d_value


def solution(mesh):
    heads_axis = mesh.shape["head"]
    ctx_count = mesh.shape["ctx"]

    def run(query, *rest):
        group = query.shape[2] // HEAD_DIM // heads_axis
        z_count = ctx_count // group
        fine = Mesh(mesh.devices.reshape(heads_axis, z_count, group), ("head", "z", "y"))
        rows_spec = P(("z", "y"), "head", None)
        cols_spec = P(("z", "y"), None, "head")
        sizes = (heads_axis, z_count, group)
        return jax.shard_map(
            lambda *args: on_device(sizes, *args),
            mesh=fine,
            in_specs=(rows_spec,) * 5 + (P(),) * 3,
            out_specs=(cols_spec,) * 4,
            check_vma=False,
        )(query, *rest)

    return run
```

```python
import jax
import jax.numpy as jnp
from jax import lax
from jax.experimental import pallas as pl
from jax.experimental.pallas import tpu as pltpu
from jax.sharding import Mesh
from jax.sharding import PartitionSpec as P

HEAD_DIM = 64
KERNEL = 31
REACH = 2
LANES = 128
QT = 256
HALO = 32
HALF = 16
NEG = -1e30
ONES = 16
F32 = jnp.float32
BF16 = jnp.bfloat16
NT_DIMS = (((1,), (1,)), ((), ()))
NN_DIMS = (((1,), (0,)), ((), ()))
VMEM_LIMIT = 12 * 1024 * 1024
CONV_COST = (3_000_000_000, 0, 0)
SCORES_COST = (9_000_000_000, 0, 0)
FAR_COST = (2_000_000_000, 0, 0)
NEAR_COST = (4_000_000_000, 0, 0)
RESID_COST = (1_000_000_000, 0, 0)


def dot(a, b, dims):
    return lax.dot_general(a, b, dims, preferred_element_type=F32)


def call(body, outs, smem=(), raw=(), scratch=(), name=None, cost=None):
    on_vmem = pl.BlockSpec(memory_space=pltpu.VMEM)
    spaces = {i: pltpu.SMEM for i in smem} | {i: pltpu.HBM for i in raw}

    def run(*args):
        return pl.pallas_call(
            body,
            out_shape=outs,
            in_specs=[pl.BlockSpec(memory_space=spaces.get(i, pltpu.VMEM)) for i in range(len(args))],
            out_specs=[on_vmem] * len(outs),
            scratch_shapes=list(scratch),
            compiler_params=pltpu.CompilerParams(vmem_limit_bytes=VMEM_LIMIT),
            cost_estimate=None if cost is None else pl.CostEstimate(*cost),
            name=name,
        )(*args)

    return run


def arr(shape, dtype=BF16):
    return jax.ShapeDtypeStruct(shape, dtype)


def vmem(shape, dtype=BF16):
    return pltpu.VMEM(shape, dtype)


def on_chip(*arrays):
    return [pltpu.with_memory_space_constraint(x, pltpu.VMEM) for x in arrays]


def in_hbm(*arrays):
    return [pltpu.with_memory_space_constraint(x, pltpu.HBM) for x in arrays]


def on_device(sizes, query, key, value, resid_in, out_grad, out_weight, conv_kernel, frame_lengths):
    heads_axis, z_count, group = sizes
    ctx_count = z_count * group
    rows = query.shape[1]
    width = query.shape[2]
    channels = resid_in.shape[2]
    block = rows * heads_axis
    supers = group * block
    members = group * heads_axis
    chips = members // 2
    half = rows // 2
    near = -(-REACH // group)
    window = REACH * block
    tiles = 2 * window // QT + 1
    per_block = block // QT
    lead = near * supers - window
    ext = (2 * near + 1) * supers
    out_cols = channels // heads_axis
    scale = HEAD_DIM ** (-0.5)

    def head_of(member):
        return group * (member % heads_axis) + member // heads_axis

    def cols(head):
        return slice(head * HEAD_DIM, (head + 1) * HEAD_DIM)

    def sides(core, slots):
        first, second = slots
        return jnp.where(core == 0, first, second), jnp.where(core == 0, second, first)

    def member_of(chip, core):
        return chip * 2 + core

    def my_chip():
        return lax.axis_index("y") * (heads_axis // 2) + lax.axis_index("head") // 2

    def my_core():
        return lax.axis_index("head") % 2

    slot = rows + half
    edge_rows = HALO + HALF

    def pack_body(q_hbm, k_hbm, v_hbm, resid_ref, grad_ref, taps_ref, *refs):
        keep_ref, send_ref, second_ref, resid_out, grad_out, taps_out, q_ref, k_ref, v_ref, sems = refs
        copies = [
            pltpu.make_async_copy(source, target, sems.at[i])
            for i, (source, target) in enumerate(
                (
                    (resid_ref, resid_out), (grad_ref, grad_out), (k_hbm, k_ref), (v_hbm, v_ref),
                    (q_hbm, q_ref), (taps_ref, taps_out),
                )
            )
        ]
        for copy in copies:
            copy.start()
        core = my_core()
        copies[0].wait()
        copies[1].wait()
        odd = core == 1
        resid_top, resid_low = resid_out[0, 0:HALO, :], resid_out[0, rows - HALO : rows, :]
        grad_top, grad_low = grad_out[0, 0:HALF, :], grad_out[0, rows - HALF : rows, :]
        second_ref[0:HALO, :] = jnp.where(odd, resid_low, resid_top)
        second_ref[HALO:edge_rows, :] = jnp.where(odd, grad_low, grad_top)
        resid_first = jnp.where(odd, resid_top, resid_low)
        grad_first = jnp.where(odd, grad_top, grad_low)
        for c in range(channels // LANES):
            at = chips * slot + c * edge_rows
            lane = slice(c * LANES, (c + 1) * LANES)
            send_ref[at : at + HALO, :] = resid_first[:, lane]
            send_ref[at + HALO : at + edge_rows, :] = grad_first[:, lane]
        for copy in copies[2:]:
            copy.wait()
        for chip in range(chips):
            heads = [cols(head_of(member_of(chip, c))) for c in (0, 1)]
            for at, width, c_ref, low, high in (
                (0, 0, k_ref, 0, rows),
                (0, HEAD_DIM, v_ref, 0, rows),
                (rows, 0, q_ref, 0, half),
                (rows, HEAD_DIM, q_ref, half, rows),
            ):
                stay, leave = sides(core, [c_ref[0, low:high, c] for c in heads])
                keep_ref[chip, at : at + high - low, width : width + HEAD_DIM] = stay
                at = at + chip * slot
                send_ref[at : at + high - low, width : width + HEAD_DIM] = leave

    raw = pl.BlockSpec(memory_space=pltpu.HBM)
    on_vmem = pl.BlockSpec(memory_space=pltpu.VMEM)
    pack_outs = [
        vmem((chips, slot, LANES)), vmem((chips * slot + edge_rows * channels // LANES, LANES)),
        vmem((edge_rows, channels)),
        vmem((1, rows, channels)), vmem((1, rows, channels)), vmem(conv_kernel.shape),
    ]
    keep, send, second, resid, upstream, taps_in = pl.pallas_call(
        pack_body,
        out_shape=pack_outs,
        in_specs=[raw] * 6,
        out_specs=[on_vmem] * 6,
        scratch_shapes=[pltpu.VMEM((1, rows, width), BF16)] * 3 + [pltpu.SemaphoreType.DMA((6,))],
        compiler_params=pltpu.CompilerParams(vmem_limit_bytes=VMEM_LIMIT),
        name="pack",
    )(*in_hbm(query, key, value, resid_in, out_grad, conv_kernel))

    mesh_axes = ("head", "z", "y")

    def place(head, z, y):
        return head * ctx_count + z * group + y

    def everyone(target):
        return [
            (place(h, z, y), place(*target(h, z, y)))
            for h in range(heads_axis)
            for z in range(z_count)
            for y in range(group)
        ]

    def core_swap(x):
        return lax.ppermute(x, mesh_axes, everyone(lambda h, z, y: (h ^ 1, z, y)))

    def step(x, d, phase):
        def target(h, z, y):
            partner = z + d if (z // d) % 2 == phase else z - d
            return (h, partner, y) if 0 <= partner < z_count else (h ^ 1, z, y)

        return lax.ppermute(x, mesh_axes, everyone(target))

    def slot_of(ref, i, like):
        size = like.shape[1]
        return ref[i] if len(ref.shape) == 3 else ref[pl.ds(pl.multiple_of(i * size, size), size), :]

    def exchange(keep, got, count, index, name):
        def body(keep_ref, got_ref, *out_refs):
            me = index()
            for m, out_ref in enumerate(out_refs, 1):
                out_ref[0] = keep_ref[me ^ m]
                out_ref[1] = slot_of(got_ref, me ^ m, keep_ref)

        per_row = heads_axis // 2

        def target(m):
            def f(h, z, y):
                chip = (y * per_row + h // 2) ^ m
                return (chip % per_row) * 2 + h % 2, z, chip // per_row

            return f

        parts = call(body, [vmem((2,) + keep.shape[1:])] * (count - 1), name=name)(*on_chip(keep, got))
        return [lax.ppermute(part, mesh_axes, everyone(target(m))) for m, part in enumerate(parts, 1)]

    def arrivals(me, core, keep_ref, got_ref, part_refs):
        out = [(member_of(me, core), lambda: keep_ref[me]), (member_of(me, 1 - core), lambda: slot_of(got_ref, me, keep_ref))]
        for m, ref in enumerate(part_refs, 1):
            out.append((member_of(me ^ m, core), lambda ref=ref: ref[0]))
            out.append((member_of(me ^ m, 1 - core), lambda ref=ref: ref[1]))
        return out

    got = core_swap(send)

    last_head = heads_axis - 1

    def inside(h, z, y):
        if 0 < h < last_head:
            return (h + 1 if h % 2 else h - 1), z, y
        return (h, z, 1 - y) if group == 2 else (last_head - h, z, y)

    outer = {}
    idle = []
    for ctx in range(ctx_count):
        for h in range(heads_axis):
            if h == last_head and ctx < ctx_count - 1:
                outer[h, ctx] = (0, ctx + 1)
                outer[0, ctx + 1] = (h, ctx)
            elif 0 < h < last_head or (h, ctx) in ((0, 0), (last_head, ctx_count - 1)):
                idle.append((h, ctx))
    def pair(one, two):
        outer[one], outer[two] = two, one

    pair((0, 0), (1, 0))
    pair((last_head, ctx_count - 1), (last_head - 1, ctx_count - 1))
    for h, ctx in idle:
        other = (h, ctx ^ group)
        if (h, ctx) not in outer and other in idle and other not in outer:
            pair((h, ctx), other)
    rest = [place for place in idle if place not in outer]
    for one, two in zip(rest[::2], rest[1::2]):
        pair(one, two)

    def outside(h, z, y):
        head, ctx = outer[h, z * group + y]
        return head, ctx // group, ctx % group

    halos = [
        lax.ppermute(second, mesh_axes, everyone(inside)),
        lax.ppermute(second, mesh_axes, everyone(outside)),
    ]
    span = rows + 2 * HALF

    part_chunks = channels // LANES * 6 // 8
    part_cols = part_chunks * LANES

    def conv_chunks(start, stop, resid_ref, grad_ref, core_ref, inside_ref, outside_ref, taps_ref, low_ref):
        head, ctx = lax.axis_index("head"), lax.axis_index("z") * group + lax.axis_index("y")
        odd = (head % 2) == 1
        edge = jnp.logical_or(head == 0, head == heads_axis - 1)
        starts = jnp.logical_and(head == 0, ctx == 0)
        ends = jnp.logical_and(head == heads_axis - 1, ctx == ctx_count - 1)

        def taps_sum(x, tap_of, length):
            total = None
            for b in range(8):
                part = None
                for a in range(4):
                    offset = 8 * a + b
                    if offset < 1 or offset > KERNEL:
                        continue
                    term = tap_of(offset - 1) * x[8 * a : 8 * a + length + 8]
                    part = term if part is None else part + term
                if b:
                    part = pltpu.roll(part, length + 8 - b, 0)
                part = part[0:length]
                total = part if total is None else total + part
            return total

        def chunk(c, carry):
            at = pl.multiple_of(c * LANES, LANES)
            lane = pl.ds(at, LANES)
            at = pl.multiple_of(chips * slot + c * edge_rows, HALF)
            first = core_ref[pl.ds(at, edge_rows), :].astype(F32)
            second = jnp.where(edge, outside_ref[:, lane].astype(F32), inside_ref[:, lane].astype(F32))
            before = jnp.where(starts, 0.0, jnp.where(odd, first, second))
            after = jnp.where(ends, 0.0, jnp.where(odd, second, first))
            taps = taps_ref[:, lane].astype(F32)
            x = jnp.concatenate([before[0:HALO], resid_ref[0, :, lane].astype(F32), after[0:HALO]], axis=0)
            middle = grad_ref[0, :, lane].astype(F32)
            g = jnp.concatenate([before[HALO:], middle, after[HALO:]], axis=0)
            pre = taps_sum(x, lambda k: taps[k : k + 1], span)
            s = 1.0 / (1.0 + jnp.exp(-pre))
            cg = g * (s * (1.0 + pre * (1.0 - s)))
            out = middle + taps_sum(cg, lambda k: taps[KERNEL - 1 - k : KERNEL - k], rows)
            low_ref[:, lane] = out.astype(BF16)
            return carry

        lax.fori_loop(start, stop, chunk, 0, unroll=2)

    def conv_first(*refs):
        conv_chunks(0, part_chunks, *refs)

    def conv_second(*refs):
        first_ref, weight_hbm, hg_keep, hg_send, dres_keep, dres_send, low_ref, weight_ref, sem = refs[6:]
        fetch = pltpu.make_async_copy(weight_hbm, weight_ref, sem)
        fetch.start()
        low_ref[:, 0:part_cols] = first_ref[...]
        conv_chunks(part_chunks, channels // LANES, *refs[:6], low_ref)
        core = my_core()
        for x in range(heads_axis // 2):
            dres_keep[x], dres_send[x] = sides(
                core, [low_ref[:, h * out_cols : (h + 1) * out_cols] for h in (2 * x, 2 * x + 1)]
            )
        fetch.wait()
        hg = dot(low_ref[...], weight_ref[...], NT_DIMS).astype(BF16)
        for chip in range(chips):
            heads = [cols(head_of(member_of(chip, c))) for c in (0, 1)]
            for at, part in ((0, slice(0, half)), (HEAD_DIM, slice(half, rows))):
                stay, leave = sides(core, [hg[part, c] for c in heads])
                hg_keep[chip, :, at : at + HEAD_DIM] = stay
                hg_send[chip, :, at : at + HEAD_DIM] = leave

    conv_in = (resid, upstream, got, *halos, taps_in)
    (conv_low,) = call(conv_first, [vmem((rows, part_cols))], name="conv", cost=CONV_COST)(*on_chip(*conv_in))
    mine = [keep, got] + exchange(keep, got, chips, my_chip, "regroup")

    def keys_body(keep_ref, got_ref, *refs):
        out_ref = refs[-1]
        for member, take in arrivals(my_chip(), my_core(), keep_ref, got_ref, refs[:-1]):
            out_ref[pl.ds(pl.multiple_of(member * rows, rows), rows), :] = take()[0:rows]

    *mine_here, _ = lax.optimization_barrier((*mine, conv_low))
    (both,) = call(keys_body, [vmem((supers, LANES))], name="keys")(*on_chip(*mine_here))

    steps = [(d, phase) for d in range(1, near + 1) for phase in (0, 1)]
    around = [step(both, d, phase) for d, phase in steps]

    conv_low, both_here = lax.optimization_barrier((conv_low, both))
    hg_keep, hg_send, dres_keep, dres_send = call(
        conv_second,
        [vmem((chips, half, LANES))] * 2 + [vmem((heads_axis // 2, rows, out_cols))] * 2,
        raw=(7,),
        scratch=[
            pltpu.VMEM((rows, channels), BF16),
            pltpu.VMEM(out_weight.shape, BF16),
            pltpu.SemaphoreType.DMA,
        ],
        name="conv_last",
        cost=CONV_COST,
    )(*on_chip(*conv_in, conv_low), *in_hbm(out_weight))
    hg_got = core_swap(hg_send)
    grads = [hg_keep, hg_got] + exchange(hg_keep, hg_got, chips, my_chip, "regroup_grads")
    q_tiles = supers // QT
    k_tiles = ext // QT
    first_tile = lead // QT
    own_tiles = range(near * q_tiles, (near + 1) * q_tiles)

    def seen(a):
        return range(a + first_tile, a + first_tile + tiles)

    def at_tile(t):
        return slice(t * QT, (t + 1) * QT)

    def score_body(*refs):
        len_ref, both_ref = refs[:2]
        mine_refs = refs[2 : 3 + chips]
        around_refs = refs[3 + chips : 3 + chips + 2 * near]
        e_ref, inv_ref, out_ref, kv, kt, qz, kb, qs, vt, s_sc = refs[3 + chips + 2 * near :]
        z = lax.axis_index("z")
        low = lax.broadcasted_iota(jnp.int32, (half, LANES), 1) < HEAD_DIM
        lane = lax.broadcasted_iota(jnp.int32, (half, LANES), 1)
        kv[near * supers : (near + 1) * supers, :] = both_ref[...]
        for member, take in arrivals(my_chip(), my_core(), mine_refs[0], mine_refs[1], mine_refs[2:]):
            q = take()[rows:slot].astype(F32) * scale
            for i, part in enumerate((q, pltpu.roll(q, HEAD_DIM, 1))):
                at = pl.ds(pl.multiple_of(member * rows + i * half, half), half)
                part = jnp.where(low, part, 0.0)
                qz[at, :] = part.astype(BF16)
                qs[at, :] = jnp.where(lane == HEAD_DIM, 1.0, part).astype(BF16)
        for d in range(1, near + 1):
            left, right = (near - d) * supers, (near + d) * supers
            odd = ((z // d) % 2) == 1

            @pl.when(odd)
            def _():
                kv[left : left + supers, :] = around_refs[2 * d - 2][...]
                kv[right : right + supers, :] = around_refs[2 * d - 1][...]

            @pl.when(jnp.logical_not(odd))
            def _():
                kv[left : left + supers, :] = around_refs[2 * d - 1][...]
                kv[right : right + supers, :] = around_refs[2 * d - 2][...]

        def limit(t):
            index = (z - near) * group + t // per_block
            inside = jnp.logical_and(index >= 0, index < ctx_count)
            length = len_ref[jnp.clip(index, 0, ctx_count - 1)]
            return jnp.where(inside, length, 0) - (t % per_block) * QT

        tile_lane = lax.broadcasted_iota(jnp.int32, (QT, LANES), 1)
        tile_row = lax.broadcasted_iota(jnp.int32, (QT, LANES), 0)

        for t in range(k_tiles):
            tile = kv[at_tile(t), :].astype(F32)
            turned = jnp.transpose(tile).astype(BF16)
            kt[:, at_tile(t)] = turned[0:HEAD_DIM]
            vt[0:HEAD_DIM, at_tile(t)] = turned[HEAD_DIM:LANES]
            dead = jnp.logical_and(tile_lane == HEAD_DIM, tile_row >= limit(t))
            kb[at_tile(t), :] = jnp.where(tile_lane < HEAD_DIM, tile, jnp.where(dead, NEG, 0.0)).astype(BF16)
        vt[HEAD_DIM:, :] = jnp.ones((ONES, ext), BF16)
        key_at = lax.broadcasted_iota(jnp.int32, (QT, QT), 0)
        query_at = lax.broadcasted_iota(jnp.int32, (QT, QT), 1)

        def scores(a, j, top):
            s = dot(kb[at_tile(a + j + first_tile), :], qs[at_tile(a), :], NT_DIMS)
            if j == 0:
                s = jnp.where(key_at >= query_at, s, NEG)
            if j == tiles - 1:
                s = jnp.where(key_at <= query_at, s, NEG)
            s_sc[a % 2, j] = s
            return jnp.maximum(top, jnp.max(s.reshape(QT // 8, 8, QT), axis=0))

        tops = [jnp.full((8, QT), NEG, F32) for _ in range(q_tiles)]
        for j in range(tiles):
            tops[0] = scores(0, j, tops[0])
        for a in range(q_tiles):
            top = jnp.max(tops[a], axis=0, keepdims=True)
            for j in range(tiles):
                if a + 1 < q_tiles:
                    tops[a + 1] = scores(a + 1, j, tops[a + 1])
                e = jnp.exp(s_sc[a % 2, j] - top)
                e_ref[a, at_tile(j), :] = e.astype(BF16)
            keys = slice((a + first_tile) * QT, (a + first_tile + tiles) * QT)
            out = dot(vt[:, keys], e_ref[a], NN_DIMS)
            inverse = 1.0 / out[HEAD_DIM : HEAD_DIM + 1]
            inv_ref[a] = inverse
            out_ref[a] = out[0:HEAD_DIM] * inverse

    exps, inverse, outs, kv, kt, qz = call(
        score_body,
        [
            vmem((q_tiles, tiles * QT, QT)),
            vmem((q_tiles, 1, QT), F32),
            vmem((q_tiles, HEAD_DIM, QT), F32),
            vmem((ext, LANES)),
            vmem((HEAD_DIM, ext)),
            vmem((supers, LANES)),
        ],
        smem=(0,),
        scratch=[
            pltpu.VMEM((ext, LANES), BF16),
            pltpu.VMEM((supers, LANES), BF16),
            pltpu.VMEM((HEAD_DIM + ONES, ext), BF16),
            pltpu.VMEM((2, tiles, QT, QT), F32),
        ],
        name="scores",
        cost=SCORES_COST,
    )(frame_lengths, *on_chip(both, *mine, *around))

    def key_tiles(a, ts, e_ref, inv_ref, delta_ref, kv, kt, qz, hz, acc, ds_sc, slopes_sc, base):
        q, g = qz[at_tile(a), :], hz[at_tile(a), :]
        keys = slice(ts[0] * QT, (ts[-1] + 1) * QT)
        slopes_sc[0 : len(ts) * QT, :] = dot(kv[keys, :], g, NT_DIMS)
        for i, t in enumerate(ts):
            p = e_ref[a, at_tile(t - a - first_tile), :].astype(F32) * inv_ref[a]
            ds = (p * (slopes_sc[at_tile(i), :] - delta_ref[a])).astype(BF16)
            ds_sc[at_tile(i), :] = ds
            part = dot(ds, q, NN_DIMS) + dot(p.astype(BF16), g, NN_DIMS)
            fresh = not any(t in seen(b) for b in range(a))
            acc[at_tile(t - base), :] = part if fresh else acc[at_tile(t - base), :] + part
        return dot(kt[:, keys], ds_sc[0 : len(ts) * QT, :], NN_DIMS)

    n_back = 2 * near

    def arrived(i, ref):
        d, phase = steps[i]
        z = lax.axis_index("z")
        partner = jnp.where((z // d) % 2 == phase, z + d, z - d)
        real = jnp.logical_and(partner >= 0, partner < z_count)
        return jnp.where(real, ref[...].astype(F32), 0.0)

    def far_call(i, first, ins):
        d, phase = steps[i]

        def body(*refs):
            if first:
                grad_refs = refs[: 1 + chips]
                e_ref, inv_ref, out_ref, kv, kt, qz, hz, delta_ref, dq, back_ref = refs[1 + chips : 11 + chips]
                low = lax.broadcasted_iota(jnp.int32, (half, LANES), 1) < HEAD_DIM
                for member, take in arrivals(my_chip(), my_core(), grad_refs[0], grad_refs[1], grad_refs[2:]):
                    g = take().astype(F32)
                    for k, piece in enumerate((pltpu.roll(g, HEAD_DIM, 1), g)):
                        at = pl.ds(pl.multiple_of(member * rows + k * half, half), half)
                        hz[at, :] = jnp.where(low, 0.0, piece).astype(BF16)
                for a in range(q_tiles):
                    g = jnp.transpose(hz[at_tile(a), :].astype(F32))[HEAD_DIM:LANES]
                    delta_ref[a] = jnp.sum(g * out_ref[a], axis=0, keepdims=True)
            else:
                e_ref, inv_ref, kv, kt, qz, hz, delta_ref, dq_in, dq, back_ref = refs[:10]
            acc, ds_sc, slopes_sc = refs[-3:]
            odd = ((lax.axis_index("z") // d) % 2) == 1
            right = odd if phase else jnp.logical_not(odd)

            def side(tiles_here):
                for t in tiles_here:
                    if not any(t in seen(a) for a in range(q_tiles)):
                        acc[at_tile(t - tiles_here[0]), :] = jnp.zeros((QT, LANES), F32)
                for a in range(q_tiles):
                    ts = [t for t in tiles_here if t in seen(a)]
                    total = jnp.zeros((HEAD_DIM, QT), F32) if first else dq_in[a]
                    if ts:
                        total = total + key_tiles(
                            a, ts, e_ref, inv_ref, delta_ref, kv, kt, qz, hz, acc,
                            ds_sc.at[a % 2], slopes_sc.at[a % 2], tiles_here[0],
                        )
                    dq[a] = total

            def tiles_at(distance):
                return range((near + distance) * q_tiles, (near + distance + 1) * q_tiles)

            @pl.when(right)
            def _():
                side(tiles_at(d))

            @pl.when(jnp.logical_not(right))
            def _():
                side(tiles_at(-d))

            back_ref[...] = acc[...].astype(BF16)

        ready = [vmem((supers, LANES)), vmem((q_tiles, 1, QT), F32)] if first else []
        return call(
            body,
            ready + [vmem((q_tiles, HEAD_DIM, QT), F32), vmem((supers, LANES))],
            scratch=[
                pltpu.VMEM((supers, LANES), F32),
                pltpu.VMEM((2, supers, QT), BF16),
                pltpu.VMEM((2, supers, QT), F32),
            ],
            name="far" if first else "far_next",
            cost=FAR_COST,
        )(*on_chip(*ins))

    hz, delta, dq_far, part_here = far_call(0, True, (*grads, exps, inverse, outs, kv, kt, qz))
    back = [step(part_here, *steps[0])]
    for i in range(1, n_back):
        dq_far, part_here = far_call(i, False, (exps, inverse, kv, kt, qz, hz, delta, dq_far))
        back.append(step(part_here, *steps[i]))

    hb = block // 2

    def near_body(*refs):
        e_ref, inv_ref, delta_ref, kv, kt, qz, hz, far_ref = refs[:8]
        acc, dq_ref = refs[8:10]
        dq_sc, ds_sc, slopes_sc = refs[-3:]
        for a in range(q_tiles):
            dq = far_ref[a] + key_tiles(
                a, own_tiles, e_ref, inv_ref, delta_ref, kv, kt, qz, hz, acc, ds_sc.at[a % 2], slopes_sc.at[a % 2],
                own_tiles[0],
            )
            dq_sc[at_tile(a), 0:HEAD_DIM] = jnp.transpose(dq * scale)
        if group == 1:
            dq_ref[0] = dq_sc[:, 0:HEAD_DIM].astype(BF16)
            return
        y = lax.axis_index("y")
        for ref, slot in ((dq_ref, y), (refs[10], 1 - y)):
            at = pl.multiple_of(slot * block, block)
            upper = dq_sc[pl.ds(at, hb), 0:HEAD_DIM]
            lower = dq_sc[pl.ds(pl.multiple_of(at + hb, hb), hb), 0:HEAD_DIM]
            ref[...] = jnp.concatenate([upper, lower], axis=1).astype(BF16)

    results = call(
        near_body,
        [vmem((supers, LANES), F32)]
        + ([arr((1, block, HEAD_DIM))] if group == 1 else [vmem((hb, LANES))] * 2),
        scratch=[
            pltpu.VMEM((supers, LANES), F32),
            pltpu.VMEM((2, supers, QT), BF16),
            pltpu.VMEM((2, supers, QT), F32),
        ],
        name="near",
        cost=NEAR_COST,
    )(*on_chip(exps, inverse, delta, kv, kt, qz, hz, dq_far))
    own, dq = results[:2]
    dres_got = core_swap(dres_send)
    dres_keep, dres_got, _ = lax.optimization_barrier((dres_keep, dres_got, results[0]))
    dres = [dres_keep, dres_got] + exchange(
        dres_keep, dres_got, heads_axis // 2, lambda: lax.axis_index("head") // 2, "regroup_resid"
    )

    def resid_body(*refs):
        for member, take in arrivals(lax.axis_index("head") // 2, my_core(), refs[0], refs[1], refs[2:-1]):
            refs[-1][0, pl.ds(pl.multiple_of(member * rows, rows), rows), :] = take()

    (d_resid,) = call(resid_body, [arr((1, block, out_cols))], name="resid", cost=RESID_COST)(*on_chip(*dres))

    if group == 1:

        def last_body(*refs):
            total = refs[0][...]
            for i in range(n_back):
                total = total + arrived(i, refs[1 + i])
            total = total.astype(BF16)
            refs[-2][0] = total[:, 0:HEAD_DIM]
            refs[-1][0] = total[:, HEAD_DIM:LANES]

        d_key, d_value = call(last_body, [arr((1, block, HEAD_DIM))] * 2, name="last")(*on_chip(own, *back))
        return d_resid, dq, d_key, d_value

    def y_swap(x):
        return lax.ppermute(x, mesh_axes, everyone(lambda h, z, y: (h, z, 1 - y)))

    def sum_body(own_ref, dq_send_ref, *refs):
        keep_ref, send_ref = refs[-2:]
        total = own_ref[...]
        for i in range(n_back):
            total = total + arrived(i, refs[i])
        total = total.astype(BF16)
        first = lax.axis_index("y") == 0
        keep_ref[...] = jnp.where(first, total[0:block], total[block:supers])
        send_ref[0:block, :] = jnp.where(first, total[block:supers], total[0:block])
        send_ref[block:, :] = dq_send_ref[...]

    keep, send = call(sum_body, [vmem((block, LANES)), vmem((block + hb, LANES))], name="sum")(
        *on_chip(own, results[2], *back)
    )
    other = y_swap(send)

    def last_body(*refs):
        keep_ref, other_ref, dq_keep_ref = refs[:3]
        dq_ref, dk_ref, dv_ref = refs[-3:]
        first = lax.axis_index("y") == 0
        low = lax.broadcasted_iota(jnp.int32, (block, LANES), 1) < HEAD_DIM

        def ordered(mine, peer):
            mine, peer = mine.astype(F32), peer.astype(F32)
            return jnp.where(first, mine, peer), jnp.where(first, peer, mine)

        lo, up = ordered(keep_ref[...], other_ref[0:block, :])
        dk_ref[0] = jnp.where(low, lo, pltpu.roll(up, HEAD_DIM, 1)).astype(BF16)
        dv_ref[0] = jnp.where(low, pltpu.roll(lo, HEAD_DIM, 1), up).astype(BF16)
        lo, up = ordered(dq_keep_ref[...], other_ref[block:, :])
        low = low[0:hb]
        dq_ref[0, 0:hb, :] = jnp.where(low, lo, pltpu.roll(up, HEAD_DIM, 1)).astype(BF16)
        dq_ref[0, hb:block, :] = jnp.where(low, pltpu.roll(lo, HEAD_DIM, 1), up).astype(BF16)

    d_query, d_key, d_value = call(last_body, [arr((1, block, LANES))] * 3, name="last")(
        *on_chip(keep, other, dq)
    )
    return d_resid, d_query, d_key, d_value


def solution(mesh):
    heads_axis = mesh.shape["head"]
    ctx_count = mesh.shape["ctx"]

    def run(query, *rest):
        group = query.shape[2] // HEAD_DIM // heads_axis
        z_count = ctx_count // group
        fine = Mesh(mesh.devices.reshape(heads_axis, z_count, group), ("head", "z", "y"))
        rows_spec = P(("z", "y"), "head", None)
        cols_spec = P(("z", "y"), None, "head")
        sizes = (heads_axis, z_count, group)
        return jax.shard_map(
            lambda *args: on_device(sizes, *args),
            mesh=fine,
            in_specs=(rows_spec,) * 5 + (P(),) * 3,
            out_specs=(cols_spec,) * 4,
            check_vma=False,
        )(query, *rest)

    return run
```

```python
import jax
import jax.numpy as jnp
from jax import lax
from jax.experimental import pallas as pl
from jax.experimental.pallas import tpu as pltpu
from jax.sharding import Mesh
from jax.sharding import PartitionSpec as P

HEAD_DIM = 64
KERNEL = 31
REACH = 2
LANES = 128
QT = 256
HALO = 32
HALF = 16
NEG = -1e30
ONES = 16
F32 = jnp.float32
BF16 = jnp.bfloat16
NT_DIMS = (((1,), (1,)), ((), ()))
NN_DIMS = (((1,), (0,)), ((), ()))
VMEM_LIMIT = 12 * 1024 * 1024
CONV_COST = (3_000_000_000, 0, 0)
SCORES_COST = (9_000_000_000, 0, 0)
FAR_COST = (2_000_000_000, 0, 0)
NEAR_COST = (4_000_000_000, 0, 0)
RESID_COST = (1_000_000_000, 0, 0)


def dot(a, b, dims):
    return lax.dot_general(a, b, dims, preferred_element_type=F32)


def call(body, outs, smem=(), raw=(), scratch=(), name=None, cost=None):
    on_vmem = pl.BlockSpec(memory_space=pltpu.VMEM)
    spaces = {i: pltpu.SMEM for i in smem} | {i: pltpu.HBM for i in raw}

    def run(*args):
        return pl.pallas_call(
            body,
            out_shape=outs,
            in_specs=[pl.BlockSpec(memory_space=spaces.get(i, pltpu.VMEM)) for i in range(len(args))],
            out_specs=[on_vmem] * len(outs),
            scratch_shapes=list(scratch),
            compiler_params=pltpu.CompilerParams(vmem_limit_bytes=VMEM_LIMIT),
            cost_estimate=None if cost is None else pl.CostEstimate(*cost),
            name=name,
        )(*args)

    return run


def arr(shape, dtype=BF16):
    return jax.ShapeDtypeStruct(shape, dtype)


def vmem(shape, dtype=BF16):
    return pltpu.VMEM(shape, dtype)


def on_chip(*arrays):
    return [pltpu.with_memory_space_constraint(x, pltpu.VMEM) for x in arrays]


def in_hbm(*arrays):
    return [pltpu.with_memory_space_constraint(x, pltpu.HBM) for x in arrays]


def on_device(sizes, query, key, value, resid_in, out_grad, out_weight, conv_kernel, frame_lengths):
    heads_axis, z_count, group = sizes
    ctx_count = z_count * group
    rows = query.shape[1]
    width = query.shape[2]
    channels = resid_in.shape[2]
    block = rows * heads_axis
    supers = group * block
    members = group * heads_axis
    chips = members // 2
    half = rows // 2
    near = -(-REACH // group)
    window = REACH * block
    tiles = 2 * window // QT + 1
    per_block = block // QT
    lead = near * supers - window
    ext = (2 * near + 1) * supers
    out_cols = channels // heads_axis
    scale = HEAD_DIM ** (-0.5)

    def head_of(member):
        return group * (member % heads_axis) + member // heads_axis

    def cols(head):
        return slice(head * HEAD_DIM, (head + 1) * HEAD_DIM)

    def sides(core, slots):
        first, second = slots
        return jnp.where(core == 0, first, second), jnp.where(core == 0, second, first)

    def member_of(chip, core):
        return chip * 2 + core

    def my_chip():
        return lax.axis_index("y") * (heads_axis // 2) + lax.axis_index("head") // 2

    def my_core():
        return lax.axis_index("head") % 2

    slot = rows + half
    edge_rows = HALO + HALF

    def pack_body(q_hbm, k_hbm, v_hbm, resid_ref, grad_ref, taps_ref, *refs):
        keep_ref, send_ref, second_ref, resid_out, grad_out, taps_out, q_ref, k_ref, v_ref, sems = refs
        copies = [
            pltpu.make_async_copy(source, target, sems.at[i])
            for i, (source, target) in enumerate(
                (
                    (resid_ref, resid_out), (grad_ref, grad_out), (k_hbm, k_ref), (v_hbm, v_ref),
                    (q_hbm, q_ref), (taps_ref, taps_out),
                )
            )
        ]
        for copy in copies:
            copy.start()
        core = my_core()
        copies[0].wait()
        copies[1].wait()
        odd = core == 1
        resid_top, resid_low = resid_out[0, 0:HALO, :], resid_out[0, rows - HALO : rows, :]
        grad_top, grad_low = grad_out[0, 0:HALF, :], grad_out[0, rows - HALF : rows, :]
        second_ref[0:HALO, :] = jnp.where(odd, resid_low, resid_top)
        second_ref[HALO:edge_rows, :] = jnp.where(odd, grad_low, grad_top)
        resid_first = jnp.where(odd, resid_top, resid_low)
        grad_first = jnp.where(odd, grad_top, grad_low)
        for c in range(channels // LANES):
            at = chips * slot + c * edge_rows
            lane = slice(c * LANES, (c + 1) * LANES)
            send_ref[at : at + HALO, :] = resid_first[:, lane]
            send_ref[at + HALO : at + edge_rows, :] = grad_first[:, lane]
        for copy in copies[2:]:
            copy.wait()
        for chip in range(chips):
            heads = [cols(head_of(member_of(chip, c))) for c in (0, 1)]
            for at, width, c_ref, low, high in (
                (0, 0, k_ref, 0, rows),
                (0, HEAD_DIM, v_ref, 0, rows),
                (rows, 0, q_ref, 0, half),
                (rows, HEAD_DIM, q_ref, half, rows),
            ):
                stay, leave = sides(core, [c_ref[0, low:high, c] for c in heads])
                keep_ref[chip, at : at + high - low, width : width + HEAD_DIM] = stay
                at = at + chip * slot
                send_ref[at : at + high - low, width : width + HEAD_DIM] = leave

    raw = pl.BlockSpec(memory_space=pltpu.HBM)
    on_vmem = pl.BlockSpec(memory_space=pltpu.VMEM)
    pack_outs = [
        vmem((chips, slot, LANES)), vmem((chips * slot + edge_rows * channels // LANES, LANES)),
        vmem((edge_rows, channels)),
        vmem((1, rows, channels)), vmem((1, rows, channels)), vmem(conv_kernel.shape),
    ]
    keep, send, second, resid, upstream, taps_in = pl.pallas_call(
        pack_body,
        out_shape=pack_outs,
        in_specs=[raw] * 6,
        out_specs=[on_vmem] * 6,
        scratch_shapes=[pltpu.VMEM((1, rows, width), BF16)] * 3 + [pltpu.SemaphoreType.DMA((6,))],
        compiler_params=pltpu.CompilerParams(vmem_limit_bytes=VMEM_LIMIT),
        name="pack",
    )(*in_hbm(query, key, value, resid_in, out_grad, conv_kernel))

    mesh_axes = ("head", "z", "y")

    def place(head, z, y):
        return head * ctx_count + z * group + y

    def everyone(target):
        return [
            (place(h, z, y), place(*target(h, z, y)))
            for h in range(heads_axis)
            for z in range(z_count)
            for y in range(group)
        ]

    def core_swap(x):
        return lax.ppermute(x, mesh_axes, everyone(lambda h, z, y: (h ^ 1, z, y)))

    def step(x, d, phase):
        def target(h, z, y):
            partner = z + d if (z // d) % 2 == phase else z - d
            return (h, partner, y) if 0 <= partner < z_count else (h ^ 1, z, y)

        return lax.ppermute(x, mesh_axes, everyone(target))

    def slot_of(ref, i, like):
        size = like.shape[1]
        return ref[i] if len(ref.shape) == 3 else ref[pl.ds(pl.multiple_of(i * size, size), size), :]

    def exchange(keep, got, count, index, name):
        def body(keep_ref, got_ref, *out_refs):
            me = index()
            for m, out_ref in enumerate(out_refs, 1):
                out_ref[0] = keep_ref[me ^ m]
                out_ref[1] = slot_of(got_ref, me ^ m, keep_ref)

        per_row = heads_axis // 2

        def target(m):
            def f(h, z, y):
                chip = (y * per_row + h // 2) ^ m
                return (chip % per_row) * 2 + h % 2, z, chip // per_row

            return f

        parts = call(body, [vmem((2,) + keep.shape[1:])] * (count - 1), name=name)(*on_chip(keep, got))
        return [lax.ppermute(part, mesh_axes, everyone(target(m))) for m, part in enumerate(parts, 1)]

    def arrivals(me, core, keep_ref, got_ref, part_refs):
        out = [(member_of(me, core), lambda: keep_ref[me]), (member_of(me, 1 - core), lambda: slot_of(got_ref, me, keep_ref))]
        for m, ref in enumerate(part_refs, 1):
            out.append((member_of(me ^ m, core), lambda ref=ref: ref[0]))
            out.append((member_of(me ^ m, 1 - core), lambda ref=ref: ref[1]))
        return out

    got = core_swap(send)

    last_head = heads_axis - 1

    def inside(h, z, y):
        if 0 < h < last_head:
            return (h + 1 if h % 2 else h - 1), z, y
        return (h, z, 1 - y) if group == 2 else (last_head - h, z, y)

    outer = {}
    idle = []
    for ctx in range(ctx_count):
        for h in range(heads_axis):
            if h == last_head and ctx < ctx_count - 1:
                outer[h, ctx] = (0, ctx + 1)
                outer[0, ctx + 1] = (h, ctx)
            elif 0 < h < last_head or (h, ctx) in ((0, 0), (last_head, ctx_count - 1)):
                idle.append((h, ctx))
    def pair(one, two):
        outer[one], outer[two] = two, one

    pair((0, 0), (1, 0))
    pair((last_head, ctx_count - 1), (last_head - 1, ctx_count - 1))
    for h, ctx in idle:
        other = (h, ctx ^ group)
        if (h, ctx) not in outer and other in idle and other not in outer:
            pair((h, ctx), other)
    rest = [place for place in idle if place not in outer]
    for one, two in zip(rest[::2], rest[1::2]):
        pair(one, two)

    def outside(h, z, y):
        head, ctx = outer[h, z * group + y]
        return head, ctx // group, ctx % group

    halos = [
        lax.ppermute(second, mesh_axes, everyone(inside)),
        lax.ppermute(second, mesh_axes, everyone(outside)),
    ]
    span = rows + 2 * HALF

    part_chunks = channels // LANES * 6 // 8
    part_cols = part_chunks * LANES

    def conv_chunks(start, stop, resid_ref, grad_ref, core_ref, inside_ref, outside_ref, taps_ref, low_ref):
        head, ctx = lax.axis_index("head"), lax.axis_index("z") * group + lax.axis_index("y")
        odd = (head % 2) == 1
        edge = jnp.logical_or(head == 0, head == heads_axis - 1)
        starts = jnp.logical_and(head == 0, ctx == 0)
        ends = jnp.logical_and(head == heads_axis - 1, ctx == ctx_count - 1)

        def taps_sum(x, tap_of, length):
            total = None
            for b in range(8):
                part = None
                for a in range(4):
                    offset = 8 * a + b
                    if offset < 1 or offset > KERNEL:
                        continue
                    term = tap_of(offset - 1) * x[8 * a : 8 * a + length + 8]
                    part = term if part is None else part + term
                if b:
                    part = pltpu.roll(part, length + 8 - b, 0)
                part = part[0:length]
                total = part if total is None else total + part
            return total

        def chunk(c, carry):
            at = pl.multiple_of(c * LANES, LANES)
            lane = pl.ds(at, LANES)
            at = pl.multiple_of(chips * slot + c * edge_rows, HALF)
            first = core_ref[pl.ds(at, edge_rows), :].astype(F32)
            second = jnp.where(edge, outside_ref[:, lane].astype(F32), inside_ref[:, lane].astype(F32))
            before = jnp.where(starts, 0.0, jnp.where(odd, first, second))
            after = jnp.where(ends, 0.0, jnp.where(odd, second, first))
            taps = taps_ref[:, lane].astype(F32)
            x = jnp.concatenate([before[0:HALO], resid_ref[0, :, lane].astype(F32), after[0:HALO]], axis=0)
            middle = grad_ref[0, :, lane].astype(F32)
            g = jnp.concatenate([before[HALO:], middle, after[HALO:]], axis=0)
            pre = taps_sum(x, lambda k: taps[k : k + 1], span)
            s = 1.0 / (1.0 + jnp.exp(-pre))
            cg = g * (s * (1.0 + pre * (1.0 - s)))
            out = middle + taps_sum(cg, lambda k: taps[KERNEL - 1 - k : KERNEL - k], rows)
            low_ref[:, lane] = out.astype(BF16)
            return carry

        lax.fori_loop(start, stop, chunk, 0, unroll=2)

    def conv_first(*refs):
        conv_chunks(0, part_chunks, *refs)

    def conv_second(*refs):
        first_ref, weight_hbm, hg_keep, hg_send, dres_keep, dres_send, low_ref, weight_ref, sem = refs[6:]
        fetch = pltpu.make_async_copy(weight_hbm, weight_ref, sem)
        fetch.start()
        low_ref[:, 0:part_cols] = first_ref[...]
        conv_chunks(part_chunks, channels // LANES, *refs[:6], low_ref)
        core = my_core()
        for x in range(heads_axis // 2):
            dres_keep[x], dres_send[x] = sides(
                core, [low_ref[:, h * out_cols : (h + 1) * out_cols] for h in (2 * x, 2 * x + 1)]
            )
        fetch.wait()
        hg = dot(low_ref[...], weight_ref[...], NT_DIMS).astype(BF16)
        for chip in range(chips):
            heads = [cols(head_of(member_of(chip, c))) for c in (0, 1)]
            for at, part in ((0, slice(0, half)), (HEAD_DIM, slice(half, rows))):
                stay, leave = sides(core, [hg[part, c] for c in heads])
                hg_keep[chip, :, at : at + HEAD_DIM] = stay
                hg_send[chip, :, at : at + HEAD_DIM] = leave

    conv_in = (resid, upstream, got, *halos, taps_in)
    (conv_low,) = call(conv_first, [vmem((rows, part_cols))], name="conv", cost=CONV_COST)(*on_chip(*conv_in))
    mine = [keep, got] + exchange(keep, got, chips, my_chip, "regroup")

    def keys_body(keep_ref, got_ref, *refs):
        out_ref = refs[-1]
        for member, take in arrivals(my_chip(), my_core(), keep_ref, got_ref, refs[:-1]):
            out_ref[pl.ds(pl.multiple_of(member * rows, rows), rows), :] = take()[0:rows]

    *mine_here, _ = lax.optimization_barrier((*mine, conv_low))
    (both,) = call(keys_body, [vmem((supers, LANES))], name="keys")(*on_chip(*mine_here))

    steps = [(d, phase) for d in range(1, near + 1) for phase in (0, 1)]
    around = [step(both, d, phase) for d, phase in steps]

    conv_low, both_here = lax.optimization_barrier((conv_low, both))
    hg_keep, hg_send, dres_keep, dres_send = call(
        conv_second,
        [vmem((chips, half, LANES))] * 2 + [vmem((heads_axis // 2, rows, out_cols))] * 2,
        raw=(7,),
        scratch=[
            pltpu.VMEM((rows, channels), BF16),
            pltpu.VMEM(out_weight.shape, BF16),
            pltpu.SemaphoreType.DMA,
        ],
        name="conv_last",
        cost=CONV_COST,
    )(*on_chip(*conv_in, conv_low), *in_hbm(out_weight))
    hg_got = core_swap(hg_send)
    grads = [hg_keep, hg_got] + exchange(hg_keep, hg_got, chips, my_chip, "regroup_grads")
    q_tiles = supers // QT
    k_tiles = ext // QT
    first_tile = lead // QT
    own_tiles = range(near * q_tiles, (near + 1) * q_tiles)

    def seen(a):
        return range(a + first_tile, a + first_tile + tiles)

    def at_tile(t):
        return slice(t * QT, (t + 1) * QT)

    def score_body(*refs):
        len_ref, both_ref = refs[:2]
        mine_refs = refs[2 : 3 + chips]
        around_refs = refs[3 + chips : 3 + chips + 2 * near]
        e_ref, inv_ref, out_ref, kv, kt, qz, kb, qs, vt, s_sc = refs[3 + chips + 2 * near :]
        z = lax.axis_index("z")
        low = lax.broadcasted_iota(jnp.int32, (half, LANES), 1) < HEAD_DIM
        lane = lax.broadcasted_iota(jnp.int32, (half, LANES), 1)
        kv[near * supers : (near + 1) * supers, :] = both_ref[...]
        for member, take in arrivals(my_chip(), my_core(), mine_refs[0], mine_refs[1], mine_refs[2:]):
            q = take()[rows:slot].astype(F32) * scale
            for i, part in enumerate((q, pltpu.roll(q, HEAD_DIM, 1))):
                at = pl.ds(pl.multiple_of(member * rows + i * half, half), half)
                part = jnp.where(low, part, 0.0)
                qz[at, :] = part.astype(BF16)
                qs[at, :] = jnp.where(lane == HEAD_DIM, 1.0, part).astype(BF16)
        for d in range(1, near + 1):
            left, right = (near - d) * supers, (near + d) * supers
            odd = ((z // d) % 2) == 1

            @pl.when(odd)
            def _():
                kv[left : left + supers, :] = around_refs[2 * d - 2][...]
                kv[right : right + supers, :] = around_refs[2 * d - 1][...]

            @pl.when(jnp.logical_not(odd))
            def _():
                kv[left : left + supers, :] = around_refs[2 * d - 1][...]
                kv[right : right + supers, :] = around_refs[2 * d - 2][...]

        def limit(t):
            index = (z - near) * group + t // per_block
            inside = jnp.logical_and(index >= 0, index < ctx_count)
            length = len_ref[jnp.clip(index, 0, ctx_count - 1)]
            return jnp.where(inside, length, 0) - (t % per_block) * QT

        tile_lane = lax.broadcasted_iota(jnp.int32, (QT, LANES), 1)
        tile_row = lax.broadcasted_iota(jnp.int32, (QT, LANES), 0)

        for t in range(k_tiles):
            tile = kv[at_tile(t), :].astype(F32)
            turned = jnp.transpose(tile).astype(BF16)
            kt[:, at_tile(t)] = turned[0:HEAD_DIM]
            vt[0:HEAD_DIM, at_tile(t)] = turned[HEAD_DIM:LANES]
            dead = jnp.logical_and(tile_lane == HEAD_DIM, tile_row >= limit(t))
            kb[at_tile(t), :] = jnp.where(tile_lane < HEAD_DIM, tile, jnp.where(dead, NEG, 0.0)).astype(BF16)
        vt[HEAD_DIM:, :] = jnp.ones((ONES, ext), BF16)
        key_at = lax.broadcasted_iota(jnp.int32, (QT, QT), 0)
        query_at = lax.broadcasted_iota(jnp.int32, (QT, QT), 1)

        def scores(a, j, top):
            s = dot(kb[at_tile(a + j + first_tile), :], qs[at_tile(a), :], NT_DIMS)
            if j == 0:
                s = jnp.where(key_at >= query_at, s, NEG)
            if j == tiles - 1:
                s = jnp.where(key_at <= query_at, s, NEG)
            s_sc[a % 2, j] = s
            return jnp.maximum(top, jnp.max(s.reshape(QT // 8, 8, QT), axis=0))

        tops = [jnp.full((8, QT), NEG, F32) for _ in range(q_tiles)]
        for j in range(tiles):
            tops[0] = scores(0, j, tops[0])
        for a in range(q_tiles):
            top = jnp.max(tops[a], axis=0, keepdims=True)
            for j in range(tiles):
                if a + 1 < q_tiles:
                    tops[a + 1] = scores(a + 1, j, tops[a + 1])
                e = jnp.exp(s_sc[a % 2, j] - top)
                e_ref[a, at_tile(j), :] = e.astype(BF16)
            keys = slice((a + first_tile) * QT, (a + first_tile + tiles) * QT)
            out = dot(vt[:, keys], e_ref[a], NN_DIMS)
            inverse = 1.0 / out[HEAD_DIM : HEAD_DIM + 1]
            inv_ref[a] = inverse
            out_ref[a] = out[0:HEAD_DIM] * inverse

    exps, inverse, outs, kv, kt, qz = call(
        score_body,
        [
            vmem((q_tiles, tiles * QT, QT)),
            vmem((q_tiles, 1, QT), F32),
            vmem((q_tiles, HEAD_DIM, QT), F32),
            vmem((ext, LANES)),
            vmem((HEAD_DIM, ext)),
            vmem((supers, LANES)),
        ],
        smem=(0,),
        scratch=[
            pltpu.VMEM((ext, LANES), BF16),
            pltpu.VMEM((supers, LANES), BF16),
            pltpu.VMEM((HEAD_DIM + ONES, ext), BF16),
            pltpu.VMEM((2, tiles, QT, QT), F32),
        ],
        name="scores",
        cost=SCORES_COST,
    )(frame_lengths, *on_chip(both, *mine, *around))

    def key_tiles(a, ts, e_ref, inv_ref, delta_ref, kv, kt, qz, hz, acc, ds_sc, slopes_sc, base):
        q, g = qz[at_tile(a), :], hz[at_tile(a), :]
        keys = slice(ts[0] * QT, (ts[-1] + 1) * QT)
        slopes_sc[0 : len(ts) * QT, :] = dot(kv[keys, :], g, NT_DIMS)
        for i, t in enumerate(ts):
            p = e_ref[a, at_tile(t - a - first_tile), :].astype(F32) * inv_ref[a]
            ds = (p * (slopes_sc[at_tile(i), :] - delta_ref[a])).astype(BF16)
            ds_sc[at_tile(i), :] = ds
            part = dot(ds, q, NN_DIMS) + dot(p.astype(BF16), g, NN_DIMS)
            fresh = not any(t in seen(b) for b in range(a))
            acc[at_tile(t - base), :] = part if fresh else acc[at_tile(t - base), :] + part
        return dot(kt[:, keys], ds_sc[0 : len(ts) * QT, :], NN_DIMS)

    n_back = 2 * near

    def arrived(i, ref):
        d, phase = steps[i]
        z = lax.axis_index("z")
        partner = jnp.where((z // d) % 2 == phase, z + d, z - d)
        real = jnp.logical_and(partner >= 0, partner < z_count)
        return jnp.where(real, ref[...].astype(F32), 0.0)

    def far_call(i, first, ins):
        d, phase = steps[i]

        def body(*refs):
            if first:
                grad_refs = refs[: 1 + chips]
                e_ref, inv_ref, out_ref, kv, kt, qz, hz, delta_ref, dq, back_ref = refs[1 + chips : 11 + chips]
                low = lax.broadcasted_iota(jnp.int32, (half, LANES), 1) < HEAD_DIM
                for member, take in arrivals(my_chip(), my_core(), grad_refs[0], grad_refs[1], grad_refs[2:]):
                    g = take().astype(F32)
                    for k, piece in enumerate((pltpu.roll(g, HEAD_DIM, 1), g)):
                        at = pl.ds(pl.multiple_of(member * rows + k * half, half), half)
                        hz[at, :] = jnp.where(low, 0.0, piece).astype(BF16)
                for a in range(q_tiles):
                    g = jnp.transpose(hz[at_tile(a), :].astype(F32))[HEAD_DIM:LANES]
                    delta_ref[a] = jnp.sum(g * out_ref[a], axis=0, keepdims=True)
            else:
                e_ref, inv_ref, kv, kt, qz, hz, delta_ref, dq_in, dq, back_ref = refs[:10]
            acc, ds_sc, slopes_sc = refs[-3:]
            odd = ((lax.axis_index("z") // d) % 2) == 1
            right = odd if phase else jnp.logical_not(odd)

            def side(tiles_here):
                for t in tiles_here:
                    if not any(t in seen(a) for a in range(q_tiles)):
                        acc[at_tile(t - tiles_here[0]), :] = jnp.zeros((QT, LANES), F32)
                for a in range(q_tiles):
                    ts = [t for t in tiles_here if t in seen(a)]
                    total = jnp.zeros((HEAD_DIM, QT), F32) if first else dq_in[a]
                    if ts:
                        total = total + key_tiles(
                            a, ts, e_ref, inv_ref, delta_ref, kv, kt, qz, hz, acc,
                            ds_sc.at[a % 2], slopes_sc.at[a % 2], tiles_here[0],
                        )
                    dq[a] = total

            def tiles_at(distance):
                return range((near + distance) * q_tiles, (near + distance + 1) * q_tiles)

            z = lax.axis_index("z")
            partner = jnp.where(right, z + d, z - d)
            real = jnp.logical_and(partner >= 0, partner < z_count)

            @pl.when(jnp.logical_and(real, right))
            def _():
                side(tiles_at(d))

            @pl.when(jnp.logical_and(real, jnp.logical_not(right)))
            def _():
                side(tiles_at(-d))

            @pl.when(jnp.logical_not(real))
            def _():
                acc[...] = jnp.zeros_like(acc)
                dq[...] = jnp.zeros_like(dq) if first else dq_in[...]

            back_ref[...] = acc[...].astype(BF16)

        ready = [vmem((supers, LANES)), vmem((q_tiles, 1, QT), F32)] if first else []
        return call(
            body,
            ready + [vmem((q_tiles, HEAD_DIM, QT), F32), vmem((supers, LANES))],
            scratch=[
                pltpu.VMEM((supers, LANES), F32),
                pltpu.VMEM((2, supers, QT), BF16),
                pltpu.VMEM((2, supers, QT), F32),
            ],
            name="far" if first else "far_next",
            cost=FAR_COST,
        )(*on_chip(*ins))

    hz, delta, dq_far, part_here = far_call(0, True, (*grads, exps, inverse, outs, kv, kt, qz))
    back = [step(part_here, *steps[0])]
    for i in range(1, n_back):
        dq_far, part_here = far_call(i, False, (exps, inverse, kv, kt, qz, hz, delta, dq_far))
        back.append(step(part_here, *steps[i]))

    hb = block // 2

    def near_body(*refs):
        e_ref, inv_ref, delta_ref, kv, kt, qz, hz, far_ref = refs[:8]
        acc, dq_ref = refs[8:10]
        dq_sc, ds_sc, slopes_sc = refs[-3:]
        for a in range(q_tiles):
            dq = far_ref[a] + key_tiles(
                a, own_tiles, e_ref, inv_ref, delta_ref, kv, kt, qz, hz, acc, ds_sc.at[a % 2], slopes_sc.at[a % 2],
                own_tiles[0],
            )
            dq_sc[at_tile(a), 0:HEAD_DIM] = jnp.transpose(dq * scale)
        if group == 1:
            dq_ref[0] = dq_sc[:, 0:HEAD_DIM].astype(BF16)
            return
        y = lax.axis_index("y")
        for ref, slot in ((dq_ref, y), (refs[10], 1 - y)):
            at = pl.multiple_of(slot * block, block)
            upper = dq_sc[pl.ds(at, hb), 0:HEAD_DIM]
            lower = dq_sc[pl.ds(pl.multiple_of(at + hb, hb), hb), 0:HEAD_DIM]
            ref[...] = jnp.concatenate([upper, lower], axis=1).astype(BF16)

    results = call(
        near_body,
        [vmem((supers, LANES), F32)]
        + ([arr((1, block, HEAD_DIM))] if group == 1 else [vmem((hb, LANES))] * 2),
        scratch=[
            pltpu.VMEM((supers, LANES), F32),
            pltpu.VMEM((2, supers, QT), BF16),
            pltpu.VMEM((2, supers, QT), F32),
        ],
        name="near",
        cost=NEAR_COST,
    )(*on_chip(exps, inverse, delta, kv, kt, qz, hz, dq_far))
    own, dq = results[:2]
    dres_got = core_swap(dres_send)
    dres_keep, dres_got, _ = lax.optimization_barrier((dres_keep, dres_got, results[0]))
    dres = [dres_keep, dres_got] + exchange(
        dres_keep, dres_got, heads_axis // 2, lambda: lax.axis_index("head") // 2, "regroup_resid"
    )

    def resid_body(*refs):
        for member, take in arrivals(lax.axis_index("head") // 2, my_core(), refs[0], refs[1], refs[2:-1]):
            refs[-1][0, pl.ds(pl.multiple_of(member * rows, rows), rows), :] = take()

    (d_resid,) = call(resid_body, [arr((1, block, out_cols))], name="resid", cost=RESID_COST)(*on_chip(*dres))

    if group == 1:

        def last_body(*refs):
            total = refs[0][...]
            for i in range(n_back):
                total = total + arrived(i, refs[1 + i])
            total = total.astype(BF16)
            refs[-2][0] = total[:, 0:HEAD_DIM]
            refs[-1][0] = total[:, HEAD_DIM:LANES]

        d_key, d_value = call(last_body, [arr((1, block, HEAD_DIM))] * 2, name="last")(*on_chip(own, *back))
        return d_resid, dq, d_key, d_value

    def y_swap(x):
        return lax.ppermute(x, mesh_axes, everyone(lambda h, z, y: (h, z, 1 - y)))

    def sum_body(own_ref, dq_send_ref, *refs):
        keep_ref, send_ref = refs[-2:]
        total = own_ref[...]
        for i in range(n_back):
            total = total + arrived(i, refs[i])
        total = total.astype(BF16)
        first = lax.axis_index("y") == 0
        keep_ref[...] = jnp.where(first, total[0:block], total[block:supers])
        send_ref[0:block, :] = jnp.where(first, total[block:supers], total[0:block])
        send_ref[block:, :] = dq_send_ref[...]

    keep, send = call(sum_body, [vmem((block, LANES)), vmem((block + hb, LANES))], name="sum")(
        *on_chip(own, results[2], *back)
    )
    other = y_swap(send)

    def last_body(*refs):
        keep_ref, other_ref, dq_keep_ref = refs[:3]
        dq_ref, dk_ref, dv_ref = refs[-3:]
        first = lax.axis_index("y") == 0
        low = lax.broadcasted_iota(jnp.int32, (block, LANES), 1) < HEAD_DIM

        def ordered(mine, peer):
            mine, peer = mine.astype(F32), peer.astype(F32)
            return jnp.where(first, mine, peer), jnp.where(first, peer, mine)

        lo, up = ordered(keep_ref[...], other_ref[0:block, :])
        dk_ref[0] = jnp.where(low, lo, pltpu.roll(up, HEAD_DIM, 1)).astype(BF16)
        dv_ref[0] = jnp.where(low, pltpu.roll(lo, HEAD_DIM, 1), up).astype(BF16)
        lo, up = ordered(dq_keep_ref[...], other_ref[block:, :])
        low = low[0:hb]
        dq_ref[0, 0:hb, :] = jnp.where(low, lo, pltpu.roll(up, HEAD_DIM, 1)).astype(BF16)
        dq_ref[0, hb:block, :] = jnp.where(low, pltpu.roll(lo, HEAD_DIM, 1), up).astype(BF16)

    d_query, d_key, d_value = call(last_body, [arr((1, block, LANES))] * 3, name="last")(
        *on_chip(keep, other, dq)
    )
    return d_resid, d_query, d_key, d_value


def solution(mesh):
    heads_axis = mesh.shape["head"]
    ctx_count = mesh.shape["ctx"]

    def run(query, *rest):
        group = query.shape[2] // HEAD_DIM // heads_axis
        z_count = ctx_count // group
        fine = Mesh(mesh.devices.reshape(heads_axis, z_count, group), ("head", "z", "y"))
        rows_spec = P(("z", "y"), "head", None)
        cols_spec = P(("z", "y"), None, "head")
        sizes = (heads_axis, z_count, group)
        return jax.shard_map(
            lambda *args: on_device(sizes, *args),
            mesh=fine,
            in_specs=(rows_spec,) * 5 + (P(),) * 3,
            out_specs=(cols_spec,) * 4,
            check_vma=False,
        )(query, *rest)

    return run
```
